256 devices in a mesh: ep: 64 (over y, z, core), dp: 4 (over x).
Axes of the slice: x: 4, y: 4, z: 8, core: 2. Of those that a mesh axis runs over, the one named last changes fastest.
Arguments:
- tokens: bfloat16 [8192, 2048], P(('ep', 'dp')), may hold values from -6 to 6
- cotangent: bfloat16 [8192, 2048], P(('ep', 'dp')), may hold values from -6 to 6
- expert_ids: int32 [8192, 8], P(('ep', 'dp')), may hold values from 0 to 63, as said below
- route_weights: bfloat16 [8192, 8], P(('ep', 'dp')), may hold values from 0.049804688 to 0.5
- w_gate: bfloat16 [64, 2048, 768], P('ep'), may hold values from -0.125 to 0.125
- w_up: bfloat16 [64, 2048, 768], P('ep'), may hold values from -0.125 to 0.125
- w_down: bfloat16 [64, 768, 2048], P('ep'), may hold values from -0.21875 to 0.21875
Outputs:
- grad_tokens: bfloat16 [8192, 2048], P(('ep', 'dp'))
- grad_route: bfloat16 [8192, 8], P(('ep', 'dp'))
- grad_gate: bfloat16 [64, 2048, 768], P('ep', 'dp')
- grad_up: bfloat16 [64, 2048, 768], P('ep', 'dp')
- grad_down: bfloat16 [64, 768, 2048], P('ep', None, 'dp')
The draws below stay inside these ranges and needn't reach their ends.
Inputs may be any that keep to these rules, and one draw needn't show every extreme that they name: `expert_ids`: each token names 8 different experts. The tokens of one device name no expert more than 8 times; 4 experts, drawn from the seed, are named exactly 8 times by every device's tokens.
All inputs are finite; a program needn't handle non-finite values.
Results may differ from the reference program's by a relative error of at most 0.0095.
Values may be sent and summed in bfloat16 or wider, within the bound.
No kernel may reach another device: no remote copies, remote signals or barrier semaphores. Data moves between devices by JAX's collectives and lax.ppermute only.
A program may use at most 128 MiB of HBM per device.

```python
import math
import jax
import jax.numpy as jnp
from jax import lax

D = 2048
FF = 768
TOPK = 8
TOK_DEV = 32
EXPERTS = 64
CAP = 8
HOT = 4
TOKENS = 8192
N_EP = 64
N_DP = 4


def draw_expert_ids(key, part):
    blocks = TOKENS // TOK_DEV
    half_count = EXPERTS // 2
    hot_key = jax.random.fold_in(key, 11)
    pair_pick = jax.random.permutation(jax.random.fold_in(hot_key, 1), half_count)[:HOT].astype(jnp.int32)
    side_pick = jax.random.randint(jax.random.fold_in(hot_key, 2), (HOT,), 0, 2).astype(jnp.int32)
    hot_ids = pair_pick + side_pick * half_count
    is_hot = jnp.zeros((EXPERTS,), jnp.int32).at[hot_ids].set(1)
    tickets = EXPERTS * CAP
    ticket_owner = jnp.arange(tickets, dtype=jnp.int32) // CAP
    row_total = TOK_DEV * TOPK

    def one_block(index):
        block_key = jax.random.fold_in(jax.random.fold_in(key, 23), index)
        ranking = jax.random.permutation(jax.random.fold_in(block_key, 1), tickets).astype(jnp.int32)
        score = (1 - is_hot[ticket_owner]) * tickets + ranking
        chosen = jnp.argsort(score, stable=True)[:row_total]
        listed = jnp.sort(ticket_owner[chosen])
        slot_pos = jnp.arange(row_total, dtype=jnp.int32)
        token_pos = slot_pos % TOK_DEV
        column_pos = slot_pos // TOK_DEV
        shuffle = jax.random.permutation(jax.random.fold_in(block_key, 2), TOK_DEV).astype(jnp.int32)
        turned = jax.random.randint(jax.random.fold_in(block_key, 3), (TOK_DEV,), 0, TOPK).astype(jnp.int32)
        new_token = shuffle[token_pos]
        new_column = (column_pos + turned[new_token]) % TOPK
        return jnp.zeros((TOK_DEV, TOPK), jnp.int32).at[new_token, new_column].set(listed)
    drawn = lax.map(one_block, jnp.arange(blocks, dtype=jnp.int32))
    return drawn.reshape(TOKENS, TOPK)


def steps_of(rng, extent, split, low, high):
    level, own = 1.0, jax.random.fold_in(rng, 6)
    for position, blocks in split:
        draws = jnp.exp(jax.random.uniform(jax.random.fold_in(own, position), (blocks,), jnp.float32, low / len(split), high / len(split)))
        level = level * jnp.repeat(draws, extent[position] // blocks).reshape([-1 if axis == position else 1 for axis in range(len(extent))])
    return level


def centred(own_key, dims, scale, reach, shards=(), kind=jnp.bfloat16):
    array = scale * jax.random.normal(own_key, dims, jnp.float32)
    if shards:
        array = array * steps_of(own_key, dims, shards, -0.22, 0.18)
    return jnp.clip(array, -reach, reach).astype(kind)


def setup_inputs(seed: int = 0) -> dict:
    streams_of = jax.random.split(jax.random.key(seed), 8)
    tokens = centred(streams_of[0], (TOKENS, D), 1.0, 6.0, ((0, 256),))
    cotangent = centred(streams_of[1], (TOKENS, D), 1.0, 6.0, ((0, 256),))
    expert_ids = draw_expert_ids(jax.random.fold_in(streams_of[7], 71), 0)
    route_weights = jnp.clip(jnp.exp(math.log(0.5) - 2.306499 * jax.random.uniform(streams_of[3], (TOKENS, TOPK), jnp.float32) ** steps_of(streams_of[3], (TOKENS, TOPK), ((0, 256),), -0.2, 0.2)), 0.049804688, 0.5).astype(jnp.bfloat16)
    w_gate = centred(streams_of[4], (EXPERTS, D, FF), D ** -0.5, 0.125, ((0, 64),))
    w_up = centred(streams_of[5], (EXPERTS, D, FF), D ** -0.5, 0.125, ((0, 64),))
    w_down = centred(streams_of[6], (EXPERTS, FF, D), FF ** -0.5, 0.21875, ((0, 64),))
    return {"tokens": tokens, "cotangent": cotangent, "expert_ids": expert_ids, "route_weights": route_weights, "w_gate": w_gate, "w_up": w_up, "w_down": w_down}


contract_last = (((1,), (1,)), ((), ()))
contract_first = (((0,), (0,)), ((), ()))


def silu_parts(gate_pre):
    sig = jax.nn.sigmoid(gate_pre)
    return gate_pre * sig, sig * (1.0 + gate_pre * (1.0 - sig))


def expert_rows(tok_rows, cot_rows, weight, w_gate_one, w_up_one, w_down_one):
    gate_pre = jnp.dot(tok_rows, w_gate_one, preferred_element_type=jnp.float32)
    up_pre = jnp.dot(tok_rows, w_up_one, preferred_element_type=jnp.float32)
    act, slope = silu_parts(gate_pre)
    hidden = lax.optimization_barrier((act * up_pre).astype(jnp.bfloat16))
    back = lax.dot_general(cot_rows, w_down_one, contract_last, preferred_element_type=jnp.float32)
    route_grad = jnp.sum(hidden.astype(jnp.float32) * back, axis=1)
    scaled = weight * back
    grad_gate_pre = (scaled * up_pre * slope).astype(jnp.bfloat16)
    grad_up_pre = (scaled * act).astype(jnp.bfloat16)
    scaled_cot = (weight * cot_rows.astype(jnp.float32)).astype(jnp.bfloat16)
    slot_grad = lax.dot_general(grad_gate_pre, w_gate_one, contract_last, preferred_element_type=jnp.float32)
    slot_grad = slot_grad + lax.dot_general(grad_up_pre, w_up_one, contract_last, preferred_element_type=jnp.float32)
    part_gate = lax.dot_general(tok_rows, grad_gate_pre, contract_first, preferred_element_type=jnp.float32)
    part_up = lax.dot_general(tok_rows, grad_up_pre, contract_first, preferred_element_type=jnp.float32)
    part_down = lax.dot_general(hidden, scaled_cot, contract_first, preferred_element_type=jnp.float32)
    return slot_grad, route_grad, part_gate, part_up, part_down


def reference(tokens, cotangent, expert_ids, route_weights, w_gate, w_up, w_down):
    slots = TOKENS * TOPK
    rows = N_EP * CAP
    flat_ids = expert_ids.reshape(slots)
    flat_w = route_weights.reshape(slots)
    slot_index = jnp.arange(slots, dtype=jnp.int32)
    group_of = (slot_index // (TOK_DEV * TOPK)) % N_DP

    def one_expert(expert):
        w_gate_one = w_gate[expert]
        w_up_one = w_up[expert]
        w_down_one = w_down[expert]
        total_gate = jnp.zeros((D, FF), jnp.float32)
        total_up = jnp.zeros((D, FF), jnp.float32)
        total_down = jnp.zeros((FF, D), jnp.float32)
        slot_list = []
        route_list = []
        target_list = []
        for group in range(N_DP):
            keyed = jnp.where((flat_ids == expert) & (group_of == group), slot_index, slots)
            order = jnp.argsort(keyed, stable=True)[:rows].astype(jnp.int32)
            valid = keyed[order] < slots
            pick = jnp.where(valid, order, 0).astype(jnp.int32)
            mask = valid.astype(tokens.dtype)[:, None]
            tok_rows = tokens[pick // TOPK] * mask
            cot_rows = cotangent[pick // TOPK] * mask
            weight = (flat_w[pick] * valid.astype(flat_w.dtype)).astype(jnp.float32)[:, None]
            result = expert_rows(tok_rows, cot_rows, weight, w_gate_one, w_up_one, w_down_one)
            slot_list.append(result[0].astype(jnp.bfloat16))
            route_list.append(result[1].astype(jnp.bfloat16))
            target_list.append(jnp.where(valid, order, slots).astype(jnp.int32))
            total_gate = total_gate + lax.optimization_barrier(result[2].astype(jnp.bfloat16)).astype(jnp.float32)
            total_up = total_up + lax.optimization_barrier(result[3].astype(jnp.bfloat16)).astype(jnp.float32)
            total_down = total_down + lax.optimization_barrier(result[4].astype(jnp.bfloat16)).astype(jnp.float32)
        return (jnp.stack(slot_list), jnp.stack(route_list), jnp.stack(target_list),
                total_gate.astype(jnp.bfloat16), total_up.astype(jnp.bfloat16), total_down.astype(jnp.bfloat16))

    outs = lax.map(one_expert, jnp.arange(EXPERTS, dtype=jnp.int32))
    targets = outs[2].reshape(-1)
    placed = jnp.zeros((slots + 1, D), jnp.float32).at[targets].set(outs[0].reshape(-1, D).astype(jnp.float32))[:slots]
    grad_tokens = jnp.sum(placed.reshape(TOKENS, TOPK, D), axis=1).astype(jnp.bfloat16)
    grad_route = jnp.zeros((slots + 1,), jnp.bfloat16).at[targets].set(outs[1].reshape(-1))[:slots].reshape(TOKENS, TOPK)
    return grad_tokens, grad_route, outs[3], outs[4], outs[5]
```

```python
import jax
import jax.numpy as jnp
from jax import lax
from jax.experimental import pallas as pl
from jax.experimental.pallas import tpu as pltpu
from jax.sharding import PartitionSpec as P

bf16 = jnp.bfloat16
f32 = jnp.float32
i32 = jnp.int32

NY, NZ, NC = 4, 8, 2
CAP = 8
TOK = 32
TOPK = 8
D = 2048
FF = 768
META = 128
DA = D + META
HALF = NY * NZ * CAP
ROWS = 2 * HALF
FB = 256
NFB = FF // FB
DY = (0, -1, 1, 2)
DZ = (0, -1, -2, -3, 4, 1, 2, 3)
VLIM = 60 * 1024 * 1024

contract_last = (((1,), (1,)), ((), ()))
contract_first = (((0,), (0,)), ((), ()))
nothing = (((1,), (0,)), ((), ()))


def dot(a, b, dims=nothing):
    return lax.dot_general(a, b, dims, preferred_element_type=f32)


def flat(y, z, c):
    return ((y % NY) * NZ + (z % NZ)) * NC + c


def shift(arr, dy=0, dz=0):
    pairs = [
        (flat(y, z, c), flat(y + dy, z + dz, c))
        for y in range(NY)
        for z in range(NZ)
        for c in range(NC)
    ]
    return lax.ppermute(arr, "ep", pairs)


def swap_core(arr):
    return lax.ppermute(arr, "ep", [(i, i ^ 1) for i in range(NY * NZ * NC)])


VM = pl.BlockSpec(memory_space=pltpu.VMEM)
SM = pl.BlockSpec(memory_space=pltpu.SMEM)


def iota(shape, dim):
    return lax.broadcasted_iota(i32, shape, dim)


def pick_x_kernel(me_ref, b0, b1, b2, b3a, b3b, own_ref, sib_ref, code_ref):
    me = me_ref[0]
    n = NZ * TOK
    lane = iota((n, META), 1)
    tok = iota((n, META), 0)
    expert = jnp.where(lane < 64, me, me ^ 1).astype(f32)
    low = iota((n, n), 0)
    col = iota((n, n), 1)
    before = jnp.where((col < low) & (col // TOK == low // TOK), 1.0, 0.0).astype(bf16)
    row_pos = (lane % CAP).astype(f32)
    row_src = (lane % 64) // CAP
    for b in range(NY):
        if b < 3:
            blk = (b0, b1, b2)[b][...]
        else:
            blk = jnp.concatenate([b3a[...], b3b[...]], axis=0)
        meta = blk[:, D:].astype(f32)
        named = jnp.zeros((n, META), f32)
        for k in range(TOPK):
            ident = jnp.broadcast_to(meta[:, k : k + 1], (n, META))
            named = jnp.where(ident == expert, 1.0, named)
        earlier = dot(before, named.astype(bf16))
        code = jnp.where(named > 0, earlier, -1.0)
        code_ref[b] = code.astype(bf16)
        sel = jnp.where((code == row_pos) & (tok // TOK == row_src), 1.0, 0.0).astype(bf16)
        rows = dot(sel, blk, contract_first).astype(bf16)
        own_ref[b * 64 : (b + 1) * 64, :] = rows[:64]
        sib_ref[b * 64 : (b + 1) * 64, :] = rows[64:]


def pick_x(me, blocks):
    return pl.pallas_call(
        pick_x_kernel,
        out_shape=(
            jax.ShapeDtypeStruct((HALF, DA), bf16),
            jax.ShapeDtypeStruct((HALF, DA), bf16),
            jax.ShapeDtypeStruct((NY, NZ * TOK, META), bf16),
        ),
        in_specs=[SM] + [VM] * 5,
        out_specs=(VM, VM, VM),
        compiler_params=pltpu.CompilerParams(vmem_limit_bytes=VLIM),
        name="pick_x",
    )(me, *blocks)


def pick_cot_kernel(code_ref, *refs):
    blocks = refs[:9]
    own_ref, sib_ref, own_acc, sib_acc = refs[9:]
    n = NY * TOK
    lane = iota((n, META), 1)
    tok = iota((n, META), 0)
    row_pos = (lane % CAP).astype(f32)
    row_src = (lane % 64) // CAP
    place = 0
    for s in range(NZ):
        if DZ[s] == 4:
            blk = jnp.concatenate([blocks[place][...], blocks[place + 1][...]], axis=0)
            place += 2
        else:
            blk = blocks[place][...]
            place += 1
        code = jnp.concatenate(
            [code_ref[b, s * TOK : (s + 1) * TOK, :] for b in range(NY)], axis=0
        ).astype(f32)
        sel = jnp.where((code == row_pos) & (tok // TOK == row_src), 1.0, 0.0).astype(bf16)
        rows = dot(sel, blk, contract_first)
        for b in range(NY):
            at = b * 64 + s * CAP
            own_acc[at : at + CAP, :] = rows[b * CAP : (b + 1) * CAP]
            sib_acc[at : at + CAP, :] = rows[64 + b * CAP : 64 + (b + 1) * CAP]
    own_ref[...] = own_acc[...].astype(bf16)
    sib_ref[...] = sib_acc[...].astype(bf16)


def pick_cot(code, blocks):
    return pl.pallas_call(
        pick_cot_kernel,
        out_shape=(
            jax.ShapeDtypeStruct((HALF, D), bf16),
            jax.ShapeDtypeStruct((HALF, D), bf16),
        ),
        in_specs=[VM] * 10,
        out_specs=(VM, VM),
        scratch_shapes=[pltpu.VMEM((HALF, D), f32), pltpu.VMEM((HALF, D), f32)],
        compiler_params=pltpu.CompilerParams(vmem_limit_bytes=VLIM),
        name="pick_cot",
    )(code, *blocks)


def front_kernel(
    me_ref, own_ref, sib_ref, wg_ref, wu_ref,
    hid_ref, hid_t_ref, a_ref, b_ref, weight_ref, x_t_ref, x_scr,
):
    @pl.when(pl.program_id(0) == 0)
    def _():
        x_scr[:HALF] = own_ref[:, :D]
        x_scr[HALF:] = sib_ref[:, :D]
        x_t_ref[...] = x_scr[...].T
        meta = jnp.concatenate([own_ref[:, D:], sib_ref[:, D:]], axis=0).astype(f32)
        expert = me_ref[0].astype(f32)
        total = jnp.zeros((ROWS, 1), f32)
        for k in range(TOPK):
            total = total + jnp.where(
                meta[:, k : k + 1] == expert, meta[:, TOPK + k : TOPK + k + 1], 0.0
            )
        weight_ref[...] = jnp.broadcast_to(total, (ROWS, META))

    x = x_scr[...]
    gate = dot(x, wg_ref[...])
    up = dot(x, wu_ref[...])
    sig = jax.nn.sigmoid(gate)
    act = gate * sig
    hid = (act * up).astype(bf16)
    hid_ref[...] = hid
    hid_t_ref[...] = hid.T
    a_ref[...] = up * (sig * (1.0 + gate * (1.0 - sig)))
    b_ref[...] = act


def front(me, own, sib, wg, wu):
    whole = lambda shape: pl.BlockSpec(shape, lambda j: (0,) * len(shape))
    wide = pl.BlockSpec((ROWS, FB), lambda j: (0, j))
    return pl.pallas_call(
        front_kernel,
        grid=(NFB,),
        out_shape=(
            jax.ShapeDtypeStruct((ROWS, FF), bf16),
            jax.ShapeDtypeStruct((FF, ROWS), bf16),
            jax.ShapeDtypeStruct((ROWS, FF), f32),
            jax.ShapeDtypeStruct((ROWS, FF), f32),
            jax.ShapeDtypeStruct((ROWS, META), f32),
            jax.ShapeDtypeStruct((D, ROWS), bf16),
        ),
        in_specs=[
            SM, whole((HALF, DA)), whole((HALF, DA)),
            pl.BlockSpec((D, FB), lambda j: (0, j)),
            pl.BlockSpec((D, FB), lambda j: (0, j)),
        ],
        out_specs=(
            wide, pl.BlockSpec((FB, ROWS), lambda j: (j, 0)), wide, wide,
            whole((ROWS, META)), whole((D, ROWS)),
        ),
        scratch_shapes=[pltpu.VMEM((ROWS, D), bf16)],
        compiler_params=pltpu.CompilerParams(vmem_limit_bytes=VLIM),
        name="front",
    )(me, own, sib, wg, wu)


def grads_kernel(
    own_ref, sib_ref, hid_ref, hid_t_ref, a_ref, b_ref, weight_ref, x_t_ref, wd_ref,
    out_ref, gg_ref, gu_ref, route_ref, cot_scr, scot_scr,
):
    j = pl.program_id(0)

    @pl.when(j == 0)
    def _():
        cot_scr[:HALF] = own_ref[...]
        cot_scr[HALF:] = sib_ref[...]
        weight = weight_ref[:, :1]
        scot_scr[...] = (weight * cot_scr[...].astype(f32)).astype(bf16)
        route_ref[...] = jnp.zeros_like(route_ref)

    back = dot(cot_scr[...], wd_ref[...], contract_last)
    part = jnp.sum(hid_ref[...].astype(f32) * back, axis=1, keepdims=True)
    route_ref[...] += jnp.broadcast_to(part, (ROWS, META))
    scaled = weight_ref[:, :1] * back
    gg = (scaled * a_ref[...]).astype(bf16)
    gu = (scaled * b_ref[...]).astype(bf16)
    gg_ref[...] = gg
    gu_ref[...] = gu
    out_ref[:, :FB] = dot(x_t_ref[...], gg).astype(bf16)
    out_ref[:, FB : 2 * FB] = dot(x_t_ref[...], gu).astype(bf16)
    down = dot(hid_t_ref[...], scot_scr[...]).astype(bf16)
    for q in range(D // FB):
        out_ref[q * FB : (q + 1) * FB, 2 * FB :] = down[:, q * FB : (q + 1) * FB]


def grads(own, sib, hid, hid_t, a, b, weight, x_t, wd):
    whole = lambda shape: pl.BlockSpec(shape, lambda j: (0,) * len(shape))
    wide = pl.BlockSpec((ROWS, FB), lambda j: (0, j))
    return pl.pallas_call(
        grads_kernel,
        grid=(NFB,),
        out_shape=(
            jax.ShapeDtypeStruct((D, 3 * FF), bf16),
            jax.ShapeDtypeStruct((ROWS, FF), bf16),
            jax.ShapeDtypeStruct((ROWS, FF), bf16),
            jax.ShapeDtypeStruct((ROWS, META), f32),
        ),
        in_specs=[
            whole((HALF, D)), whole((HALF, D)), wide,
            pl.BlockSpec((FB, ROWS), lambda j: (j, 0)), wide, wide,
            whole((ROWS, META)), whole((D, ROWS)),
            pl.BlockSpec((FB, D), lambda j: (j, 0)),
        ],
        out_specs=(
            pl.BlockSpec((D, 3 * FB), lambda j: (0, j)), wide, wide, whole((ROWS, META)),
        ),
        scratch_shapes=[pltpu.VMEM((ROWS, D), bf16), pltpu.VMEM((ROWS, D), bf16)],
        compiler_params=pltpu.CompilerParams(vmem_limit_bytes=VLIM),
        name="grads",
    )(own, sib, hid, hid_t, a, b, weight, x_t, wd)


def slots_kernel(me_ref, gg_ref, gu_ref, route_ref, wg_ref, wu_ref, out_ref):
    me = me_ref[0]
    core = me % NC
    z = (me // NC) % NZ
    y = me // (NC * NZ)
    part = dot(gg_ref[...], wg_ref[...], contract_last)
    part = part + dot(gu_ref[...], wu_ref[...], contract_last)
    for h in range(2):
        for b in range(NY):
            for s in range(NZ):
                src = ((y + DY[b] + NY) % NY) * NZ + (z + DZ[s] + NZ) % NZ
                to = src * NC + (core if h == 0 else 1 - core)
                at = h * HALF + b * 64 + s * CAP
                out_ref[to, :, :D] = part[at : at + CAP].astype(bf16)
                out_ref[to, :, D:] = route_ref[at : at + CAP, :].astype(bf16)


def slots(me, gg, gu, route, wg, wu):
    return pl.pallas_call(
        slots_kernel,
        out_shape=jax.ShapeDtypeStruct((NY * NZ * NC, CAP, DA), bf16),
        in_specs=[SM] + [VM] * 5,
        out_specs=VM,
        compiler_params=pltpu.CompilerParams(vmem_limit_bytes=VLIM),
        name="slots",
    )(me, gg, gu, route, wg, wu)


def body(tokens, cotangent, expert_ids, route_weights, w_gate, w_up, w_down):
    me = lax.axis_index("ep").astype(i32).reshape(1)
    meta = jnp.concatenate(
        [expert_ids.astype(bf16), route_weights, jnp.zeros((TOK, META - 2 * TOPK), bf16)], axis=1
    )
    xa = jnp.concatenate([tokens, meta], axis=1)

    c1 = shift(cotangent, dy=1)
    c2 = shift(cotangent, dy=-1)
    c3 = shift(c1, dy=1)
    cot0 = jnp.concatenate([cotangent, c1, c2, c3], axis=0)

    u = [xa]
    d = [xa]
    for _ in range(3):
        u.append(shift(u[-1], dz=1))
        d.append(shift(d[-1], dz=-1))
    u.append(shift(u[-1], dz=1))
    x0 = jnp.concatenate(u + d[1:], axis=0)
    p1 = shift(x0, dy=1)
    m1 = shift(x0, dy=-1)
    n = NZ * TOK // 2
    qa = shift(p1[:n], dy=1)
    qb = shift(m1[n:], dy=-1)

    cu = [cot0]
    cd = [cot0]
    for _ in range(3):
        cu.append(shift(cu[-1], dz=1))
        cd.append(shift(cd[-1], dz=-1))
    n = NY * TOK // 2
    cq = [shift(cu[-1][:n], dz=1), shift(cd[-1][n:], dz=-1)]

    own_x, sib_x, code = pick_x(me, [x0, p1, m1, qa, qb])
    sib_x = swap_core(sib_x)
    wg, wu, wd = w_gate[0], w_up[0], w_down[0]
    hid, hid_t, a, b, weight, x_t = front(me, own_x, sib_x, wg, wu)

    own_c, sib_c = pick_cot(code, cu + cq + cd[1:])
    sib_c = swap_core(sib_c)
    grad, gg, gu, route = grads(own_c, sib_c, hid, hid_t, a, b, weight, x_t, wd)

    total = lax.psum_scatter(grad, "dp", scatter_dimension=0, tiled=True)
    out = slots(me, gg, gu, route, wg, wu)
    got = lax.all_to_all(out, "ep", split_axis=0, concat_axis=0, tiled=True)

    experts = NY * NZ * NC
    one = (expert_ids[:, :, None] == jnp.arange(experts, dtype=i32)).astype(i32)
    named = jnp.sum(one, axis=1)
    token = jnp.arange(TOK, dtype=i32)
    lower = (token[None, :] < token[:, None]).astype(bf16)
    earlier = dot(lower, named.astype(bf16)).astype(i32)
    row = jnp.arange(experts * CAP, dtype=i32)
    code_of = jnp.repeat(jnp.where(named > 0, earlier, -1), CAP, axis=1)
    sel = code_of == (row % CAP)[None, :]
    got = got.reshape(experts * CAP, DA)
    grad_tokens = dot(sel.astype(bf16), got[:, :D]).astype(bf16)
    mine = sel[:, None, :] & (expert_ids[:, :, None] == (row // CAP)[None, None, :])
    grad_route = jnp.sum(jnp.where(mine, got[:, D].astype(f32), 0.0), axis=2).astype(bf16)

    per = D // 4
    grad_gate = jnp.concatenate([total[:, j * FF : j * FF + FB] for j in range(NFB)], axis=1)
    grad_up = jnp.concatenate(
        [total[:, j * FF + FB : j * FF + 2 * FB] for j in range(NFB)], axis=1
    )
    grad_down = jnp.concatenate(
        [
            jnp.concatenate(
                [
                    total[q * FB : (q + 1) * FB, j * FF + 2 * FB : (j + 1) * FF]
                    for q in range(per // FB)
                ],
                axis=1,
            )
            for j in range(NFB)
        ],
        axis=0,
    )
    return grad_tokens, grad_route, grad_gate[None], grad_up[None], grad_down[None]


def solution(mesh):
    row = P(("ep", "dp"), None)
    expert = P("ep", None, None)
    return jax.shard_map(
        body,
        mesh=mesh,
        in_specs=(row, row, row, row, expert, expert, expert),
        out_specs=(row, row, P("ep", "dp", None), P("ep", "dp", None), P("ep", None, "dp")),
        check_vma=False,
    )
```

```python
import functools

import jax
import jax.numpy as jnp
from jax import lax
from jax.experimental import pallas as pl
from jax.experimental.pallas import tpu as pltpu
from jax.sharding import PartitionSpec as P

bf16 = jnp.bfloat16
f32 = jnp.float32
i32 = jnp.int32

NY, NZ, NC = 4, 8, 2
CAP = 8
TOK = 32
TOPK = 8
D = 2048
FF = 768
META = 128
DA = D + META
HALF = NY * NZ * CAP
ROWS = 2 * HALF
FB = 256
NFB = FF // FB
DY = (0, -1, 1, 2)
DZ = (0, -1, 1, -2, 2, -3, 3, 4)
FIRST = 5
NDP = 4
PIECE = D // NDP // 2
VLIM = 60 * 1024 * 1024

contract_last = (((1,), (1,)), ((), ()))
contract_first = (((0,), (0,)), ((), ()))
nothing = (((1,), (0,)), ((), ()))


def dot(a, b, dims=nothing):
    return lax.dot_general(a, b, dims, preferred_element_type=f32)


def flat(y, z, c):
    return ((y % NY) * NZ + (z % NZ)) * NC + c


def shift(arr, dy=0, dz=0):
    pairs = [
        (flat(y, z, c), flat(y + dy, z + dz, c))
        for y in range(NY)
        for z in range(NZ)
        for c in range(NC)
    ]
    return lax.ppermute(arr, "ep", pairs)


def swap_core(arr):
    return lax.ppermute(arr, "ep", [(i, i ^ 1) for i in range(NY * NZ * NC)])


def shift_dp(arr, by):
    return lax.ppermute(arr, "dp", [(i, (i + by) % NDP) for i in range(NDP)])


def join_kernel(count, *refs):
    out_ref = refs[-1]
    at = 0
    for ref in refs[:count]:
        out_ref[at : at + ref.shape[0], :] = ref[...]
        at += ref.shape[0]


def join(parts, after=()):
    rows = sum(part.shape[0] for part in parts)
    return pl.pallas_call(
        functools.partial(join_kernel, len(parts)),
        out_shape=jax.ShapeDtypeStruct((rows, parts[0].shape[1]), parts[0].dtype),
        in_specs=[VM] * len(parts) + [pl.BlockSpec(memory_space=pl.ANY)] * len(after),
        out_specs=VM,
        name="join",
    )(*parts, *after)


VM = pl.BlockSpec(memory_space=pltpu.VMEM)
SM = pl.BlockSpec(memory_space=pltpu.SMEM)


def iota(shape, dim):
    return lax.broadcasted_iota(i32, shape, dim)


def pick_x_kernel(me_ref, *refs):
    blocks = refs[:10]
    own_ref, sib_ref, code_ref = refs[10:]
    me = me_ref[0]
    n = NZ * TOK
    lane = iota((n, META), 1)
    tok = iota((n, META), 0)
    expert = jnp.where(lane < 64, me, me ^ 1).astype(f32)
    low = iota((n, n), 0)
    col = iota((n, n), 1)
    before = jnp.where((col < low) & (col // TOK == low // TOK), 1.0, 0.0).astype(bf16)
    row_pos = (lane % CAP).astype(f32)
    row_src = (lane % 64) // CAP
    for b in range(NY):
        mine = blocks[2 * b : 2 * b + 2] if b < 3 else blocks[6:]
        blk = jnp.concatenate([ref[...] for ref in mine], axis=0)
        meta = blk[:, D:].astype(f32)
        named = jnp.zeros((n, META), f32)
        for k in range(TOPK):
            ident = jnp.broadcast_to(meta[:, k : k + 1], (n, META))
            named = jnp.where(ident == expert, 1.0, named)
        earlier = dot(before, named.astype(bf16))
        code = jnp.where(named > 0, earlier, -1.0)
        code_ref[b] = code.astype(bf16)
        sel = jnp.where((code == row_pos) & (tok // TOK == row_src), 1.0, 0.0).astype(bf16)
        rows = dot(sel, blk, contract_first).astype(bf16)
        own_ref[b * 64 : (b + 1) * 64, :] = rows[:64]
        sib_ref[b * 64 : (b + 1) * 64, :] = rows[64:]


def pick_x(me, blocks):
    return pl.pallas_call(
        pick_x_kernel,
        out_shape=(
            jax.ShapeDtypeStruct((HALF, DA), bf16),
            jax.ShapeDtypeStruct((HALF, DA), bf16),
            jax.ShapeDtypeStruct((NY, NZ * TOK, META), bf16),
        ),
        in_specs=[SM] + [VM] * 10,
        out_specs=(VM, VM, VM),
        compiler_params=pltpu.CompilerParams(vmem_limit_bytes=VLIM),
        name="pick_x",
    )(me, *blocks)


def pick_cot_kernel(code_ref, *refs):
    blocks = refs[:9]
    own_ref, sib_ref, own_acc, sib_acc = refs[9:]
    n = NY * TOK
    lane = iota((n, META), 1)
    tok = iota((n, META), 0)
    row_pos = (lane % CAP).astype(f32)
    row_src = (lane % 64) // CAP
    place = 0
    for s in range(NZ):
        if DZ[s] == 4:
            blk = jnp.concatenate([blocks[place][...], blocks[place + 1][...]], axis=0)
            place += 2
        else:
            blk = blocks[place][...]
            place += 1
        code = jnp.concatenate(
            [code_ref[b, s * TOK : (s + 1) * TOK, :] for b in range(NY)], axis=0
        ).astype(f32)
        sel = jnp.where((code == row_pos) & (tok // TOK == row_src), 1.0, 0.0).astype(bf16)
        rows = dot(sel, blk, contract_first)
        for b in range(NY):
            at = b * 64 + s * CAP
            own_acc[at : at + CAP, :] = rows[b * CAP : (b + 1) * CAP]
            sib_acc[at : at + CAP, :] = rows[64 + b * CAP : 64 + (b + 1) * CAP]
    own_ref[...] = own_acc[...].astype(bf16)
    sib_ref[...] = sib_acc[...].astype(bf16)


def pick_cot(code, blocks):
    return pl.pallas_call(
        pick_cot_kernel,
        out_shape=(
            jax.ShapeDtypeStruct((HALF, D), bf16),
            jax.ShapeDtypeStruct((HALF, D), bf16),
        ),
        in_specs=[VM] * 10,
        out_specs=(VM, VM),
        scratch_shapes=[pltpu.VMEM((HALF, D), f32), pltpu.VMEM((HALF, D), f32)],
        compiler_params=pltpu.CompilerParams(vmem_limit_bytes=VLIM),
        name="pick_cot",
    )(code, *blocks)


def front_kernel(
    me_ref, own_ref, sib_ref, wg_ref, wu_ref,
    hid_ref, hid_t_ref, a_ref, b_ref, weight_ref, x_t_ref, x_scr,
):
    @pl.when(pl.program_id(0) == 0)
    def _():
        x_scr[:HALF] = own_ref[:, :D]
        x_scr[HALF:] = sib_ref[:, :D]
        x_t_ref[...] = x_scr[...].T
        meta = jnp.concatenate([own_ref[:, D:], sib_ref[:, D:]], axis=0).astype(f32)
        expert = me_ref[0].astype(f32)
        total = jnp.zeros((ROWS, 1), f32)
        for k in range(TOPK):
            total = total + jnp.where(
                meta[:, k : k + 1] == expert, meta[:, TOPK + k : TOPK + k + 1], 0.0
            )
        weight_ref[...] = jnp.broadcast_to(total, (ROWS, META))

    x = x_scr[...]
    gate = dot(x, wg_ref[...])
    up = dot(x, wu_ref[...])
    sig = jax.nn.sigmoid(gate)
    act = gate * sig
    hid = (act * up).astype(bf16)
    hid_ref[...] = hid
    hid_t_ref[...] = hid.T
    a_ref[...] = up * (sig * (1.0 + gate * (1.0 - sig)))
    b_ref[...] = act


def front(me, own, sib, wg, wu):
    whole = lambda shape: pl.BlockSpec(shape, lambda j: (0,) * len(shape))
    wide = pl.BlockSpec((ROWS, FB), lambda j: (0, j))
    return pl.pallas_call(
        front_kernel,
        grid=(NFB,),
        out_shape=(
            jax.ShapeDtypeStruct((ROWS, FF), bf16),
            jax.ShapeDtypeStruct((FF, ROWS), bf16),
            jax.ShapeDtypeStruct((ROWS, FF), f32),
            jax.ShapeDtypeStruct((ROWS, FF), f32),
            jax.ShapeDtypeStruct((ROWS, META), f32),
            jax.ShapeDtypeStruct((D, ROWS), bf16),
        ),
        in_specs=[
            SM, whole((HALF, DA)), whole((HALF, DA)),
            pl.BlockSpec((D, FB), lambda j: (0, j)),
            pl.BlockSpec((D, FB), lambda j: (0, j)),
        ],
        out_specs=(
            wide, pl.BlockSpec((FB, ROWS), lambda j: (j, 0)), wide, wide,
            whole((ROWS, META)), whole((D, ROWS)),
        ),
        scratch_shapes=[pltpu.VMEM((ROWS, D), bf16)],
        compiler_params=pltpu.CompilerParams(vmem_limit_bytes=VLIM),
        name="front",
    )(me, own, sib, wg, wu)


def piece_of(x_rows, gg, gu, hid_t, scot_cols):
    down = dot(hid_t, scot_cols)
    return [dot(x_rows, gg), dot(x_rows, gu)] + [down[q * FB : (q + 1) * FB] for q in range(NFB)]


def widths():
    return [(0, FF), (FF, 2 * FF)] + [(2 * FF + q * FB, 2 * FF + (q + 1) * FB) for q in range(NFB)]


def mid_kernel(
    at_ref, own_ref, sib_ref, hid_ref, hid_t_ref, a_ref, b_ref, weight_ref, xa_ref, xb_ref, wd_ref,
    pa_ref, pb_ref, gg_ref, gu_ref, route_ref, scot_ref, cot_scr,
):
    j = pl.program_id(0)

    @pl.when(j == 0)
    def _():
        cot_scr[:HALF] = own_ref[...]
        cot_scr[HALF:] = sib_ref[...]
        weight = weight_ref[:, :1]
        scot_ref[...] = (weight * cot_scr[...].astype(f32)).astype(bf16)
        route_ref[...] = jnp.zeros_like(route_ref)

    back = dot(cot_scr[...], wd_ref[...], contract_last)
    part = jnp.sum(hid_ref[...].astype(f32) * back, axis=1, keepdims=True)
    route_ref[...] += jnp.broadcast_to(part, (ROWS, META))
    scaled = weight_ref[:, :1] * back
    cols = pl.ds(pl.multiple_of(j * FB, FB), FB)
    gg_ref[:, cols] = (scaled * a_ref[...]).astype(bf16)
    gu_ref[:, cols] = (scaled * b_ref[...]).astype(bf16)

    @pl.when(j == NFB - 1)
    def _():
        for n, (x_ref, out_ref) in enumerate(((xa_ref, pa_ref), (xb_ref, pb_ref))):
            some = pl.ds(pl.multiple_of(at_ref[n] * PIECE, PIECE), PIECE)
            values = piece_of(
                x_ref[...], gg_ref[...], gu_ref[...], hid_t_ref[...], scot_ref[:, some]
            )
            for value, (low, high) in zip(values, widths()):
                out_ref[:, low:high] = value.astype(bf16)


def whole(shape):
    return pl.BlockSpec(shape, lambda *_: (0,) * len(shape))


def mid(at, own, sib, hid, hid_t, a, b, weight, x_t, wd):
    wide = pl.BlockSpec((ROWS, FB), lambda j, at_ref: (0, j))
    return pl.pallas_call(
        mid_kernel,
        out_shape=(
            jax.ShapeDtypeStruct((PIECE, 3 * FF), bf16),
            jax.ShapeDtypeStruct((PIECE, 3 * FF), bf16),
            jax.ShapeDtypeStruct((ROWS, FF), bf16),
            jax.ShapeDtypeStruct((ROWS, FF), bf16),
            jax.ShapeDtypeStruct((ROWS, META), f32),
            jax.ShapeDtypeStruct((ROWS, D), bf16),
        ),
        grid_spec=pltpu.PrefetchScalarGridSpec(
            num_scalar_prefetch=1,
            grid=(NFB,),
            in_specs=[
                whole((HALF, D)), whole((HALF, D)), wide, whole((FF, ROWS)), wide, wide,
                whole((ROWS, META)),
                pl.BlockSpec((PIECE, ROWS), lambda j, at_ref: (at_ref[0], 0)),
                pl.BlockSpec((PIECE, ROWS), lambda j, at_ref: (at_ref[1], 0)),
                pl.BlockSpec((FB, D), lambda j, at_ref: (j, 0)),
            ],
            out_specs=(
                whole((PIECE, 3 * FF)), whole((PIECE, 3 * FF)), whole((ROWS, FF)),
                whole((ROWS, FF)), whole((ROWS, META)), whole((ROWS, D)),
            ),
            scratch_shapes=[pltpu.VMEM((ROWS, D), bf16)],
        ),
        compiler_params=pltpu.CompilerParams(vmem_limit_bytes=VLIM),
        name="mid",
    )(at, own, sib, hid, hid_t, a, b, weight, x_t, x_t, wd)


def pieces_kernel(adds, *refs):
    at_ref, xa_ref, xb_ref, ca_ref, cb_ref, gg_ref, gu_ref, hid_t_ref = refs[:8]
    more = refs[8 : 8 + 2 * adds]
    outs = refs[8 + 2 * adds :]
    for n, (x_ref, c_ref) in enumerate(((xa_ref, ca_ref), (xb_ref, cb_ref))):
        values = piece_of(x_ref[...], gg_ref[...], gu_ref[...], hid_t_ref[...], c_ref[...])
        for value, (low, high) in zip(values, widths()):
            for k in range(adds):
                value = value + more[2 * k + n][:, low:high].astype(f32)
            outs[n][:, low:high] = value.astype(bf16)


def piece_specs():
    return [
        pl.BlockSpec((PIECE, ROWS), lambda j, at_ref: (at_ref[0], 0)),
        pl.BlockSpec((PIECE, ROWS), lambda j, at_ref: (at_ref[1], 0)),
        pl.BlockSpec((ROWS, PIECE), lambda j, at_ref: (0, at_ref[0])),
        pl.BlockSpec((ROWS, PIECE), lambda j, at_ref: (0, at_ref[1])),
        whole((ROWS, FF)), whole((ROWS, FF)), whole((FF, ROWS)),
    ]


def pieces(at, x_t, scot, gg, gu, hid_t, *more):
    size = (PIECE, 3 * FF)
    return pl.pallas_call(
        functools.partial(pieces_kernel, len(more) // 2),
        out_shape=(jax.ShapeDtypeStruct(size, bf16), jax.ShapeDtypeStruct(size, bf16)),
        grid_spec=pltpu.PrefetchScalarGridSpec(
            num_scalar_prefetch=1,
            grid=(1,),
            in_specs=piece_specs() + [whole(size)] * len(more),
            out_specs=(whole(size), whole(size)),
        ),
        compiler_params=pltpu.CompilerParams(vmem_limit_bytes=VLIM),
        name="pieces",
    )(at, x_t, x_t, scot, scot, gg, gu, hid_t, *more)


def final_kernel(*refs):
    at_ref, xa_ref, xb_ref, ca_ref, cb_ref, gg_ref, gu_ref, hid_t_ref = refs[:8]
    more = refs[8:12]
    gate_ref, up_ref, down_ref = refs[12:]
    for n, (x_ref, c_ref) in enumerate(((xa_ref, ca_ref), (xb_ref, cb_ref))):
        values = piece_of(x_ref[...], gg_ref[...], gu_ref[...], hid_t_ref[...], c_ref[...])
        side = slice(n * PIECE, (n + 1) * PIECE)
        for i, (value, (low, high)) in enumerate(zip(values, widths())):
            for k in range(2):
                value = value + more[2 * k + n][:, low:high].astype(f32)
            value = value.astype(bf16)
            if i < 2:
                (gate_ref, up_ref)[i][0, side, :] = value
            else:
                down_ref[0, (i - 2) * FB : (i - 1) * FB, side] = value


def final(at, x_t, scot, gg, gu, hid_t, *more):
    size = (PIECE, 3 * FF)
    per = D // NDP
    return pl.pallas_call(
        final_kernel,
        out_shape=(
            jax.ShapeDtypeStruct((1, per, FF), bf16),
            jax.ShapeDtypeStruct((1, per, FF), bf16),
            jax.ShapeDtypeStruct((1, FF, per), bf16),
        ),
        grid_spec=pltpu.PrefetchScalarGridSpec(
            num_scalar_prefetch=1,
            grid=(1,),
            in_specs=piece_specs() + [whole(size)] * 4,
            out_specs=(whole((1, per, FF)), whole((1, per, FF)), whole((1, FF, per))),
        ),
        compiler_params=pltpu.CompilerParams(vmem_limit_bytes=VLIM),
        name="final",
    )(at, x_t, x_t, scot, scot, gg, gu, hid_t, *more)


def slots_kernel(me_ref, gg_ref, gu_ref, route_ref, wg_ref, wu_ref, out_ref):
    me = me_ref[0]
    core = me % NC
    z = (me // NC) % NZ
    y = me // (NC * NZ)
    part = dot(gg_ref[...], wg_ref[...], contract_last)
    part = part + dot(gu_ref[...], wu_ref[...], contract_last)
    for h in range(2):
        for b in range(NY):
            for s in range(NZ):
                src = ((y + DY[b] + NY) % NY) * NZ + (z + DZ[s] + NZ) % NZ
                to = src * NC + (core if h == 0 else 1 - core)
                at = h * HALF + b * 64 + s * CAP
                out_ref[to, :, :D] = part[at : at + CAP].astype(bf16)
                out_ref[to, :, D:] = route_ref[at : at + CAP, :].astype(bf16)


def slots(me, gg, gu, route, wg, wu):
    return pl.pallas_call(
        slots_kernel,
        out_shape=jax.ShapeDtypeStruct((NY * NZ * NC, CAP, DA), bf16),
        in_specs=[SM] + [VM] * 5,
        out_specs=VM,
        compiler_params=pltpu.CompilerParams(vmem_limit_bytes=VLIM),
        name="slots",
    )(me, gg, gu, route, wg, wu)


def body(tokens, cotangent, expert_ids, route_weights, w_gate, w_up, w_down):
    me = lax.axis_index("ep").astype(i32).reshape(1)
    meta = jnp.concatenate(
        [expert_ids.astype(bf16), route_weights, jnp.zeros((TOK, META - 2 * TOPK), bf16)], axis=1
    )
    xa = jnp.concatenate([tokens, meta], axis=1)

    c1 = shift(cotangent, dy=1)
    c2 = shift(cotangent, dy=-1)
    c3 = shift(c1, dy=1)

    u = [xa]
    d = [xa]
    for _ in range(3):
        u.append(shift(u[-1], dz=1))
        d.append(shift(d[-1], dz=-1))
    u.append(shift(u[-1], dz=1))

    def ring_y(part):
        p1 = shift(part, dy=1)
        m1 = shift(part, dy=-1)
        n = part.shape[0] // 2
        return part, p1, m1, shift(p1[:n], dy=1), shift(m1[n:], dy=-1)

    y1 = ring_y(join([xa, u[1], d[1], u[2], d[2]]))
    y2 = ring_y(join([u[3], d[3], u[4]]))
    blocks = [y1[0], y2[0], y1[1], y2[1], y1[2], y2[2], *y1[3:], *y2[3:]]

    cot0 = join([cotangent, c1, c2, c3], after=[u[2], d[2]])
    cu = [cot0]
    cd = [cot0]
    for _ in range(3):
        cu.append(shift(cu[-1], dz=1))
        cd.append(shift(cd[-1], dz=-1))
    n = NY * TOK // 2
    cq = [shift(cu[-1][:n], dz=1), shift(cd[-1][n:], dz=-1)]

    own_x, sib_x, code = pick_x(me, blocks)
    sib_x = swap_core(sib_x)
    wg, wu, wd = w_gate[0], w_up[0], w_down[0]
    hid, hid_t, a, b, weight, x_t = front(me, own_x, sib_x, wg, wu)

    own_c, sib_c = pick_cot(code, [cot0, cu[1], cd[1], cu[2], cd[2], cu[3], cd[3], *cq])
    sib_c = swap_core(sib_c)

    dp = lax.axis_index("dp").astype(i32)
    at = lambda *which: jnp.stack([2 * ((dp + r) % NDP) + h for r, h in which])
    p2a, p2b, gg, gu, route, scot = mid(
        at((2, 0), (2, 1)), own_c, sib_c, hid, hid_t, a, b, weight, x_t, wd
    )
    args = (x_t, scot, gg, gu, hid_t)
    r1a, r1b = shift_dp(p2a, 1), shift_dp(p2b, -1)
    p1b, p3a = pieces(at((1, 1), (3, 0)), *args)
    r2b, r2a = shift_dp(p1b, 1), shift_dp(p3a, -1)
    out = slots(me, gg, gu, route, wg, wu)
    got = lax.all_to_all(out, "ep", split_axis=0, concat_axis=0, tiled=True)
    p1a, p3b = pieces(at((1, 0), (3, 1)), *args, r1a, r1b)
    r3a, r3b = shift_dp(p1a, 1), shift_dp(p3b, -1)
    grad_gate, grad_up, grad_down = final(at((0, 0), (0, 1)), *args, r2a, r2b, r3a, r3b)

    experts = NY * NZ * NC
    one = (expert_ids[:, :, None] == jnp.arange(experts, dtype=i32)).astype(i32)
    named = jnp.sum(one, axis=1)
    token = jnp.arange(TOK, dtype=i32)
    lower = (token[None, :] < token[:, None]).astype(bf16)
    earlier = dot(lower, named.astype(bf16)).astype(i32)
    row = jnp.arange(experts * CAP, dtype=i32)
    code_of = jnp.repeat(jnp.where(named > 0, earlier, -1), CAP, axis=1)
    sel = code_of == (row % CAP)[None, :]
    got = got.reshape(experts * CAP, DA)
    grad_tokens = dot(sel.astype(bf16), got[:, :D]).astype(bf16)
    mine = sel[:, None, :] & (expert_ids[:, :, None] == (row // CAP)[None, None, :])
    grad_route = jnp.sum(jnp.where(mine, got[:, D].astype(f32), 0.0), axis=2).astype(bf16)

    return grad_tokens, grad_route, grad_gate, grad_up, grad_down


def solution(mesh):
    row = P(("ep", "dp"), None)
    expert = P("ep", None, None)
    return jax.shard_map(
        body,
        mesh=mesh,
        in_specs=(row, row, row, row, expert, expert, expert),
        out_specs=(row, row, P("ep", "dp", None), P("ep", "dp", None), P("ep", None, "dp")),
        check_vma=False,
    )
```

```python
import functools

import jax
import jax.numpy as jnp
from jax import lax
from jax.experimental import pallas as pl
from jax.experimental.pallas import tpu as pltpu
from jax.sharding import PartitionSpec as P

bf16 = jnp.bfloat16
f32 = jnp.float32
i32 = jnp.int32

NY, NZ, NC = 4, 8, 2
CAP = 8
TOK = 32
TOPK = 8
D = 2048
FF = 768
META = 128
DA = D + META
HALF = NY * NZ * CAP
ROWS = 2 * HALF
FB = 256
NFB = FF // FB
DY = (0, -1, 1, 2)
DZ = (0, -1, 1, -2, 2, -3, 3, 4)
NDP = 4
PIECE = D // NDP // 2
VLIM = 60 * 1024 * 1024

contract_last = (((1,), (1,)), ((), ()))
contract_first = (((0,), (0,)), ((), ()))
nothing = (((1,), (0,)), ((), ()))


def dot(a, b, dims=nothing):
    return lax.dot_general(a, b, dims, preferred_element_type=f32)


def flat(y, z, c):
    return ((y % NY) * NZ + (z % NZ)) * NC + c


def shift(arr, dy=0, dz=0):
    pairs = [
        (flat(y, z, c), flat(y + dy, z + dz, c))
        for y in range(NY)
        for z in range(NZ)
        for c in range(NC)
    ]
    return lax.ppermute(arr, "ep", pairs)


def swap_core(arr):
    return lax.ppermute(arr, "ep", [(i, i ^ 1) for i in range(NY * NZ * NC)])


def shift_dp(arr, by):
    return lax.ppermute(arr, "dp", [(i, (i + by) % NDP) for i in range(NDP)])


def join_kernel(count, *refs):
    out_ref = refs[-1]
    at = 0
    for ref in refs[:count]:
        out_ref[at : at + ref.shape[0], :] = ref[...]
        at += ref.shape[0]


def join(parts, after=()):
    rows = sum(part.shape[0] for part in parts)
    return pl.pallas_call(
        functools.partial(join_kernel, len(parts)),
        out_shape=jax.ShapeDtypeStruct((rows, parts[0].shape[1]), parts[0].dtype),
        in_specs=[VM] * len(parts) + [pl.BlockSpec(memory_space=pl.ANY)] * len(after),
        out_specs=VM,
        name="join",
    )(*parts, *after)


def cost(flops):
    return pl.CostEstimate(flops=flops, transcendentals=0, bytes_accessed=0)


VM = pl.BlockSpec(memory_space=pltpu.VMEM)
SM = pl.BlockSpec(memory_space=pltpu.SMEM)


def iota(shape, dim):
    return lax.broadcasted_iota(i32, shape, dim)


def pick_x_kernel(me_ref, *refs):
    blocks = refs[:5]
    own_ref, sib_ref, code_ref = refs[5:]
    me = me_ref[0]
    n = NZ * TOK
    lane = iota((n, META), 1)
    tok = iota((n, META), 0)
    expert = jnp.where(lane < 64, me, me ^ 1).astype(f32)
    low = iota((n, n), 0)
    col = iota((n, n), 1)
    before = jnp.where((col < low) & (col // TOK == low // TOK), 1.0, 0.0).astype(bf16)
    row_pos = (lane % CAP).astype(f32)
    row_src = (lane % 64) // CAP
    for b in range(NY):
        mine = blocks[b : b + 1] if b < 3 else blocks[3:]
        blk = jnp.concatenate([ref[...] for ref in mine], axis=0)
        meta = blk[:, D:].astype(f32)
        named = jnp.zeros((n, META), f32)
        for k in range(TOPK):
            ident = jnp.broadcast_to(meta[:, k : k + 1], (n, META))
            named = jnp.where(ident == expert, 1.0, named)
        earlier = dot(before, named.astype(bf16))
        code = jnp.where(named > 0, earlier, -1.0)
        code_ref[b] = code.astype(bf16)
        sel = jnp.where((code == row_pos) & (tok // TOK == row_src), 1.0, 0.0).astype(bf16)
        rows = dot(sel, blk, contract_first).astype(bf16)
        own_ref[b * 64 : (b + 1) * 64, :] = rows[:64]
        sib_ref[b * 64 : (b + 1) * 64, :] = rows[64:]


def pick_x(me, blocks):
    return pl.pallas_call(
        pick_x_kernel,
        out_shape=(
            jax.ShapeDtypeStruct((HALF, DA), bf16),
            jax.ShapeDtypeStruct((HALF, DA), bf16),
            jax.ShapeDtypeStruct((NY, NZ * TOK, META), bf16),
        ),
        in_specs=[SM] + [VM] * 5,
        out_specs=(VM, VM, VM),
        compiler_params=pltpu.CompilerParams(vmem_limit_bytes=VLIM),
        name="pick_x",
    )(me, *blocks)


def pick_cot_kernel(code_ref, *refs):
    blocks = refs[:9]
    own_ref, sib_ref, own_acc, sib_acc = refs[9:]
    n = NY * TOK
    lane = iota((n, META), 1)
    tok = iota((n, META), 0)
    row_pos = (lane % CAP).astype(f32)
    row_src = (lane % 64) // CAP
    place = 0
    for s in range(NZ):
        if DZ[s] == 4:
            blk = jnp.concatenate([blocks[place][...], blocks[place + 1][...]], axis=0)
            place += 2
        else:
            blk = blocks[place][...]
            place += 1
        code = jnp.concatenate(
            [code_ref[b, s * TOK : (s + 1) * TOK, :] for b in range(NY)], axis=0
        ).astype(f32)
        sel = jnp.where((code == row_pos) & (tok // TOK == row_src), 1.0, 0.0).astype(bf16)
        rows = dot(sel, blk, contract_first)
        for b in range(NY):
            at = b * 64 + s * CAP
            own_acc[at : at + CAP, :] = rows[b * CAP : (b + 1) * CAP]
            sib_acc[at : at + CAP, :] = rows[64 + b * CAP : 64 + (b + 1) * CAP]
    own_ref[...] = own_acc[...].astype(bf16)
    sib_ref[...] = sib_acc[...].astype(bf16)


def pick_cot(code, blocks):
    return pl.pallas_call(
        pick_cot_kernel,
        out_shape=(
            jax.ShapeDtypeStruct((HALF, D), bf16),
            jax.ShapeDtypeStruct((HALF, D), bf16),
        ),
        in_specs=[VM] * 10,
        out_specs=(VM, VM),
        scratch_shapes=[pltpu.VMEM((HALF, D), f32), pltpu.VMEM((HALF, D), f32)],
        compiler_params=pltpu.CompilerParams(vmem_limit_bytes=VLIM),
        name="pick_cot",
    )(code, *blocks)


def front_kernel(
    me_ref, own_ref, sib_ref, wg_ref, wu_ref,
    hid_ref, hid_t_ref, a_ref, b_ref, weight_ref, x_t_ref, x_scr,
):
    @pl.when(pl.program_id(0) == 0)
    def _():
        x_scr[:HALF] = own_ref[:, :D]
        x_scr[HALF:] = sib_ref[:, :D]
        x_t_ref[...] = x_scr[...].T
        meta = jnp.concatenate([own_ref[:, D:], sib_ref[:, D:]], axis=0).astype(f32)
        expert = me_ref[0].astype(f32)
        total = jnp.zeros((ROWS, 1), f32)
        for k in range(TOPK):
            total = total + jnp.where(
                meta[:, k : k + 1] == expert, meta[:, TOPK + k : TOPK + k + 1], 0.0
            )
        weight_ref[...] = jnp.broadcast_to(total, (ROWS, META))

    x = x_scr[...]
    gate = dot(x, wg_ref[...])
    up = dot(x, wu_ref[...])
    sig = jax.nn.sigmoid(gate)
    act = gate * sig
    hid = (act * up).astype(bf16)
    hid_ref[...] = hid
    hid_t_ref[...] = hid.T
    a_ref[...] = up * (sig * (1.0 + gate * (1.0 - sig)))
    b_ref[...] = act


def front(me, own, sib, wg, wu):
    whole = lambda shape: pl.BlockSpec(shape, lambda j: (0,) * len(shape))
    wide = pl.BlockSpec((ROWS, FB), lambda j: (0, j))
    return pl.pallas_call(
        front_kernel,
        grid=(NFB,),
        out_shape=(
            jax.ShapeDtypeStruct((ROWS, FF), bf16),
            jax.ShapeDtypeStruct((FF, ROWS), bf16),
            jax.ShapeDtypeStruct((ROWS, FF), f32),
            jax.ShapeDtypeStruct((ROWS, FF), f32),
            jax.ShapeDtypeStruct((ROWS, META), f32),
            jax.ShapeDtypeStruct((D, ROWS), bf16),
        ),
        in_specs=[
            SM, whole((HALF, DA)), whole((HALF, DA)),
            pl.BlockSpec((D, FB), lambda j: (0, j)),
            pl.BlockSpec((D, FB), lambda j: (0, j)),
        ],
        out_specs=(
            wide, pl.BlockSpec((FB, ROWS), lambda j: (j, 0)), wide, wide,
            whole((ROWS, META)), whole((D, ROWS)),
        ),
        scratch_shapes=[pltpu.VMEM((ROWS, D), bf16)],
        compiler_params=pltpu.CompilerParams(vmem_limit_bytes=VLIM),
        cost_estimate=cost(3_000_000_000),
        name="front",
    )(me, own, sib, wg, wu)


def piece_of(x_rows, gg, gu, hid_t, scot_cols):
    down = dot(hid_t, scot_cols)
    return [dot(x_rows, gg), dot(x_rows, gu)] + [down[q * FB : (q + 1) * FB] for q in range(NFB)]


def widths():
    return [(0, FF), (FF, 2 * FF)] + [(2 * FF + q * FB, 2 * FF + (q + 1) * FB) for q in range(NFB)]


def mid_kernel(
    at_ref, own_ref, sib_ref, hid_ref, hid_t_ref, a_ref, b_ref, weight_ref, xa_ref, xb_ref, wd_ref,
    pa_ref, pb_ref, gg_ref, gu_ref, route_ref, scot_ref, cot_scr,
):
    j = pl.program_id(0)

    @pl.when(j == 0)
    def _():
        cot_scr[:HALF] = own_ref[...]
        cot_scr[HALF:] = sib_ref[...]
        weight = weight_ref[:, :1]
        scot_ref[...] = (weight * cot_scr[...].astype(f32)).astype(bf16)
        route_ref[...] = jnp.zeros_like(route_ref)

    back = dot(cot_scr[...], wd_ref[...], contract_last)
    part = jnp.sum(hid_ref[...].astype(f32) * back, axis=1, keepdims=True)
    route_ref[...] += jnp.broadcast_to(part, (ROWS, META))
    scaled = weight_ref[:, :1] * back
    cols = pl.ds(pl.multiple_of(j * FB, FB), FB)
    gg_ref[:, cols] = (scaled * a_ref[...]).astype(bf16)
    gu_ref[:, cols] = (scaled * b_ref[...]).astype(bf16)

    @pl.when(j == NFB - 1)
    def _():
        for n, (x_ref, out_ref) in enumerate(((xa_ref, pa_ref), (xb_ref, pb_ref))):
            some = pl.ds(pl.multiple_of(at_ref[n] * PIECE, PIECE), PIECE)
            values = piece_of(
                x_ref[...], gg_ref[...], gu_ref[...], hid_t_ref[...], scot_ref[:, some]
            )
            for value, (low, high) in zip(values, widths()):
                out_ref[:, low:high] = value.astype(bf16)


def whole(shape):
    return pl.BlockSpec(shape, lambda *_: (0,) * len(shape))


def mid(at, own, sib, hid, hid_t, a, b, weight, x_t, wd):
    wide = pl.BlockSpec((ROWS, FB), lambda j, at_ref: (0, j))
    return pl.pallas_call(
        mid_kernel,
        out_shape=(
            jax.ShapeDtypeStruct((PIECE, 3 * FF), bf16),
            jax.ShapeDtypeStruct((PIECE, 3 * FF), bf16),
            jax.ShapeDtypeStruct((ROWS, FF), bf16),
            jax.ShapeDtypeStruct((ROWS, FF), bf16),
            jax.ShapeDtypeStruct((ROWS, META), f32),
            jax.ShapeDtypeStruct((ROWS, D), bf16),
        ),
        grid_spec=pltpu.PrefetchScalarGridSpec(
            num_scalar_prefetch=1,
            grid=(NFB,),
            in_specs=[
                whole((HALF, D)), whole((HALF, D)), wide, whole((FF, ROWS)), wide, wide,
                whole((ROWS, META)),
                pl.BlockSpec((PIECE, ROWS), lambda j, at_ref: (at_ref[0], 0)),
                pl.BlockSpec((PIECE, ROWS), lambda j, at_ref: (at_ref[1], 0)),
                pl.BlockSpec((FB, D), lambda j, at_ref: (j, 0)),
            ],
            out_specs=(
                whole((PIECE, 3 * FF)), whole((PIECE, 3 * FF)), whole((ROWS, FF)),
                whole((ROWS, FF)), whole((ROWS, META)), whole((ROWS, D)),
            ),
            scratch_shapes=[pltpu.VMEM((ROWS, D), bf16)],
        ),
        compiler_params=pltpu.CompilerParams(vmem_limit_bytes=VLIM),
        name="mid",
    )(at, own, sib, hid, hid_t, a, b, weight, x_t, x_t, wd)


def pieces_kernel(adds, *refs):
    at_ref, xa_ref, xb_ref, ca_ref, cb_ref, gg_ref, gu_ref, hid_t_ref = refs[:8]
    more = refs[8 : 8 + 2 * adds]
    outs = refs[8 + 2 * adds :]
    for n, (x_ref, c_ref) in enumerate(((xa_ref, ca_ref), (xb_ref, cb_ref))):
        values = piece_of(x_ref[...], gg_ref[...], gu_ref[...], hid_t_ref[...], c_ref[...])
        for value, (low, high) in zip(values, widths()):
            for k in range(adds):
                value = value + more[2 * k + n][:, low:high].astype(f32)
            outs[n][:, low:high] = value.astype(bf16)


def piece_specs():
    return [
        pl.BlockSpec((PIECE, ROWS), lambda j, at_ref: (at_ref[0], 0)),
        pl.BlockSpec((PIECE, ROWS), lambda j, at_ref: (at_ref[1], 0)),
        pl.BlockSpec((ROWS, PIECE), lambda j, at_ref: (0, at_ref[0])),
        pl.BlockSpec((ROWS, PIECE), lambda j, at_ref: (0, at_ref[1])),
        whole((ROWS, FF)), whole((ROWS, FF)), whole((FF, ROWS)),
    ]


def pieces(at, x_t, scot, gg, gu, hid_t, *more):
    size = (PIECE, 3 * FF)
    return pl.pallas_call(
        functools.partial(pieces_kernel, len(more) // 2),
        out_shape=(jax.ShapeDtypeStruct(size, bf16), jax.ShapeDtypeStruct(size, bf16)),
        grid_spec=pltpu.PrefetchScalarGridSpec(
            num_scalar_prefetch=1,
            grid=(1,),
            in_specs=piece_specs() + [whole(size)] * len(more),
            out_specs=(whole(size), whole(size)),
        ),
        compiler_params=pltpu.CompilerParams(vmem_limit_bytes=VLIM),
        name="pieces",
    )(at, x_t, x_t, scot, scot, gg, gu, hid_t, *more)


def final_kernel(*refs):
    at_ref, xa_ref, xb_ref, ca_ref, cb_ref, gg_ref, gu_ref, hid_t_ref = refs[:8]
    more = refs[8:12]
    gate_ref, up_ref, down_ref = refs[12:]
    for n, (x_ref, c_ref) in enumerate(((xa_ref, ca_ref), (xb_ref, cb_ref))):
        values = piece_of(x_ref[...], gg_ref[...], gu_ref[...], hid_t_ref[...], c_ref[...])
        side = slice(n * PIECE, (n + 1) * PIECE)
        for i, (value, (low, high)) in enumerate(zip(values, widths())):
            for k in range(2):
                value = value + more[2 * k + n][:, low:high].astype(f32)
            value = value.astype(bf16)
            if i < 2:
                (gate_ref, up_ref)[i][0, side, :] = value
            else:
                down_ref[0, (i - 2) * FB : (i - 1) * FB, side] = value


def final(at, x_t, scot, gg, gu, hid_t, *more):
    size = (PIECE, 3 * FF)
    per = D // NDP
    return pl.pallas_call(
        final_kernel,
        out_shape=(
            jax.ShapeDtypeStruct((1, per, FF), bf16),
            jax.ShapeDtypeStruct((1, per, FF), bf16),
            jax.ShapeDtypeStruct((1, FF, per), bf16),
        ),
        grid_spec=pltpu.PrefetchScalarGridSpec(
            num_scalar_prefetch=1,
            grid=(1,),
            in_specs=piece_specs() + [whole(size)] * 4,
            out_specs=(whole((1, per, FF)), whole((1, per, FF)), whole((1, FF, per))),
        ),
        compiler_params=pltpu.CompilerParams(vmem_limit_bytes=VLIM),
        cost_estimate=cost(30_000_000_000),
        name="final",
    )(at, x_t, x_t, scot, scot, gg, gu, hid_t, *more)


def slots_kernel(me_ref, gg_ref, gu_ref, route_ref, wg_ref, wu_ref, out_ref):
    me = me_ref[0]
    core = me % NC
    z = (me // NC) % NZ
    y = me // (NC * NZ)
    part = dot(gg_ref[...], wg_ref[...], contract_last)
    part = part + dot(gu_ref[...], wu_ref[...], contract_last)
    for h in range(2):
        for b in range(NY):
            for s in range(NZ):
                src = ((y + DY[b] + NY) % NY) * NZ + (z + DZ[s] + NZ) % NZ
                to = src * NC + (core if h == 0 else 1 - core)
                at = h * HALF + b * 64 + s * CAP
                out_ref[to, :, :D] = part[at : at + CAP].astype(bf16)
                out_ref[to, :, D:] = route_ref[at : at + CAP, :].astype(bf16)


def slots(me, gg, gu, route, wg, wu):
    return pl.pallas_call(
        slots_kernel,
        out_shape=jax.ShapeDtypeStruct((NY * NZ * NC, CAP, DA), bf16),
        in_specs=[SM] + [VM] * 5,
        out_specs=VM,
        compiler_params=pltpu.CompilerParams(vmem_limit_bytes=VLIM),
        name="slots",
    )(me, gg, gu, route, wg, wu)


def body(tokens, cotangent, expert_ids, route_weights, w_gate, w_up, w_down):
    me = lax.axis_index("ep").astype(i32).reshape(1)
    meta = jnp.concatenate(
        [expert_ids.astype(bf16), route_weights, jnp.zeros((TOK, META - 2 * TOPK), bf16)], axis=1
    )
    xa = jnp.concatenate([tokens, meta], axis=1)

    c1 = shift(cotangent, dy=1)
    c2 = shift(cotangent, dy=-1)
    c3 = shift(c1, dy=1)

    u = [xa]
    d = [xa]
    for _ in range(3):
        u.append(shift(u[-1], dz=1))
        d.append(shift(d[-1], dz=-1))
    u.append(shift(u[-1], dz=1))

    def ring_y(part):
        p1 = shift(part, dy=1)
        m1 = shift(part, dy=-1)
        n = part.shape[0] // 2
        return part, p1, m1, shift(p1[:n], dy=1), shift(m1[n:], dy=-1)

    blocks = ring_y(join([xa, u[1], d[1], u[2], d[2], u[3], d[3], u[4]], after=[c2, c3]))
    cot0 = join([cotangent, c1, c2, c3], after=[u[3], d[3]])
    cu = [cot0]
    cd = [cot0]
    for _ in range(3):
        cu.append(shift(cu[-1], dz=1))
        cd.append(shift(cd[-1], dz=-1))
    n = NY * TOK // 2
    cq = [shift(cu[-1][:n], dz=1), shift(cd[-1][n:], dz=-1)]

    own_x, sib_x, code = pick_x(me, blocks)
    sib_x = swap_core(sib_x)
    wg, wu, wd = w_gate[0], w_up[0], w_down[0]
    hid, hid_t, a, b, weight, x_t = front(me, own_x, sib_x, wg, wu)

    own_c, sib_c = pick_cot(code, [cot0, cu[1], cd[1], cu[2], cd[2], cu[3], cd[3], *cq])
    sib_c = swap_core(sib_c)

    dp = lax.axis_index("dp").astype(i32)
    at = lambda *which: jnp.stack([2 * ((dp + r) % NDP) + h for r, h in which])
    p2a, p2b, gg, gu, route, scot = mid(
        at((2, 0), (2, 1)), own_c, sib_c, hid, hid_t, a, b, weight, x_t, wd
    )
    args = (x_t, scot, gg, gu, hid_t)
    r1a, r1b = shift_dp(p2a, 1), shift_dp(p2b, -1)
    p1b, p3a = pieces(at((1, 1), (3, 0)), *args)
    r2b, r2a = shift_dp(p1b, 1), shift_dp(p3a, -1)
    out = slots(me, gg, gu, route, wg, wu)
    got = lax.all_to_all(out, "ep", split_axis=0, concat_axis=0, tiled=True)
    p1a, p3b = pieces(at((1, 0), (3, 1)), *args, r1a, r1b)
    r3a, r3b = shift_dp(p1a, 1), shift_dp(p3b, -1)
    grad_gate, grad_up, grad_down = final(at((0, 0), (0, 1)), *args, r2a, r2b, r3a, r3b)

    experts = NY * NZ * NC
    one = (expert_ids[:, :, None] == jnp.arange(experts, dtype=i32)).astype(i32)
    named = jnp.sum(one, axis=1)
    token = jnp.arange(TOK, dtype=i32)
    lower = (token[None, :] < token[:, None]).astype(bf16)
    earlier = dot(lower, named.astype(bf16)).astype(i32)
    row = jnp.arange(experts * CAP, dtype=i32)
    code_of = jnp.repeat(jnp.where(named > 0, earlier, -1), CAP, axis=1)
    sel = code_of == (row % CAP)[None, :]
    got = got.reshape(experts * CAP, DA)
    grad_tokens = dot(sel.astype(bf16), got[:, :D]).astype(bf16)
    mine = sel[:, None, :] & (expert_ids[:, :, None] == (row // CAP)[None, None, :])
    grad_route = jnp.sum(jnp.where(mine, got[:, D].astype(f32), 0.0), axis=2).astype(bf16)

    return grad_tokens, grad_route, grad_gate, grad_up, grad_down


def solution(mesh):
    row = P(("ep", "dp"), None)
    expert = P("ep", None, None)
    return jax.shard_map(
        body,
        mesh=mesh,
        in_specs=(row, row, row, row, expert, expert, expert),
        out_specs=(row, row, P("ep", "dp", None), P("ep", "dp", None), P("ep", None, "dp")),
        check_vma=False,
    )
```

```python
import functools

import jax
import jax.numpy as jnp
from jax import lax
from jax.experimental import pallas as pl
from jax.experimental.pallas import tpu as pltpu
from jax.sharding import PartitionSpec as P

bf16 = jnp.bfloat16
f32 = jnp.float32
i32 = jnp.int32

NY, NZ, NC = 4, 8, 2
CAP = 8
TOK = 32
TOPK = 8
D = 2048
FF = 768
META = 128
DA = D + META
HALF = NY * NZ * CAP
ROWS = 2 * HALF
FB = 256
NFB = FF // FB
DY = (0, -1, 1, 2)
DZ = (0, -1, 1, -2, 2, -3, 3, 4)
NDP = 4
PIECE = D // NDP // 2
VLIM = 60 * 1024 * 1024

contract_last = (((1,), (1,)), ((), ()))
contract_first = (((0,), (0,)), ((), ()))
nothing = (((1,), (0,)), ((), ()))


def dot(a, b, dims=nothing):
    return lax.dot_general(a, b, dims, preferred_element_type=f32)


def flat(y, z, c):
    return ((y % NY) * NZ + (z % NZ)) * NC + c


def shift(arr, dy=0, dz=0):
    pairs = [
        (flat(y, z, c), flat(y + dy, z + dz, c))
        for y in range(NY)
        for z in range(NZ)
        for c in range(NC)
    ]
    return lax.ppermute(arr, "ep", pairs)


def swap_core(arr):
    return lax.ppermute(arr, "ep", [(i, i ^ 1) for i in range(NY * NZ * NC)])


def shift_dp(arr, by):
    return lax.ppermute(arr, "dp", [(i, (i + by) % NDP) for i in range(NDP)])


def join_kernel(count, *refs):
    out_ref = refs[-1]
    at = 0
    for ref in refs[:count]:
        out_ref[at : at + ref.shape[0], :] = ref[...]
        at += ref.shape[0]


def join(parts, after=()):
    rows = sum(part.shape[0] for part in parts)
    return pl.pallas_call(
        functools.partial(join_kernel, len(parts)),
        out_shape=jax.ShapeDtypeStruct((rows, parts[0].shape[1]), parts[0].dtype),
        in_specs=[VM] * len(parts) + [pl.BlockSpec(memory_space=pl.ANY)] * len(after),
        out_specs=VM,
        name="join",
    )(*parts, *after)


def cost(flops):
    return pl.CostEstimate(flops=flops, transcendentals=0, bytes_accessed=0)


VM = pl.BlockSpec(memory_space=pltpu.VMEM)
SM = pl.BlockSpec(memory_space=pltpu.SMEM)


def iota(shape, dim):
    return lax.broadcasted_iota(i32, shape, dim)


def pick_x_kernel(me_ref, *refs):
    blocks = refs[:5]
    own_ref, sib_ref, code_ref, meta_scr, sel_scr = refs[5:]
    me = me_ref[0]
    n = NZ * TOK
    at = 0
    for ref in blocks:
        meta_scr[at : at + ref.shape[0]] = ref[:, D:]
        at += ref.shape[0]
    lane = iota((n, META), 1)
    tok = iota((n, META), 0)
    low = iota((n, n), 0)
    col = iota((n, n), 1)
    before = jnp.where((col < low) & (col // TOK == low // TOK), 1.0, 0.0).astype(bf16)
    which = iota((2 * META, META), 0) // META == iota((2 * META, META), 1) // 64
    spread = jnp.where(which, 1.0, 0.0).astype(bf16)
    row_pos = (lane % CAP).astype(f32)
    here = tok // TOK == (lane % 64) // CAP
    mine = me.astype(f32)
    other = (me ^ 1).astype(f32)

    def step(b, _):
        part = pl.ds(pl.multiple_of(b * n, n), n)
        meta = meta_scr[part].astype(f32)
        ids = lane < TOPK
        hits = jnp.concatenate(
            [
                jnp.where(ids & (meta == mine), 1.0, 0.0).astype(bf16),
                jnp.where(ids & (meta == other), 1.0, 0.0).astype(bf16),
            ],
            axis=1,
        )
        named = dot(hits, spread)
        earlier = dot(before, named.astype(bf16))
        code = jnp.where(named > 0, earlier, -1.0)
        code_ref[b] = code.astype(bf16)
        sel_scr[part] = jnp.where((code == row_pos) & here, 1.0, 0.0).astype(bf16)
        return 0

    lax.fori_loop(0, NY, step, 0)
    for b in range(NY):
        mine_refs = blocks[b : b + 1] if b < 3 else blocks[3:]
        rows = 0.0
        at = b * n
        for ref in mine_refs:
            size = ref.shape[0]
            rows = rows + dot(sel_scr[at : at + size], ref[...], contract_first)
            at += size
        rows = rows.astype(bf16)
        own_ref[b * 64 : (b + 1) * 64, :] = rows[:64]
        sib_ref[b * 64 : (b + 1) * 64, :] = rows[64:]


def pick_x(me, blocks):
    return pl.pallas_call(
        pick_x_kernel,
        out_shape=(
            jax.ShapeDtypeStruct((HALF, DA), bf16),
            jax.ShapeDtypeStruct((HALF, DA), bf16),
            jax.ShapeDtypeStruct((NY, NZ * TOK, META), bf16),
        ),
        in_specs=[SM] + [VM] * 5,
        out_specs=(VM, VM, VM),
        scratch_shapes=[
            pltpu.VMEM((NY * NZ * TOK, META), bf16), pltpu.VMEM((NY * NZ * TOK, META), bf16),
        ],
        compiler_params=pltpu.CompilerParams(vmem_limit_bytes=VLIM),
        name="pick_x",
    )(me, *blocks)


def pick_cot_kernel(code_ref, *refs):
    blocks = refs[:9]
    own_ref, sib_ref, own_acc, sib_acc = refs[10:]
    n = NY * TOK
    lane = iota((n, META), 1)
    tok = iota((n, META), 0)
    row_pos = (lane % CAP).astype(f32)
    row_src = (lane % 64) // CAP
    place = 0
    for s in range(NZ):
        if DZ[s] == 4:
            blk = jnp.concatenate([blocks[place][...], blocks[place + 1][...]], axis=0)
            place += 2
        else:
            blk = blocks[place][...]
            place += 1
        code = jnp.concatenate(
            [code_ref[b, s * TOK : (s + 1) * TOK, :] for b in range(NY)], axis=0
        ).astype(f32)
        sel = jnp.where((code == row_pos) & (tok // TOK == row_src), 1.0, 0.0).astype(bf16)
        rows = dot(sel, blk, contract_first)
        for b in range(NY):
            at = b * 64 + s * CAP
            own_acc[at : at + CAP, :] = rows[b * CAP : (b + 1) * CAP]
            sib_acc[at : at + CAP, :] = rows[64 + b * CAP : 64 + (b + 1) * CAP]
    own_ref[...] = own_acc[...].astype(bf16)
    sib_ref[...] = sib_acc[...].astype(bf16)


def pick_cot(code, blocks, after):
    return pl.pallas_call(
        pick_cot_kernel,
        out_shape=(
            jax.ShapeDtypeStruct((HALF, D), bf16),
            jax.ShapeDtypeStruct((HALF, D), bf16),
        ),
        in_specs=[VM] * 10 + [pl.BlockSpec(memory_space=pl.ANY)],
        out_specs=(VM, VM),
        scratch_shapes=[pltpu.VMEM((HALF, D), f32), pltpu.VMEM((HALF, D), f32)],
        compiler_params=pltpu.CompilerParams(vmem_limit_bytes=VLIM),
        cost_estimate=cost(20_000_000_000),
        name="pick_cot",
    )(code, *blocks, after)


def front_kernel(
    me_ref, own_ref, sib_ref, wg_ref, wu_ref,
    hid_ref, hid_t_ref, a_ref, b_ref, weight_ref, x_scr,
):
    @pl.when(pl.program_id(0) == 0)
    def _():
        x_scr[:HALF] = own_ref[:, :D]
        x_scr[HALF:] = sib_ref[:, :D]
        meta = jnp.concatenate([own_ref[:, D:], sib_ref[:, D:]], axis=0).astype(f32)
        expert = me_ref[0].astype(f32)
        total = jnp.zeros((ROWS, 1), f32)
        for k in range(TOPK):
            total = total + jnp.where(
                meta[:, k : k + 1] == expert, meta[:, TOPK + k : TOPK + k + 1], 0.0
            )
        weight_ref[...] = jnp.broadcast_to(total, (ROWS, META))

    x = x_scr[...]
    gate = dot(x, wg_ref[...])
    up = dot(x, wu_ref[...])
    sig = jax.nn.sigmoid(gate)
    act = gate * sig
    hid = (act * up).astype(bf16)
    hid_ref[...] = hid
    hid_t_ref[...] = hid.T
    a_ref[...] = up * (sig * (1.0 + gate * (1.0 - sig)))
    b_ref[...] = act


def front(me, own, sib, wg, wu):
    whole = lambda shape: pl.BlockSpec(shape, lambda j: (0,) * len(shape))
    wide = pl.BlockSpec((ROWS, FB), lambda j: (0, j))
    return pl.pallas_call(
        front_kernel,
        grid=(NFB,),
        out_shape=(
            jax.ShapeDtypeStruct((ROWS, FF), bf16),
            jax.ShapeDtypeStruct((FF, ROWS), bf16),
            jax.ShapeDtypeStruct((ROWS, FF), f32),
            jax.ShapeDtypeStruct((ROWS, FF), f32),
            jax.ShapeDtypeStruct((ROWS, META), f32),
        ),
        in_specs=[
            SM, whole((HALF, DA)), whole((HALF, DA)),
            pl.BlockSpec((D, FB), lambda j: (0, j)),
            pl.BlockSpec((D, FB), lambda j: (0, j)),
        ],
        out_specs=(
            wide, pl.BlockSpec((FB, ROWS), lambda j: (j, 0)), wide, wide,
            whole((ROWS, META)),
        ),
        scratch_shapes=[pltpu.VMEM((ROWS, D), bf16)],
        compiler_params=pltpu.CompilerParams(vmem_limit_bytes=VLIM),
        cost_estimate=cost(1_000_000_000),
        name="front",
    )(me, own, sib, wg, wu)


def piece_into(out_ref, x_own, x_sib, gg_ref, gu_ref, hid_t_ref, scot_cols):
    for n, ref in enumerate((gg_ref, gu_ref)):
        value = dot(x_own, ref[:HALF], contract_first) + dot(x_sib, ref[HALF:], contract_first)
        out_ref[:, n * FF : (n + 1) * FF] = value.astype(bf16)
    for q in range(NFB):
        value = dot(hid_t_ref[q * FB : (q + 1) * FB], scot_cols)
        out_ref[:, 2 * FF + q * FB : 2 * FF + (q + 1) * FB] = value.astype(bf16)


def place(pos_ref, piece):
    return (2 * pos_ref[1] + piece) % (2 * NDP)


def mid_kernel(
    pos_ref, own_ref, sib_ref, hid_ref, hid_t_ref, a_ref, b_ref, weight_ref,
    xoa_ref, xsa_ref, xob_ref, xsb_ref, wd_ref,
    pa_ref, pb_ref, gg_ref, gu_ref, route_ref, scot_ref, cot_scr, x_scr, out_scr,
):
    j = pl.program_id(0)

    @pl.when(j == 0)
    def _():
        cot_scr[:HALF] = own_ref[...]
        cot_scr[HALF:] = sib_ref[...]
        weight = weight_ref[:, :1]
        scot_ref[...] = (weight * cot_scr[...].astype(f32)).astype(bf16)
        route_ref[...] = jnp.zeros_like(route_ref)
        for n, ref in enumerate((xoa_ref, xsa_ref, xob_ref, xsb_ref)):
            x_scr[n] = ref[...]

    back = dot(cot_scr[...], wd_ref[...], contract_last)
    part = jnp.sum(hid_ref[...].astype(f32) * back, axis=1, keepdims=True)
    route_ref[...] += jnp.broadcast_to(part, (ROWS, META))
    scaled = weight_ref[:, :1] * back
    cols = pl.ds(pl.multiple_of(j * FB, FB), FB)
    gg_ref[:, cols] = (scaled * a_ref[...]).astype(bf16)
    gu_ref[:, cols] = (scaled * b_ref[...]).astype(bf16)

    @pl.when(j == NFB - 1)
    def _():
        def step(n, _):
            some = pl.ds(pl.multiple_of(place(pos_ref, 4 + n) * PIECE, PIECE), PIECE)
            piece_into(
                out_scr.at[n], x_scr[2 * n], x_scr[2 * n + 1], gg_ref, gu_ref, hid_t_ref,
                scot_ref[:, some],
            )
            return 0

        lax.fori_loop(0, 2, step, 0)
        pa_ref[...] = out_scr[0]
        pb_ref[...] = out_scr[1]


def whole(shape):
    return pl.BlockSpec(shape, lambda *_: (0,) * len(shape))


def mid(pos, own, sib, hid, hid_t, a, b, weight, x_own, x_sib, wd):
    wide = pl.BlockSpec((ROWS, FB), lambda j, pos_ref: (0, j))
    xa = pl.BlockSpec((HALF, PIECE), lambda j, pos_ref: (0, place(pos_ref, 4)))
    xb = pl.BlockSpec((HALF, PIECE), lambda j, pos_ref: (0, place(pos_ref, 5)))
    return pl.pallas_call(
        mid_kernel,
        out_shape=(
            jax.ShapeDtypeStruct((PIECE, 3 * FF), bf16),
            jax.ShapeDtypeStruct((PIECE, 3 * FF), bf16),
            jax.ShapeDtypeStruct((ROWS, FF), bf16),
            jax.ShapeDtypeStruct((ROWS, FF), bf16),
            jax.ShapeDtypeStruct((ROWS, META), f32),
            jax.ShapeDtypeStruct((ROWS, D), bf16),
        ),
        grid_spec=pltpu.PrefetchScalarGridSpec(
            num_scalar_prefetch=1,
            grid=(NFB,),
            in_specs=[
                whole((HALF, D)), whole((HALF, D)), wide, whole((FF, ROWS)), wide, wide,
                whole((ROWS, META)), xa, xa, xb, xb,
                pl.BlockSpec((FB, D), lambda j, pos_ref: (j, 0)),
            ],
            out_specs=(
                whole((PIECE, 3 * FF)), whole((PIECE, 3 * FF)), whole((ROWS, FF)),
                whole((ROWS, FF)), whole((ROWS, META)), whole((ROWS, D)),
            ),
            scratch_shapes=[
                pltpu.VMEM((ROWS, D), bf16),
                pltpu.VMEM((4, HALF, PIECE), bf16),
                pltpu.VMEM((2, PIECE, 3 * FF), bf16),
            ],
        ),
        compiler_params=pltpu.CompilerParams(vmem_limit_bytes=VLIM),
        name="mid",
    )(pos, own, sib, hid, hid_t, a, b, weight, x_own, x_sib, x_own, x_sib, wd)


def rest_piece(n):
    first = jnp.where(n == 0, 3, 6)
    second = jnp.where(n == 2, 2, 7)
    return jnp.where(n < 2, first, jnp.where(n < 4, second, n - 4))


def rest_kernel(
    pos_ref, x_own_ref, x_sib_ref, scot_ref, gg_ref, gu_ref, hid_t_ref,
    pa_ref, pb_ref, more_ref, out_scr,
):
    n = pl.program_id(0)
    piece_into(
        out_scr, x_own_ref[...], x_sib_ref[...], gg_ref, gu_ref, hid_t_ref, scot_ref[...]
    )

    @pl.when(n == 0)
    def _():
        pa_ref[...] = out_scr[...]

    @pl.when(n == 1)
    def _():
        pb_ref[...] = out_scr[...]

    @pl.when(n > 1)
    def _():
        more_ref[...] = out_scr[...]


def rest(pos, x_own, x_sib, scot, gg, gu, hid_t):
    size = (PIECE, 3 * FF)
    x_spec = pl.BlockSpec((HALF, PIECE), lambda n, pos_ref: (0, place(pos_ref, rest_piece(n))))
    return pl.pallas_call(
        rest_kernel,
        out_shape=(
            jax.ShapeDtypeStruct(size, bf16),
            jax.ShapeDtypeStruct(size, bf16),
            jax.ShapeDtypeStruct((4 * PIECE, 3 * FF), bf16),
        ),
        grid_spec=pltpu.PrefetchScalarGridSpec(
            num_scalar_prefetch=1,
            grid=(6,),
            in_specs=[
                x_spec, x_spec,
                pl.BlockSpec((ROWS, PIECE), lambda n, pos_ref: (0, place(pos_ref, rest_piece(n)))),
                whole((ROWS, FF)), whole((ROWS, FF)), whole((FF, ROWS)),
            ],
            out_specs=(
                whole(size), whole(size),
                pl.BlockSpec(size, lambda n, pos_ref: (jnp.maximum(n - 2, 0), 0)),
            ),
            scratch_shapes=[pltpu.VMEM(size, bf16)],
        ),
        compiler_params=pltpu.CompilerParams(vmem_limit_bytes=VLIM),
        name="rest",
    )(pos, x_own, x_sib, scot, gg, gu, hid_t)


def add_kernel(more_ref, ra_ref, rb_ref, _, oa_ref, ob_ref):
    for n, (r_ref, o_ref) in enumerate(((ra_ref, oa_ref), (rb_ref, ob_ref))):
        value = more_ref[n * PIECE : (n + 1) * PIECE].astype(f32) + r_ref[...].astype(f32)
        o_ref[...] = value.astype(bf16)


def add(more, ra, rb, after):
    size = (PIECE, 3 * FF)
    thin = pl.BlockSpec((PIECE, FF), lambda j: (0, j))
    return pl.pallas_call(
        add_kernel,
        grid=(3,),
        out_shape=(jax.ShapeDtypeStruct(size, bf16), jax.ShapeDtypeStruct(size, bf16)),
        in_specs=[
            pl.BlockSpec((2 * PIECE, FF), lambda j: (0, j)), thin, thin,
            pl.BlockSpec(memory_space=pl.ANY),
        ],
        out_specs=(thin, thin),
        name="add",
    )(more, ra, rb, after)


def final_kernel(more_ref, r2a, r2b, r3a, r3b, gate_ref, up_ref, down_ref):
    j = pl.program_id(0)
    for n, refs in enumerate(((r2a, r3a), (r2b, r3b))):
        side = slice(n * PIECE, (n + 1) * PIECE)
        value = more_ref[side].astype(f32)
        for ref in refs:
            value = value + ref[...].astype(f32)
        value = value.astype(bf16)

        @pl.when(j == 0)
        def _():
            gate_ref[0, side, :] = value

        @pl.when(j == 1)
        def _():
            up_ref[0, side, :] = value

        @pl.when(j == 2)
        def _():
            for q in range(NFB):
                down_ref[0, q * FB : (q + 1) * FB, side] = value[:, q * FB : (q + 1) * FB]


def final(more, *arrived):
    per = D // NDP
    thin = pl.BlockSpec((PIECE, FF), lambda j: (0, j))
    return pl.pallas_call(
        final_kernel,
        grid=(3,),
        out_shape=(
            jax.ShapeDtypeStruct((1, per, FF), bf16),
            jax.ShapeDtypeStruct((1, per, FF), bf16),
            jax.ShapeDtypeStruct((1, FF, per), bf16),
        ),
        in_specs=[pl.BlockSpec((2 * PIECE, FF), lambda j: (1, j))] + [thin] * 4,
        out_specs=(whole((1, per, FF)), whole((1, per, FF)), whole((1, FF, per))),
        compiler_params=pltpu.CompilerParams(vmem_limit_bytes=VLIM),
        cost_estimate=cost(30_000_000_000),
        name="final",
    )(more, *arrived)


def slots_kernel(me_ref, gg_ref, gu_ref, route_ref, wg_ref, wu_ref, _, out_ref, scr):
    me = me_ref[0]
    core = me % NC
    z = (me // NC) % NZ
    y = me // (NC * NZ)
    quarter = ROWS // 4

    def part(i, _):
        rows = pl.ds(pl.multiple_of(i * quarter, quarter), quarter)
        scr[rows] = dot(gg_ref[rows], wg_ref[...], contract_last) + dot(
            gu_ref[rows], wu_ref[...], contract_last
        )
        return 0

    lax.fori_loop(0, 4, part, 0)

    def put(i, _):
        h, b, s = i // (NY * NZ), (i // NZ) % NY, i % NZ
        dy = jnp.where(b == 1, NY - 1, jnp.where(b == 2, 1, b - b // 3))
        dz = jnp.where(s % 2 == 1, NZ - (s + 1) // 2, s // 2)
        to = (((y + dy) % NY) * NZ + (z + dz) % NZ) * NC + (core + h) % NC
        rows = pl.ds(pl.multiple_of(i * CAP, CAP), CAP)
        out_ref[to, :, :D] = scr[rows, :].astype(bf16)
        out_ref[to, :, D:] = route_ref[rows, :].astype(bf16)
        return 0

    lax.fori_loop(0, 2 * NY * NZ, put, 0)


def slots(me, gg, gu, route, wg, wu, after):
    return pl.pallas_call(
        slots_kernel,
        out_shape=jax.ShapeDtypeStruct((NY * NZ * NC, CAP, DA), bf16),
        in_specs=[SM] + [VM] * 5 + [pl.BlockSpec(memory_space=pl.ANY)],
        out_specs=VM,
        scratch_shapes=[pltpu.VMEM((ROWS, D), f32)],
        compiler_params=pltpu.CompilerParams(vmem_limit_bytes=VLIM),
        name="slots",
    )(me, gg, gu, route, wg, wu, after)


def body(tokens, cotangent, expert_ids, route_weights, w_gate, w_up, w_down):
    pos = jnp.stack([lax.axis_index("ep"), lax.axis_index("dp")]).astype(i32)
    meta = jnp.concatenate(
        [expert_ids.astype(bf16), route_weights, jnp.zeros((TOK, META - 2 * TOPK), bf16)], axis=1
    )
    xa = jnp.concatenate([tokens, meta], axis=1)

    c1 = shift(cotangent, dy=1)
    c2 = shift(cotangent, dy=-1)
    c3 = shift(c1, dy=1)

    u = [xa]
    d = [xa]
    for _ in range(3):
        u.append(shift(u[-1], dz=1))
        d.append(shift(d[-1], dz=-1))
    u.append(shift(u[-1], dz=1))

    def ring_y(part):
        p1 = shift(part, dy=1)
        m1 = shift(part, dy=-1)
        n = part.shape[0] // 2
        return part, p1, m1, shift(p1[:n], dy=1), shift(m1[n:], dy=-1)

    blocks = ring_y(join([xa, u[1], d[1], u[2], d[2], u[3], d[3], u[4]], after=[c2, c3]))
    cot0 = join([cotangent, c1, c2, c3], after=[u[3], d[3]])
    cu = [cot0]
    cd = [cot0]
    for _ in range(3):
        cu.append(shift(cu[-1], dz=1))
        cd.append(shift(cd[-1], dz=-1))
    n = NY * TOK // 2
    cq = [shift(cu[-1][:n], dz=1), shift(cd[-1][n:], dz=-1)]

    own_x, sib_x, code = pick_x(pos, blocks)
    sib_x = swap_core(sib_x)
    wg, wu, wd = w_gate[0], w_up[0], w_down[0]
    hid, hid_t, a, b, weight = front(pos, own_x, sib_x, wg, wu)

    parts = [cot0, cu[1], cd[1], cu[2], cd[2], cu[3], cd[3], *cq]
    own_c, sib_c = pick_cot(code, parts, after=hid)
    sib_c = swap_core(sib_c)

    p2a, p2b, gg, gu, route, scot = mid(
        pos, own_c, sib_c, hid, hid_t, a, b, weight, own_x, sib_x, wd
    )
    r1a, r1b = shift_dp(p2a, 1), shift_dp(p2b, -1)
    p1b, p3a, more = rest(pos, own_x, sib_x, scot, gg, gu, hid_t)
    r2b, r2a = shift_dp(p1b, 1), shift_dp(p3a, -1)
    out = slots(pos, gg, gu, route, wg, wu, after=p1b)
    got = lax.all_to_all(out, "ep", split_axis=0, concat_axis=0, tiled=True)
    p1a, p3b = add(more, r1a, r1b, after=out)
    r3a, r3b = shift_dp(p1a, 1), shift_dp(p3b, -1)
    grad_gate, grad_up, grad_down = final(more, r2a, r2b, r3a, r3b)

    experts = NY * NZ * NC
    one = (expert_ids[:, :, None] == jnp.arange(experts, dtype=i32)).astype(i32)
    named = jnp.sum(one, axis=1)
    token = jnp.arange(TOK, dtype=i32)
    lower = (token[None, :] < token[:, None]).astype(bf16)
    earlier = dot(lower, named.astype(bf16)).astype(i32)
    row = jnp.arange(experts * CAP, dtype=i32)
    code_of = jnp.repeat(jnp.where(named > 0, earlier, -1), CAP, axis=1)
    sel = code_of == (row % CAP)[None, :]
    got = got.reshape(experts * CAP, DA)
    grad_tokens = dot(sel.astype(bf16), got[:, :D]).astype(bf16)
    mine = sel[:, None, :] & (expert_ids[:, :, None] == (row // CAP)[None, None, :])
    grad_route = jnp.sum(jnp.where(mine, got[:, D].astype(f32), 0.0), axis=2).astype(bf16)

    return grad_tokens, grad_route, grad_gate, grad_up, grad_down


def solution(mesh):
    row = P(("ep", "dp"), None)
    expert = P("ep", None, None)
    return jax.shard_map(
        body,
        mesh=mesh,
        in_specs=(row, row, row, row, expert, expert, expert),
        out_specs=(row, row, P("ep", "dp", None), P("ep", "dp", None), P("ep", None, "dp")),
        check_vma=False,
    )
```

```python
import functools

import jax
import jax.numpy as jnp
from jax import lax
from jax.experimental import pallas as pl
from jax.experimental.pallas import tpu as pltpu
from jax.sharding import PartitionSpec as P

bf16 = jnp.bfloat16
f32 = jnp.float32
i32 = jnp.int32

NY, NZ, NC = 4, 8, 2
CAP = 8
TOK = 32
TOPK = 8
D = 2048
FF = 768
META = 128
DA = D + META
HALF = NY * NZ * CAP
ROWS = 2 * HALF
FB = 256
NFB = FF // FB
DY = (0, -1, 1, 2)
DZ = (0, -1, 1, -2, 2, -3, 3, 4)
NDP = 4
PIECE = D // NDP // 2
VLIM = 60 * 1024 * 1024

contract_last = (((1,), (1,)), ((), ()))
contract_first = (((0,), (0,)), ((), ()))
nothing = (((1,), (0,)), ((), ()))


def dot(a, b, dims=nothing):
    return lax.dot_general(a, b, dims, preferred_element_type=f32)


def flat(y, z, c):
    return ((y % NY) * NZ + (z % NZ)) * NC + c


def shift(arr, dy=0, dz=0):
    pairs = [
        (flat(y, z, c), flat(y + dy, z + dz, c))
        for y in range(NY)
        for z in range(NZ)
        for c in range(NC)
    ]
    return lax.ppermute(arr, "ep", pairs)


def swap_core(arr):
    return lax.ppermute(arr, "ep", [(i, i ^ 1) for i in range(NY * NZ * NC)])


def shift_dp(arr, by):
    return lax.ppermute(arr, "dp", [(i, (i + by) % NDP) for i in range(NDP)])


def join_kernel(count, *refs):
    out_ref = refs[-1]
    at = 0
    for ref in refs[:count]:
        out_ref[at : at + ref.shape[0], :] = ref[...]
        at += ref.shape[0]


def halves_kernel(a_ref, b_ref, *refs):
    n = a_ref.shape[0] // 2
    refs[-2][...] = a_ref[:n]
    refs[-1][...] = b_ref[n:]


def halves(a, b, after):
    half = jax.ShapeDtypeStruct((a.shape[0] // 2, a.shape[1]), a.dtype)
    return pl.pallas_call(
        halves_kernel,
        out_shape=(half, half),
        in_specs=[VM, VM] + [pl.BlockSpec(memory_space=pl.ANY)] * len(after),
        out_specs=(VM, VM),
        name="halves",
    )(a, b, *after)


def join(parts, after=()):
    rows = sum(part.shape[0] for part in parts)
    return pl.pallas_call(
        functools.partial(join_kernel, len(parts)),
        out_shape=jax.ShapeDtypeStruct((rows, parts[0].shape[1]), parts[0].dtype),
        in_specs=[VM] * len(parts) + [pl.BlockSpec(memory_space=pl.ANY)] * len(after),
        out_specs=VM,
        name="join",
    )(*parts, *after)


def cost(flops):
    return pl.CostEstimate(flops=flops, transcendentals=0, bytes_accessed=0)


VM = pl.BlockSpec(memory_space=pltpu.VMEM)
SM = pl.BlockSpec(memory_space=pltpu.SMEM)


def iota(shape, dim):
    return lax.broadcasted_iota(i32, shape, dim)


def pick_x_kernel(me_ref, *refs):
    blocks = refs[:5]
    own_ref, sib_ref, code_ref, meta_scr, sel_scr = refs[5:]
    me = me_ref[0]
    n = NZ * TOK
    at = 0
    for ref in blocks:
        meta_scr[at : at + ref.shape[0]] = ref[:, D:]
        at += ref.shape[0]
    lane = iota((n, META), 1)
    tok = iota((n, META), 0)
    low = iota((n, n), 0)
    col = iota((n, n), 1)
    before = jnp.where((col < low) & (col // TOK == low // TOK), 1.0, 0.0).astype(bf16)
    which = iota((2 * META, META), 0) // META == iota((2 * META, META), 1) // 64
    spread = jnp.where(which, 1.0, 0.0).astype(bf16)
    row_pos = (lane % CAP).astype(f32)
    here = tok // TOK == (lane % 64) // CAP
    mine = me.astype(f32)
    other = (me ^ 1).astype(f32)

    def step(b, _):
        part = pl.ds(pl.multiple_of(b * n, n), n)
        meta = meta_scr[part].astype(f32)
        ids = lane < TOPK
        hits = jnp.concatenate(
            [
                jnp.where(ids & (meta == mine), 1.0, 0.0).astype(bf16),
                jnp.where(ids & (meta == other), 1.0, 0.0).astype(bf16),
            ],
            axis=1,
        )
        named = dot(hits, spread)
        earlier = dot(before, named.astype(bf16))
        code = jnp.where(named > 0, earlier, -1.0)
        code_ref[b] = code.astype(bf16)
        sel_scr[part] = jnp.where((code == row_pos) & here, 1.0, 0.0).astype(bf16)
        return 0

    lax.fori_loop(0, NY, step, 0)
    for b in range(NY):
        mine_refs = blocks[b : b + 1] if b < 3 else blocks[3:]
        rows = 0.0
        at = b * n
        for ref in mine_refs:
            size = ref.shape[0]
            rows = rows + dot(sel_scr[at : at + size], ref[...], contract_first)
            at += size
        rows = rows.astype(bf16)
        own_ref[b * 64 : (b + 1) * 64, :] = rows[:64]
        sib_ref[b * 64 : (b + 1) * 64, :] = rows[64:]


def pick_x(me, blocks):
    return pl.pallas_call(
        pick_x_kernel,
        out_shape=(
            jax.ShapeDtypeStruct((HALF, DA), bf16),
            jax.ShapeDtypeStruct((HALF, DA), bf16),
            jax.ShapeDtypeStruct((NY, NZ * TOK, META), bf16),
        ),
        in_specs=[SM] + [VM] * 5,
        out_specs=(VM, VM, VM),
        scratch_shapes=[
            pltpu.VMEM((NY * NZ * TOK, META), bf16), pltpu.VMEM((NY * NZ * TOK, META), bf16),
        ],
        compiler_params=pltpu.CompilerParams(vmem_limit_bytes=VLIM),
        name="pick_x",
    )(me, *blocks)


def pick_cot_kernel(code_ref, *refs):
    blocks = refs[:9]
    own_ref, sib_ref, own_acc, sib_acc = refs[10:]
    n = NY * TOK
    lane = iota((n, META), 1)
    tok = iota((n, META), 0)
    row_pos = (lane % CAP).astype(f32)
    row_src = (lane % 64) // CAP
    place = 0
    for s in range(NZ):
        if DZ[s] == 4:
            blk = jnp.concatenate([blocks[place][...], blocks[place + 1][...]], axis=0)
            place += 2
        else:
            blk = blocks[place][...]
            place += 1
        code = jnp.concatenate(
            [code_ref[b, s * TOK : (s + 1) * TOK, :] for b in range(NY)], axis=0
        ).astype(f32)
        sel = jnp.where((code == row_pos) & (tok // TOK == row_src), 1.0, 0.0).astype(bf16)
        rows = dot(sel, blk, contract_first)
        for b in range(NY):
            at = b * 64 + s * CAP
            own_acc[at : at + CAP, :] = rows[b * CAP : (b + 1) * CAP]
            sib_acc[at : at + CAP, :] = rows[64 + b * CAP : 64 + (b + 1) * CAP]
    own_ref[...] = own_acc[...].astype(bf16)
    sib_ref[...] = sib_acc[...].astype(bf16)


def pick_cot(code, blocks, after):
    return pl.pallas_call(
        pick_cot_kernel,
        out_shape=(
            jax.ShapeDtypeStruct((HALF, D), bf16),
            jax.ShapeDtypeStruct((HALF, D), bf16),
        ),
        in_specs=[VM] * 10 + [pl.BlockSpec(memory_space=pl.ANY)],
        out_specs=(VM, VM),
        scratch_shapes=[pltpu.VMEM((HALF, D), f32), pltpu.VMEM((HALF, D), f32)],
        compiler_params=pltpu.CompilerParams(vmem_limit_bytes=VLIM),
        cost_estimate=cost(PICK_COST),
        name="pick_cot",
    )(code, *blocks, after)


def front_kernel(
    me_ref, own_ref, sib_ref, wg_ref, wu_ref,
    hid_ref, hid_t_ref, a_ref, b_ref, weight_ref, x_scr,
):
    @pl.when(pl.program_id(0) == 0)
    def _():
        x_scr[:HALF] = own_ref[:, :D]
        x_scr[HALF:] = sib_ref[:, :D]
        meta = jnp.concatenate([own_ref[:, D:], sib_ref[:, D:]], axis=0).astype(f32)
        expert = me_ref[0].astype(f32)
        total = jnp.zeros((ROWS, 1), f32)
        for k in range(TOPK):
            total = total + jnp.where(
                meta[:, k : k + 1] == expert, meta[:, TOPK + k : TOPK + k + 1], 0.0
            )
        weight_ref[...] = jnp.broadcast_to(total, (ROWS, META))

    x = x_scr[...]
    gate = dot(x, wg_ref[...])
    up = dot(x, wu_ref[...])
    sig = jax.nn.sigmoid(gate)
    act = gate * sig
    hid = (act * up).astype(bf16)
    hid_ref[...] = hid
    hid_t_ref[...] = hid.T
    a_ref[...] = up * (sig * (1.0 + gate * (1.0 - sig)))
    b_ref[...] = act


def front(me, own, sib, wg, wu):
    whole = lambda shape: pl.BlockSpec(shape, lambda j: (0,) * len(shape))
    wide = pl.BlockSpec((ROWS, FB), lambda j: (0, j))
    return pl.pallas_call(
        front_kernel,
        grid=(NFB,),
        out_shape=(
            jax.ShapeDtypeStruct((ROWS, FF), bf16),
            jax.ShapeDtypeStruct((FF, ROWS), bf16),
            jax.ShapeDtypeStruct((ROWS, FF), f32),
            jax.ShapeDtypeStruct((ROWS, FF), f32),
            jax.ShapeDtypeStruct((ROWS, META), f32),
        ),
        in_specs=[
            SM, whole((HALF, DA)), whole((HALF, DA)),
            pl.BlockSpec((D, FB), lambda j: (0, j)),
            pl.BlockSpec((D, FB), lambda j: (0, j)),
        ],
        out_specs=(
            wide, pl.BlockSpec((FB, ROWS), lambda j: (j, 0)), wide, wide,
            whole((ROWS, META)),
        ),
        scratch_shapes=[pltpu.VMEM((ROWS, D), bf16)],
        compiler_params=pltpu.CompilerParams(vmem_limit_bytes=VLIM),
        cost_estimate=cost(FRONT_COST),
        name="front",
    )(me, own, sib, wg, wu)


def whole(shape):
    return pl.BlockSpec(shape, lambda *_: (0,) * len(shape))


def place(pos_ref, piece):
    return (2 * pos_ref[1] + piece) % (2 * NDP)


def scale(weight_ref, own, sib):
    weight = weight_ref[:, :1]
    cot = jnp.concatenate([own, sib], axis=0)
    return (weight * cot.astype(f32)).astype(bf16)


def piece_into(out_ref, x_own, x_sib, g_ref, hid_t_ref, scot_cols):
    def side(n, _):
        value = dot(x_own, g_ref[n, :HALF], contract_first)
        value = value + dot(x_sib, g_ref[n, HALF:], contract_first)
        out_ref[:, pl.ds(pl.multiple_of(n * FF, FF), FF)] = value.astype(out_ref.dtype)
        return 0

    lax.fori_loop(0, 2, side, 0)
    for q in range(NFB):
        value = dot(hid_t_ref[q * FB : (q + 1) * FB], scot_cols)
        out_ref[:, 2 * FF + q * FB : 2 * FF + (q + 1) * FB] = value.astype(out_ref.dtype)


def mid_kernel(
    pos_ref, own_ref, sib_ref, hid_ref, hid_t_ref, a_ref, b_ref, weight_ref,
    xoa_ref, xsa_ref, xob_ref, xsb_ref, wd_ref,
    pa_ref, pb_ref, g_ref, route_ref, cot_scr, x_scr, out_scr,
):
    j = pl.program_id(0)

    @pl.when(j == 0)
    def _():
        cot_scr[:HALF] = own_ref[...]
        cot_scr[HALF:] = sib_ref[...]
        route_ref[...] = jnp.zeros_like(route_ref)
        for n, ref in enumerate((xoa_ref, xsa_ref, xob_ref, xsb_ref)):
            x_scr[n] = ref[...]

    back = dot(cot_scr[...], wd_ref[...], contract_last)
    part = jnp.sum(hid_ref[...].astype(f32) * back, axis=1, keepdims=True)
    route_ref[...] += jnp.broadcast_to(part, (ROWS, META))
    scaled = weight_ref[:, :1] * back
    cols = pl.ds(pl.multiple_of(j * FB, FB), FB)
    g_ref[0, :, cols] = (scaled * a_ref[...]).astype(bf16)
    g_ref[1, :, cols] = (scaled * b_ref[...]).astype(bf16)

    @pl.when(j == NFB - 1)
    def _():
        def step(n, _):
            some = pl.ds(pl.multiple_of(place(pos_ref, 4 + n) * PIECE, PIECE), PIECE)
            piece_into(
                out_scr.at[n], x_scr[2 * n], x_scr[2 * n + 1], g_ref, hid_t_ref,
                scale(weight_ref, own_ref[:, some], sib_ref[:, some]),
            )
            return 0

        lax.fori_loop(0, 2, step, 0)
        pa_ref[...] = out_scr[0]
        pb_ref[...] = out_scr[1]


def mid(pos, own, sib, hid, hid_t, a, b, weight, x_own, x_sib, wd):
    wide = pl.BlockSpec((ROWS, FB), lambda j, pos_ref: (0, j))
    xa = pl.BlockSpec((HALF, PIECE), lambda j, pos_ref: (0, place(pos_ref, 4)))
    xb = pl.BlockSpec((HALF, PIECE), lambda j, pos_ref: (0, place(pos_ref, 5)))
    return pl.pallas_call(
        mid_kernel,
        out_shape=(
            jax.ShapeDtypeStruct((PIECE, 3 * FF), bf16),
            jax.ShapeDtypeStruct((PIECE, 3 * FF), bf16),
            jax.ShapeDtypeStruct((2, ROWS, FF), bf16),
            jax.ShapeDtypeStruct((ROWS, META), f32),
        ),
        grid_spec=pltpu.PrefetchScalarGridSpec(
            num_scalar_prefetch=1,
            grid=(NFB,),
            in_specs=[
                whole((HALF, D)), whole((HALF, D)), wide, whole((FF, ROWS)), wide, wide,
                whole((ROWS, META)), xa, xa, xb, xb,
                pl.BlockSpec((FB, D), lambda j, pos_ref: (j, 0)),
            ],
            out_specs=(
                whole((PIECE, 3 * FF)), whole((PIECE, 3 * FF)), whole((2, ROWS, FF)),
                whole((ROWS, META)),
            ),
            scratch_shapes=[
                pltpu.VMEM((ROWS, D), bf16),
                pltpu.VMEM((4, HALF, PIECE), bf16),
                pltpu.VMEM((2, PIECE, 3 * FF), bf16),
            ],
        ),
        compiler_params=pltpu.CompilerParams(vmem_limit_bytes=VLIM),
        name="mid",
    )(pos, own, sib, hid, hid_t, a, b, weight, x_own, x_sib, x_own, x_sib, wd)


def pick_pieces(*which):
    def index(n, pos_ref):
        piece = which[0]
        for i in range(1, len(which)):
            piece = jnp.where(n == i, which[i], piece)
        return (0, place(pos_ref, piece))

    half = pl.BlockSpec((HALF, PIECE), index)
    return [half] * 4 + [whole((ROWS, META)), whole((2, ROWS, FF)), whole((FF, ROWS))]


def plain_kernel(
    pos_ref, xo, xs, co, cs, weight_ref, g_ref, hid_t_ref, a_ref, b_ref, own_ref, scr
):
    piece_into(scr, xo[...], xs[...], g_ref, hid_t_ref, scale(weight_ref, co[...], cs[...]))

    @pl.when(pl.program_id(0) == 0)
    def _():
        a_ref[...] = scr[...]

    @pl.when(pl.program_id(0) == 1)
    def _():
        b_ref[...] = scr[...]

    @pl.when(pl.program_id(0) > 1)
    def _():
        own_ref[...] = scr[...]


def plain(pos, *args):
    size = (PIECE, 3 * FF)
    return pl.pallas_call(
        plain_kernel,
        out_shape=(
            jax.ShapeDtypeStruct(size, bf16),
            jax.ShapeDtypeStruct(size, bf16),
            jax.ShapeDtypeStruct((2 * PIECE, 3 * FF), bf16),
        ),
        grid_spec=pltpu.PrefetchScalarGridSpec(
            num_scalar_prefetch=1,
            grid=(4,),
            in_specs=pick_pieces(3, 6, 0, 1),
            out_specs=(
                whole(size), whole(size),
                pl.BlockSpec(size, lambda n, pos_ref: (jnp.maximum(n - 2, 0), 0)),
            ),
            scratch_shapes=[pltpu.VMEM(size, bf16)],
        ),
        compiler_params=pltpu.CompilerParams(vmem_limit_bytes=VLIM),
        name="plain",
    )(pos, *args)


def added_kernel(
    pos_ref, xo, xs, co, cs, weight_ref, g_ref, hid_t_ref, ra_ref, rb_ref,
    a_ref, ad_ref, b_ref, bd_ref, scr,
):
    piece_into(
        scr, xo[...], xs[...], g_ref, hid_t_ref, scale(weight_ref, co[...], cs[...])
    )
    for n, (r_ref, o_ref, d_ref) in enumerate(((ra_ref, a_ref, ad_ref), (rb_ref, b_ref, bd_ref))):

        @pl.when(pl.program_id(0) == n)
        def _():
            o_ref[...] = (scr[:, : 2 * FF] + r_ref[:, : 2 * FF].astype(f32)).astype(bf16)
            d_ref[...] = (scr[:, 2 * FF :] + r_ref[:, 2 * FF :].astype(f32)).astype(bf16)


def added(pos, *args):
    size = (PIECE, 3 * FF)
    sizes = ((PIECE, 2 * FF), (PIECE, FF)) * 2
    return pl.pallas_call(
        added_kernel,
        out_shape=tuple(jax.ShapeDtypeStruct(shape, bf16) for shape in sizes),
        grid_spec=pltpu.PrefetchScalarGridSpec(
            num_scalar_prefetch=1,
            grid=(2,),
            in_specs=pick_pieces(2, 7) + [whole(size)] * 2,
            out_specs=tuple(whole(shape) for shape in sizes),
            scratch_shapes=[pltpu.VMEM(size, f32)],
        ),
        compiler_params=pltpu.CompilerParams(vmem_limit_bytes=VLIM),
        name="added",
    )(pos, *args)


def chunk_kernel(own_ref, r2a, r2b, r3a, r3b, gate_ref, up_ref, down_ref):
    for n, (r2, r3) in enumerate(((r2a, r3a), (r2b, r3b))):

        @pl.when(pl.program_id(0) == n)
        def _():
            def rows(i, _):
                some = pl.ds(pl.multiple_of(i * 64, 64), 64)
                to = pl.ds(pl.multiple_of(n * PIECE + i * 64, 64), 64)
                for k, ref in enumerate((gate_ref, up_ref)):
                    cols = slice(k * FF, (k + 1) * FF)
                    value = own_ref[some, cols].astype(f32) + r2[some, cols].astype(f32)
                    ref[0, to, :] = (value + r3[some, cols].astype(f32)).astype(bf16)
                cols = slice(2 * FF, 3 * FF)
                down_ref[to, :] = own_ref[some, cols].astype(f32) + r2[some, cols].astype(f32)
                return 0

            lax.fori_loop(0, PIECE // 64, rows, 0)


def chunk(own, *arrived):
    size = (PIECE, 3 * FF)
    per = D // NDP
    return pl.pallas_call(
        chunk_kernel,
        grid=(2,),
        out_shape=(
            jax.ShapeDtypeStruct((1, per, FF), bf16),
            jax.ShapeDtypeStruct((1, per, FF), bf16),
            jax.ShapeDtypeStruct((per, FF), f32),
        ),
        in_specs=[pl.BlockSpec(size, lambda n: (n, 0))]
        + [whole(size)] * 2 + [whole((PIECE, 2 * FF))] * 2,
        out_specs=(whole((1, per, FF)), whole((1, per, FF)), whole((per, FF))),
        compiler_params=pltpu.CompilerParams(vmem_limit_bytes=VLIM),
        name="chunk",
    )(own, *arrived)


def tail_kernel(sum_ref, ra_ref, rb_ref, out_ref):
    for n, ref in enumerate((ra_ref, rb_ref)):
        side = slice(n * PIECE, (n + 1) * PIECE)
        for q in range(NFB):
            cols = slice(q * FB, (q + 1) * FB)
            out_ref[0, cols, side] = (sum_ref[side, cols] + ref[:, cols].astype(f32)).astype(bf16)


def tail(partial, ra, rb):
    return pl.pallas_call(
        tail_kernel,
        out_shape=jax.ShapeDtypeStruct((1, FF, D // NDP), bf16),
        in_specs=[VM] * 3,
        out_specs=VM,
        compiler_params=pltpu.CompilerParams(vmem_limit_bytes=VLIM),
        cost_estimate=cost(TAIL_COST),
        name="tail",
    )(partial, ra, rb)


def slots_kernel(pos_ref, g_ref, route_ref, wg_ref, wu_ref, out_ref):
    me = pos_ref[0]
    j = pl.program_id(0)
    core = me % NC
    z = (me // NC) % NZ
    y = me // (NC * NZ)
    part = dot(g_ref[0], wg_ref[...], contract_last)
    part = part + dot(g_ref[1], wu_ref[...], contract_last)
    cols = pl.ds(pl.multiple_of(j * WIDE, WIDE), WIDE)
    for h in range(2):
        for b in range(NY):
            for s in range(NZ):
                src = ((y + DY[b] + NY) % NY) * NZ + (z + DZ[s] + NZ) % NZ
                to = src * NC + (core + h) % NC
                at = h * HALF + b * 64 + s * CAP
                out_ref[to, :, cols] = part[at : at + CAP].astype(bf16)

    @pl.when(j == 0)
    def _():
        def put(i, _):
            h, b, s = i // (NY * NZ), (i // NZ) % NY, i % NZ
            dy = jnp.where(b == 1, NY - 1, jnp.where(b == 2, 1, b - b // 3))
            dz = jnp.where(s % 2 == 1, NZ - (s + 1) // 2, s // 2)
            to = (((y + dy) % NY) * NZ + (z + dz) % NZ) * NC + (core + h) % NC
            rows = pl.ds(pl.multiple_of(i * CAP, CAP), CAP)
            out_ref[to, :, D:] = route_ref[rows, :].astype(bf16)
            return 0

        lax.fori_loop(0, 2 * NY * NZ, put, 0)


WIDE = 512
TAIL_COST = 30_000_000_000
PICK_COST = 0
FRONT_COST = 5_000_000_000


def slots(pos, g, route, wg, wu):
    size = (NY * NZ * NC, CAP, DA)
    return pl.pallas_call(
        slots_kernel,
        grid=(D // WIDE,),
        out_shape=jax.ShapeDtypeStruct(size, bf16),
        in_specs=[
            SM, whole((2, ROWS, FF)), whole((ROWS, META)),
            pl.BlockSpec((WIDE, FF), lambda j: (j, 0)),
            pl.BlockSpec((WIDE, FF), lambda j: (j, 0)),
        ],
        out_specs=whole(size),
        compiler_params=pltpu.CompilerParams(vmem_limit_bytes=VLIM),
        name="slots",
    )(pos, g, route, wg, wu)


def body(tokens, cotangent, expert_ids, route_weights, w_gate, w_up, w_down):
    pos = jnp.stack([lax.axis_index("ep"), lax.axis_index("dp")]).astype(i32)
    meta = jnp.concatenate(
        [expert_ids.astype(bf16), route_weights, jnp.zeros((TOK, META - 2 * TOPK), bf16)], axis=1
    )
    xa = jnp.concatenate([tokens, meta], axis=1)

    c1 = shift(cotangent, dy=1)
    c2 = shift(cotangent, dy=-1)
    c3 = shift(c1, dy=1)

    u = [xa]
    d = [xa]
    for _ in range(3):
        u.append(shift(u[-1], dz=1))
        d.append(shift(d[-1], dz=-1))
    u.append(shift(u[-1], dz=1))

    x0 = join([xa, u[1], d[1], u[2], d[2], u[3], d[3], u[4]], after=[c2, c3])
    p1 = shift(x0, dy=1)
    m1 = shift(x0, dy=-1)

    cot0 = join([cotangent, c1, c2, c3], after=[x0])
    cu = [cot0]
    cd = [cot0]
    for _ in range(3):
        cu.append(shift(cu[-1], dz=1))
        cd.append(shift(cd[-1], dz=-1))

    qa, qb = halves(p1, m1, after=[])
    blocks = x0, p1, m1, shift(qa, dy=1), shift(qb, dy=-1)

    qa, qb = halves(cu[-1], cd[-1], after=[])
    cq = [shift(qa, dz=1), shift(qb, dz=-1)]

    own_x, sib_x, code = pick_x(pos, blocks)
    sib_x = swap_core(sib_x)
    wg, wu, wd = w_gate[0], w_up[0], w_down[0]
    hid, hid_t, a, b, weight = front(pos, own_x, sib_x, wg, wu)

    parts = [cot0, cu[1], cd[1], cu[2], cd[2], cu[3], cd[3], *cq]
    own_c, sib_c = pick_cot(code, parts, after=code)
    sib_c = swap_core(sib_c)

    p2a, p2b, g, route = mid(
        pos, own_c, sib_c, hid, hid_t, a, b, weight, own_x, sib_x, wd
    )
    r1a, r1b = shift_dp(p2a, 1), shift_dp(p2b, -1)
    out = slots(pos, g, route, wg, wu)
    got = lax.all_to_all(out, "ep", split_axis=0, concat_axis=0, tiled=True)
    args = (own_x, sib_x, own_c, sib_c, weight, g, hid_t)
    p1b, p3a, own = plain(pos, *args)
    r2b, r2a = shift_dp(p1b, 1), shift_dp(p3a, -1)
    p1a, p1a_down, p3b, p3b_down = added(pos, *args, r1a, r1b)
    r3a, r3b = shift_dp(p1a, 1), shift_dp(p3b, -1)
    r3a_down, r3b_down = shift_dp(p1a_down, 1), shift_dp(p3b_down, -1)
    grad_gate, grad_up, partial = chunk(own, r2a, r2b, r3a, r3b)
    grad_down = tail(partial, r3a_down, r3b_down)

    experts = NY * NZ * NC
    one = (expert_ids[:, :, None] == jnp.arange(experts, dtype=i32)).astype(i32)
    named = jnp.sum(one, axis=1)
    token = jnp.arange(TOK, dtype=i32)
    lower = (token[None, :] < token[:, None]).astype(bf16)
    earlier = dot(lower, named.astype(bf16)).astype(i32)
    row = jnp.arange(experts * CAP, dtype=i32)
    code_of = jnp.repeat(jnp.where(named > 0, earlier, -1), CAP, axis=1)
    sel = code_of == (row % CAP)[None, :]
    got = got.reshape(experts * CAP, DA)
    grad_tokens = dot(sel.astype(bf16), got[:, :D]).astype(bf16)
    mine = sel[:, None, :] & (expert_ids[:, :, None] == (row // CAP)[None, None, :])
    grad_route = jnp.sum(jnp.where(mine, got[:, D].astype(f32), 0.0), axis=2).astype(bf16)

    return grad_tokens, grad_route, grad_gate, grad_up, grad_down


def solution(mesh):
    row = P(("ep", "dp"), None)
    expert = P("ep", None, None)
    return jax.shard_map(
        body,
        mesh=mesh,
        in_specs=(row, row, row, row, expert, expert, expert),
        out_specs=(row, row, P("ep", "dp", None), P("ep", "dp", None), P("ep", None, "dp")),
        check_vma=False,
    )
```

```python
import functools

import jax
import jax.numpy as jnp
from jax import lax
from jax.experimental import pallas as pl
from jax.experimental.pallas import tpu as pltpu
from jax.sharding import PartitionSpec as P

bf16 = jnp.bfloat16
f32 = jnp.float32
i32 = jnp.int32

NY, NZ, NC = 4, 8, 2
CAP = 8
TOK = 32
TOPK = 8
D = 2048
FF = 768
META = 128
DA = D + META
HALF = NY * NZ * CAP
ROWS = 2 * HALF
FB = 256
NFB = FF // FB
DY = (0, -1, 1, 2)
DZ = (0, -1, 1, -2, 2, -3, 3, 4)
NDP = 4
PIECE = D // NDP // 2
VLIM = 60 * 1024 * 1024

contract_last = (((1,), (1,)), ((), ()))
contract_first = (((0,), (0,)), ((), ()))
nothing = (((1,), (0,)), ((), ()))


def dot(a, b, dims=nothing):
    return lax.dot_general(a, b, dims, preferred_element_type=f32)


def flat(y, z, c):
    return ((y % NY) * NZ + (z % NZ)) * NC + c


def shift(arr, dy=0, dz=0):
    pairs = [
        (flat(y, z, c), flat(y + dy, z + dz, c))
        for y in range(NY)
        for z in range(NZ)
        for c in range(NC)
    ]
    return lax.ppermute(arr, "ep", pairs)


def swap_core(arr):
    return lax.ppermute(arr, "ep", [(i, i ^ 1) for i in range(NY * NZ * NC)])


def shift_dp(arr, by):
    return lax.ppermute(arr, "dp", [(i, (i + by) % NDP) for i in range(NDP)])


def join_kernel(count, *refs):
    out_ref = refs[-1]
    at = 0
    for ref in refs[:count]:
        out_ref[at : at + ref.shape[0], :] = ref[...]
        at += ref.shape[0]


def join(parts, after=()):
    rows = sum(part.shape[0] for part in parts)
    return pl.pallas_call(
        functools.partial(join_kernel, len(parts)),
        out_shape=jax.ShapeDtypeStruct((rows, parts[0].shape[1]), parts[0].dtype),
        in_specs=[VM] * len(parts) + [pl.BlockSpec(memory_space=pl.ANY)] * len(after),
        out_specs=VM,
        name="join",
    )(*parts, *after)


def cost(flops):
    return pl.CostEstimate(flops=flops, transcendentals=0, bytes_accessed=0)


VM = pl.BlockSpec(memory_space=pltpu.VMEM)
SM = pl.BlockSpec(memory_space=pltpu.SMEM)


def iota(shape, dim):
    return lax.broadcasted_iota(i32, shape, dim)


def pick_x_kernel(me_ref, *refs):
    blocks = refs[:5]
    own_ref, sib_ref, code_ref, meta_scr, sel_scr = refs[5:]
    me = me_ref[0]
    n = NZ * TOK
    at = 0
    for ref in blocks:
        meta_scr[at : at + ref.shape[0]] = ref[:, D:]
        at += ref.shape[0]
    lane = iota((n, META), 1)
    tok = iota((n, META), 0)
    low = iota((n, n), 0)
    col = iota((n, n), 1)
    before = jnp.where((col < low) & (col // TOK == low // TOK), 1.0, 0.0).astype(bf16)
    which = iota((2 * META, META), 0) // META == iota((2 * META, META), 1) // 64
    spread = jnp.where(which, 1.0, 0.0).astype(bf16)
    row_pos = (lane % CAP).astype(f32)
    here = tok // TOK == (lane % 64) // CAP
    mine = me.astype(f32)
    other = (me ^ 1).astype(f32)

    def step(b, _):
        part = pl.ds(pl.multiple_of(b * n, n), n)
        meta = meta_scr[part].astype(f32)
        ids = lane < TOPK
        hits = jnp.concatenate(
            [
                jnp.where(ids & (meta == mine), 1.0, 0.0).astype(bf16),
                jnp.where(ids & (meta == other), 1.0, 0.0).astype(bf16),
            ],
            axis=1,
        )
        named = dot(hits, spread)
        earlier = dot(before, named.astype(bf16))
        code = jnp.where(named > 0, earlier, -1.0)
        code_ref[b] = code.astype(bf16)
        sel_scr[part] = jnp.where((code == row_pos) & here, 1.0, 0.0).astype(bf16)
        return 0

    lax.fori_loop(0, NY, step, 0)
    for b in range(NY):
        mine_refs = blocks[b : b + 1] if b < 3 else blocks[3:]
        rows = 0.0
        at = b * n
        for ref in mine_refs:
            size = ref.shape[0]
            rows = rows + dot(sel_scr[at : at + size], ref[...], contract_first)
            at += size
        rows = rows.astype(bf16)
        own_ref[b * 64 : (b + 1) * 64, :] = rows[:64]
        sib_ref[b * 64 : (b + 1) * 64, :] = rows[64:]


def pick_x(me, blocks):
    return pl.pallas_call(
        pick_x_kernel,
        out_shape=(
            jax.ShapeDtypeStruct((HALF, DA), bf16),
            jax.ShapeDtypeStruct((HALF, DA), bf16),
            jax.ShapeDtypeStruct((NY, NZ * TOK, META), bf16),
        ),
        in_specs=[SM] + [VM] * 5,
        out_specs=(VM, VM, VM),
        scratch_shapes=[
            pltpu.VMEM((NY * NZ * TOK, META), bf16), pltpu.VMEM((NY * NZ * TOK, META), bf16),
        ],
        compiler_params=pltpu.CompilerParams(vmem_limit_bytes=VLIM),
        name="pick_x",
    )(me, *blocks)


def pick_cot_kernel(code_ref, *refs):
    blocks = refs[:9]
    own_ref, sib_ref, own_acc, sib_acc = refs[10:]
    n = NY * TOK
    lane = iota((n, META), 1)
    tok = iota((n, META), 0)
    row_pos = (lane % CAP).astype(f32)
    row_src = (lane % 64) // CAP
    place = 0
    for s in range(NZ):
        if DZ[s] == 4:
            blk = jnp.concatenate([blocks[place][...], blocks[place + 1][...]], axis=0)
            place += 2
        else:
            blk = blocks[place][...]
            place += 1
        code = jnp.concatenate(
            [code_ref[b, s * TOK : (s + 1) * TOK, :] for b in range(NY)], axis=0
        ).astype(f32)
        sel = jnp.where((code == row_pos) & (tok // TOK == row_src), 1.0, 0.0).astype(bf16)
        rows = dot(sel, blk, contract_first)
        for b in range(NY):
            at = b * 64 + s * CAP
            own_acc[at : at + CAP, :] = rows[b * CAP : (b + 1) * CAP]
            sib_acc[at : at + CAP, :] = rows[64 + b * CAP : 64 + (b + 1) * CAP]
    own_ref[...] = own_acc[...].astype(bf16)
    sib_ref[...] = sib_acc[...].astype(bf16)


def pick_cot(code, blocks, after):
    return pl.pallas_call(
        pick_cot_kernel,
        out_shape=(
            jax.ShapeDtypeStruct((HALF, D), bf16),
            jax.ShapeDtypeStruct((HALF, D), bf16),
        ),
        in_specs=[VM] * 10 + [pl.BlockSpec(memory_space=pl.ANY)],
        out_specs=(VM, VM),
        scratch_shapes=[pltpu.VMEM((HALF, D), f32), pltpu.VMEM((HALF, D), f32)],
        compiler_params=pltpu.CompilerParams(vmem_limit_bytes=VLIM),
        cost_estimate=cost(PICK_COST),
        name="pick_cot",
    )(code, *blocks, after)


def front_kernel(
    me_ref, own_ref, sib_ref, wg_ref, wu_ref,
    hid_ref, hid_t_ref, a_ref, b_ref, weight_ref, x_t_ref, x_scr,
):
    @pl.when(pl.program_id(0) == 0)
    def _():
        x_scr[:HALF] = own_ref[:, :D]
        x_scr[HALF:] = sib_ref[:, :D]
        x_t_ref[...] = x_scr[...].T
        meta = jnp.concatenate([own_ref[:, D:], sib_ref[:, D:]], axis=0).astype(f32)
        expert = me_ref[0].astype(f32)
        total = jnp.zeros((ROWS, 1), f32)
        for k in range(TOPK):
            total = total + jnp.where(
                meta[:, k : k + 1] == expert, meta[:, TOPK + k : TOPK + k + 1], 0.0
            )
        weight_ref[...] = jnp.broadcast_to(total, (ROWS, META))

    x = x_scr[...]
    gate = dot(x, wg_ref[...])
    up = dot(x, wu_ref[...])
    sig = jax.nn.sigmoid(gate)
    act = gate * sig
    hid = (act * up).astype(bf16)
    hid_ref[...] = hid
    hid_t_ref[...] = hid.T
    a_ref[...] = up * (sig * (1.0 + gate * (1.0 - sig)))
    b_ref[...] = act


def front(me, own, sib, wg, wu):
    whole = lambda shape: pl.BlockSpec(shape, lambda j: (0,) * len(shape))
    wide = pl.BlockSpec((ROWS, FB), lambda j: (0, j))
    return pl.pallas_call(
        front_kernel,
        grid=(NFB,),
        out_shape=(
            jax.ShapeDtypeStruct((ROWS, FF), bf16),
            jax.ShapeDtypeStruct((FF, ROWS), bf16),
            jax.ShapeDtypeStruct((ROWS, FF), f32),
            jax.ShapeDtypeStruct((ROWS, FF), f32),
            jax.ShapeDtypeStruct((ROWS, META), f32),
            jax.ShapeDtypeStruct((D, ROWS), bf16),
        ),
        in_specs=[
            SM, whole((HALF, DA)), whole((HALF, DA)),
            pl.BlockSpec((D, FB), lambda j: (0, j)),
            pl.BlockSpec((D, FB), lambda j: (0, j)),
        ],
        out_specs=(
            wide, pl.BlockSpec((FB, ROWS), lambda j: (j, 0)), wide, wide,
            whole((ROWS, META)), whole((D, ROWS)),
        ),
        scratch_shapes=[pltpu.VMEM((ROWS, D), bf16)],
        compiler_params=pltpu.CompilerParams(vmem_limit_bytes=VLIM),
        cost_estimate=cost(FRONT_COST),
        name="front",
    )(me, own, sib, wg, wu)


def whole(shape):
    return pl.BlockSpec(shape, lambda *_: (0,) * len(shape))


def place(pos_ref, piece):
    return (2 * pos_ref[1] + piece) % (2 * NDP)


def piece_into(out_ref, x_rows, g_ref, hid_t_ref, scot_cols):
    for n in range(2):
        out_ref[:, n * FF : (n + 1) * FF] = dot(x_rows, g_ref[n]).astype(bf16)
    for q in range(NFB):
        value = dot(hid_t_ref[q * FB : (q + 1) * FB], scot_cols)
        out_ref[:, 2 * FF + q * FB : 2 * FF + (q + 1) * FB] = value.astype(bf16)


def mid_kernel(
    pos_ref, own_ref, sib_ref, hid_ref, hid_t_ref, a_ref, b_ref, weight_ref, x_t_ref, wd_ref,
    pa_ref, pb_ref, g_ref, route_ref, scot_ref, cot_scr, out_scr,
):
    j = pl.program_id(0)

    @pl.when(j == 0)
    def _():
        cot_scr[:HALF] = own_ref[...]
        cot_scr[HALF:] = sib_ref[...]
        scot_ref[...] = (weight_ref[:, :1] * cot_scr[...].astype(f32)).astype(bf16)
        route_ref[...] = jnp.zeros_like(route_ref)

    back = dot(cot_scr[...], wd_ref[...], contract_last)
    part = jnp.sum(hid_ref[...].astype(f32) * back, axis=1, keepdims=True)
    route_ref[...] += jnp.broadcast_to(part, (ROWS, META))
    scaled = weight_ref[:, :1] * back
    cols = pl.ds(pl.multiple_of(j * FB, FB), FB)
    g_ref[0, :, cols] = (scaled * a_ref[...]).astype(bf16)
    g_ref[1, :, cols] = (scaled * b_ref[...]).astype(bf16)

    @pl.when(j == NFB - 1)
    def _():
        def step(n, _):
            piece = jnp.where(n == 0, 4, jnp.where(n == 1, 3, jnp.where(n == 2, 5, 6)))
            some = pl.ds(pl.multiple_of(place(pos_ref, piece) * PIECE, PIECE), PIECE)
            piece_into(
                out_scr.at[n], x_t_ref[some, :], g_ref, hid_t_ref, scot_ref[:, some]
            )
            return 0

        lax.fori_loop(0, 4, step, 0)
        for n in range(2):
            pa_ref[n * PIECE : (n + 1) * PIECE] = out_scr[n]
            pb_ref[n * PIECE : (n + 1) * PIECE] = out_scr[2 + n]


def mid(pos, own, sib, hid, hid_t, a, b, weight, x_t, wd):
    wide = pl.BlockSpec((ROWS, FB), lambda j, pos_ref: (0, j))
    size = (2 * PIECE, 3 * FF)
    return pl.pallas_call(
        mid_kernel,
        out_shape=(
            jax.ShapeDtypeStruct(size, bf16),
            jax.ShapeDtypeStruct(size, bf16),
            jax.ShapeDtypeStruct((2, ROWS, FF), bf16),
            jax.ShapeDtypeStruct((ROWS, META), f32),
            jax.ShapeDtypeStruct((ROWS, D), bf16),
        ),
        grid_spec=pltpu.PrefetchScalarGridSpec(
            num_scalar_prefetch=1,
            grid=(NFB,),
            in_specs=[
                whole((HALF, D)), whole((HALF, D)), wide, whole((FF, ROWS)), wide, wide,
                whole((ROWS, META)), whole((D, ROWS)),
                pl.BlockSpec((FB, D), lambda j, pos_ref: (j, 0)),
            ],
            out_specs=(
                whole(size), whole(size), whole((2, ROWS, FF)), whole((ROWS, META)),
                whole((ROWS, D)),
            ),
            scratch_shapes=[
                pltpu.VMEM((ROWS, D), bf16), pltpu.VMEM((4, PIECE, 3 * FF), bf16),
            ],
        ),
        compiler_params=pltpu.CompilerParams(vmem_limit_bytes=VLIM),
        name="mid",
    )(pos, own, sib, hid, hid_t, a, b, weight, x_t, wd)


def plain_kernel(pos_ref, x_ref, c_ref, g_ref, hid_t_ref, out_ref):
    piece_into(out_ref, x_ref[...], g_ref, hid_t_ref, c_ref[...])


def plain(pos, x_t, scot, g, hid_t):
    def index(n, pos_ref):
        return place(pos_ref, jnp.where(n == 0, 2, jnp.where(n == 1, 7, n - 2)))

    return pl.pallas_call(
        plain_kernel,
        out_shape=jax.ShapeDtypeStruct((4 * PIECE, 3 * FF), bf16),
        grid_spec=pltpu.PrefetchScalarGridSpec(
            num_scalar_prefetch=1,
            grid=(4,),
            in_specs=[
                pl.BlockSpec((PIECE, ROWS), lambda n, pos_ref: (index(n, pos_ref), 0)),
                pl.BlockSpec((ROWS, PIECE), lambda n, pos_ref: (0, index(n, pos_ref))),
                whole((2, ROWS, FF)), whole((FF, ROWS)),
            ],
            out_specs=pl.BlockSpec((PIECE, 3 * FF), lambda n, pos_ref: (n, 0)),
        ),
        compiler_params=pltpu.CompilerParams(vmem_limit_bytes=VLIM),
        name="plain",
    )(pos, x_t, scot, g, hid_t)


def chunk_kernel(own_ref, r2a, r2b, r3a, r3b, gate_ref, up_ref, down_ref):
    for n, (r2, r3) in enumerate(((r2a, r3a), (r2b, r3b))):

        @pl.when(pl.program_id(0) == n)
        def _():
            def rows(i, _):
                some = pl.ds(pl.multiple_of(i * 64, 64), 64)
                to = pl.ds(pl.multiple_of(n * PIECE + i * 64, 64), 64)
                for k, ref in enumerate((gate_ref, up_ref)):
                    cols = slice(k * FF, (k + 1) * FF)
                    value = own_ref[some, cols].astype(f32) + r2[some, cols].astype(f32)
                    ref[0, to, :] = (value + r3[some, cols].astype(f32)).astype(bf16)
                cols = slice(2 * FF, 3 * FF)
                down_ref[to, :] = own_ref[some, cols].astype(f32) + r2[some, cols].astype(f32)
                return 0

            lax.fori_loop(0, PIECE // 64, rows, 0)


def chunk(more, *arrived):
    size = (PIECE, 3 * FF)
    per = D // NDP
    return pl.pallas_call(
        chunk_kernel,
        grid=(2,),
        out_shape=(
            jax.ShapeDtypeStruct((1, per, FF), bf16),
            jax.ShapeDtypeStruct((1, per, FF), bf16),
            jax.ShapeDtypeStruct((per, FF), f32),
        ),
        in_specs=[pl.BlockSpec(size, lambda n: (n + 2, 0))]
        + [pl.BlockSpec(size, lambda n: (1, 0))] * 2 + [whole((PIECE, 2 * FF))] * 2,
        out_specs=(whole((1, per, FF)), whole((1, per, FF)), whole((per, FF))),
        compiler_params=pltpu.CompilerParams(vmem_limit_bytes=VLIM),
        name="chunk",
    )(more, *arrived)


def tail_kernel(sum_ref, ra_ref, rb_ref, out_ref):
    for n, ref in enumerate((ra_ref, rb_ref)):
        side = slice(n * PIECE, (n + 1) * PIECE)
        for q in range(NFB):
            cols = slice(q * FB, (q + 1) * FB)
            out_ref[0, cols, side] = (sum_ref[side, cols] + ref[:, cols].astype(f32)).astype(bf16)


def tail(partial, ra, rb):
    return pl.pallas_call(
        tail_kernel,
        out_shape=jax.ShapeDtypeStruct((1, FF, D // NDP), bf16),
        in_specs=[VM] * 3,
        out_specs=VM,
        compiler_params=pltpu.CompilerParams(vmem_limit_bytes=VLIM),
        cost_estimate=cost(TAIL_COST),
        name="tail",
    )(partial, ra, rb)


def slots_kernel(pos_ref, g_ref, route_ref, wg_ref, wu_ref, out_ref):
    me = pos_ref[0]
    j = pl.program_id(0)
    core = me % NC
    z = (me // NC) % NZ
    y = me // (NC * NZ)
    part = dot(g_ref[0], wg_ref[...], contract_last)
    part = part + dot(g_ref[1], wu_ref[...], contract_last)
    cols = pl.ds(pl.multiple_of(j * WIDE, WIDE), WIDE)
    for h in range(2):
        for b in range(NY):
            for s in range(NZ):
                src = ((y + DY[b] + NY) % NY) * NZ + (z + DZ[s] + NZ) % NZ
                to = src * NC + (core + h) % NC
                at = h * HALF + b * 64 + s * CAP
                out_ref[to, :, cols] = part[at : at + CAP].astype(bf16)

    @pl.when(j == 0)
    def _():
        def put(i, _):
            h, b, s = i // (NY * NZ), (i // NZ) % NY, i % NZ
            dy = jnp.where(b == 1, NY - 1, jnp.where(b == 2, 1, b - b // 3))
            dz = jnp.where(s % 2 == 1, NZ - (s + 1) // 2, s // 2)
            to = (((y + dy) % NY) * NZ + (z + dz) % NZ) * NC + (core + h) % NC
            rows = pl.ds(pl.multiple_of(i * CAP, CAP), CAP)
            out_ref[to, :, D:] = route_ref[rows, :].astype(bf16)
            return 0

        lax.fori_loop(0, 2 * NY * NZ, put, 0)


WIDE = 512
TAIL_COST = 30_000_000_000
PICK_COST = 0
FRONT_COST = 5_000_000_000


def slots(pos, g, route, wg, wu):
    size = (NY * NZ * NC, CAP, DA)
    return pl.pallas_call(
        slots_kernel,
        grid=(D // WIDE,),
        out_shape=jax.ShapeDtypeStruct(size, bf16),
        in_specs=[
            SM, whole((2, ROWS, FF)), whole((ROWS, META)),
            pl.BlockSpec((WIDE, FF), lambda j: (j, 0)),
            pl.BlockSpec((WIDE, FF), lambda j: (j, 0)),
        ],
        out_specs=whole(size),
        compiler_params=pltpu.CompilerParams(vmem_limit_bytes=VLIM),
        name="slots",
    )(pos, g, route, wg, wu)


def body(tokens, cotangent, expert_ids, route_weights, w_gate, w_up, w_down):
    pos = jnp.stack([lax.axis_index("ep"), lax.axis_index("dp")]).astype(i32)
    meta = jnp.concatenate(
        [expert_ids.astype(bf16), route_weights, jnp.zeros((TOK, META - 2 * TOPK), bf16)], axis=1
    )
    xa = jnp.concatenate([tokens, meta], axis=1)

    c1 = shift(cotangent, dy=1)
    c2 = shift(cotangent, dy=-1)
    c3 = shift(c1, dy=1)

    u = [xa]
    d = [xa]
    for _ in range(3):
        u.append(shift(u[-1], dz=1))
        d.append(shift(d[-1], dz=-1))
    u.append(shift(u[-1], dz=1))

    x0 = join([xa, u[1], d[1], u[2], d[2], u[3], d[3], u[4]], after=[c2, c3])
    p1 = shift(x0, dy=1)
    m1 = shift(x0, dy=-1)

    cot0 = join([cotangent, c1, c2, c3], after=[x0])
    cu = [cot0]
    cd = [cot0]
    for _ in range(3):
        cu.append(shift(cu[-1], dz=1))
        cd.append(shift(cd[-1], dz=-1))

    n = NZ * TOK // 2
    qa, qb = p1[:n], m1[n:]
    blocks = x0, p1, m1, shift(qa, dy=1), shift(qb, dy=-1)

    n = NY * TOK // 2
    qa, qb = cu[-1][:n], cd[-1][n:]
    cq = [shift(qa, dz=1), shift(qb, dz=-1)]

    own_x, sib_x, code = pick_x(pos, blocks)
    sib_x = swap_core(sib_x)
    wg, wu, wd = w_gate[0], w_up[0], w_down[0]
    hid, hid_t, a, b, weight, x_t = front(pos, own_x, sib_x, wg, wu)

    parts = [cot0, cu[1], cd[1], cu[2], cd[2], cu[3], cd[3], *cq]
    own_c, sib_c = pick_cot(code, parts, after=code)
    sib_c = swap_core(sib_c)

    pa, pb, g, route, scot = mid(pos, own_c, sib_c, hid, hid_t, a, b, weight, x_t, wd)
    ra, rb = shift_dp(pa, 1), shift_dp(pb, -1)
    out = slots(pos, g, route, wg, wu)
    got = lax.all_to_all(out, "ep", split_axis=0, concat_axis=0, tiled=True)
    more = plain(pos, x_t, scot, g, hid_t)

    def added(n, arrived, cols):
        mine = more[n * PIECE : (n + 1) * PIECE, cols].astype(f32)
        return (mine + arrived[:PIECE, cols].astype(f32)).astype(bf16)

    first, last = slice(0, 2 * FF), slice(2 * FF, 3 * FF)
    r3a, r3b = shift_dp(added(0, ra, first), 1), shift_dp(added(1, rb, first), -1)
    r3a_down, r3b_down = shift_dp(added(0, ra, last), 1), shift_dp(added(1, rb, last), -1)
    grad_gate, grad_up, partial = chunk(more, rb, ra, r3a, r3b)
    grad_down = tail(partial, r3a_down, r3b_down)

    experts = NY * NZ * NC
    one = (expert_ids[:, :, None] == jnp.arange(experts, dtype=i32)).astype(i32)
    named = jnp.sum(one, axis=1)
    token = jnp.arange(TOK, dtype=i32)
    lower = (token[None, :] < token[:, None]).astype(bf16)
    earlier = dot(lower, named.astype(bf16)).astype(i32)
    row = jnp.arange(experts * CAP, dtype=i32)
    code_of = jnp.repeat(jnp.where(named > 0, earlier, -1), CAP, axis=1)
    sel = code_of == (row % CAP)[None, :]
    got = got.reshape(experts * CAP, DA)
    grad_tokens = dot(sel.astype(bf16), got[:, :D]).astype(bf16)
    mine = sel[:, None, :] & (expert_ids[:, :, None] == (row // CAP)[None, None, :])
    grad_route = jnp.sum(jnp.where(mine, got[:, D].astype(f32), 0.0), axis=2).astype(bf16)

    return grad_tokens, grad_route, grad_gate, grad_up, grad_down


def solution(mesh):
    row = P(("ep", "dp"), None)
    expert = P("ep", None, None)
    return jax.shard_map(
        body,
        mesh=mesh,
        in_specs=(row, row, row, row, expert, expert, expert),
        out_specs=(row, row, P("ep", "dp", None), P("ep", "dp", None), P("ep", None, "dp")),
        check_vma=False,
    )
```

```python
import functools

import jax
import jax.numpy as jnp
from jax import lax
from jax.experimental import pallas as pl
from jax.experimental.pallas import tpu as pltpu
from jax.sharding import PartitionSpec as P

bf16 = jnp.bfloat16
f32 = jnp.float32
i32 = jnp.int32

NY, NZ, NC = 4, 8, 2
CAP = 8
TOK = 32
TOPK = 8
D = 2048
FF = 768
META = 128
DA = D + META
HALF = NY * NZ * CAP
ROWS = 2 * HALF
FB = 256
NFB = FF // FB
DY = (0, -1, 1, 2)
DZ = (0, -1, 1, -2, 2, -3, 3, 4)
NDP = 4
PIECE = D // NDP // 2
VLIM = 60 * 1024 * 1024

contract_last = (((1,), (1,)), ((), ()))
contract_first = (((0,), (0,)), ((), ()))
nothing = (((1,), (0,)), ((), ()))


def dot(a, b, dims=nothing):
    return lax.dot_general(a, b, dims, preferred_element_type=f32)


def flat(y, z, c):
    return ((y % NY) * NZ + (z % NZ)) * NC + c


def shift(arr, dy=0, dz=0):
    pairs = [
        (flat(y, z, c), flat(y + dy, z + dz, c))
        for y in range(NY)
        for z in range(NZ)
        for c in range(NC)
    ]
    return lax.ppermute(arr, "ep", pairs)


def swap_core(arr):
    return lax.ppermute(arr, "ep", [(i, i ^ 1) for i in range(NY * NZ * NC)])


def shift_dp(arr, by):
    return lax.ppermute(arr, "dp", [(i, (i + by) % NDP) for i in range(NDP)])


def join_kernel(count, *refs):
    out_ref = refs[-1]
    at = 0
    for ref in refs[:count]:
        out_ref[at : at + ref.shape[0], :] = ref[...]
        at += ref.shape[0]


def join(parts, after=()):
    rows = sum(part.shape[0] for part in parts)
    return pl.pallas_call(
        functools.partial(join_kernel, len(parts)),
        out_shape=jax.ShapeDtypeStruct((rows, parts[0].shape[1]), parts[0].dtype),
        in_specs=[VM] * len(parts) + [pl.BlockSpec(memory_space=pl.ANY)] * len(after),
        out_specs=VM,
        name="join",
    )(*parts, *after)


def cost(flops):
    return pl.CostEstimate(flops=flops, transcendentals=0, bytes_accessed=0)


VM = pl.BlockSpec(memory_space=pltpu.VMEM)
SM = pl.BlockSpec(memory_space=pltpu.SMEM)


def iota(shape, dim):
    return lax.broadcasted_iota(i32, shape, dim)


def pick_x_kernel(me_ref, *refs):
    blocks = refs[:5]
    own_ref, sib_ref, code_ref, meta_scr, sel_scr = refs[5:]
    me = me_ref[0]
    n = NZ * TOK
    at = 0
    for ref in blocks:
        meta_scr[at : at + ref.shape[0]] = ref[:, D:]
        at += ref.shape[0]
    lane = iota((n, META), 1)
    tok = iota((n, META), 0)
    low = iota((n, n), 0)
    col = iota((n, n), 1)
    before = jnp.where((col < low) & (col // TOK == low // TOK), 1.0, 0.0).astype(bf16)
    which = iota((2 * META, META), 0) // META == iota((2 * META, META), 1) // 64
    spread = jnp.where(which, 1.0, 0.0).astype(bf16)
    row_pos = (lane % CAP).astype(f32)
    here = tok // TOK == (lane % 64) // CAP
    mine = me.astype(f32)
    other = (me ^ 1).astype(f32)

    def step(b, _):
        part = pl.ds(pl.multiple_of(b * n, n), n)
        meta = meta_scr[part].astype(f32)
        ids = lane < TOPK
        hits = jnp.concatenate(
            [
                jnp.where(ids & (meta == mine), 1.0, 0.0).astype(bf16),
                jnp.where(ids & (meta == other), 1.0, 0.0).astype(bf16),
            ],
            axis=1,
        )
        named = dot(hits, spread)
        earlier = dot(before, named.astype(bf16))
        code = jnp.where(named > 0, earlier, -1.0)
        code_ref[b] = code.astype(bf16)
        sel_scr[part] = jnp.where((code == row_pos) & here, 1.0, 0.0).astype(bf16)
        return 0

    lax.fori_loop(0, NY, step, 0)
    for b in range(NY):
        mine_refs = blocks[b : b + 1] if b < 3 else blocks[3:]
        rows = 0.0
        at = b * n
        for ref in mine_refs:
            size = ref.shape[0]
            rows = rows + dot(sel_scr[at : at + size], ref[...], contract_first)
            at += size
        rows = rows.astype(bf16)
        own_ref[b * 64 : (b + 1) * 64, :] = rows[:64]
        sib_ref[b * 64 : (b + 1) * 64, :] = rows[64:]


def pick_x(me, blocks):
    return pl.pallas_call(
        pick_x_kernel,
        out_shape=(
            jax.ShapeDtypeStruct((HALF, DA), bf16),
            jax.ShapeDtypeStruct((HALF, DA), bf16),
            jax.ShapeDtypeStruct((NY, NZ * TOK, META), bf16),
        ),
        in_specs=[SM] + [VM] * 5,
        out_specs=(VM, VM, VM),
        scratch_shapes=[
            pltpu.VMEM((NY * NZ * TOK, META), bf16), pltpu.VMEM((NY * NZ * TOK, META), bf16),
        ],
        compiler_params=pltpu.CompilerParams(vmem_limit_bytes=VLIM),
        name="pick_x",
    )(me, *blocks)


def pick_cot_kernel(code_ref, *refs):
    blocks = refs[:9]
    own_ref, sib_ref, own_acc, sib_acc = refs[10:]
    n = NY * TOK
    lane = iota((n, META), 1)
    tok = iota((n, META), 0)
    row_pos = (lane % CAP).astype(f32)
    row_src = (lane % 64) // CAP
    place = 0
    for s in range(NZ):
        if DZ[s] == 4:
            blk = jnp.concatenate([blocks[place][...], blocks[place + 1][...]], axis=0)
            place += 2
        else:
            blk = blocks[place][...]
            place += 1
        code = jnp.concatenate(
            [code_ref[b, s * TOK : (s + 1) * TOK, :] for b in range(NY)], axis=0
        ).astype(f32)
        sel = jnp.where((code == row_pos) & (tok // TOK == row_src), 1.0, 0.0).astype(bf16)
        rows = dot(sel, blk, contract_first)
        for b in range(NY):
            at = b * 64 + s * CAP
            own_acc[at : at + CAP, :] = rows[b * CAP : (b + 1) * CAP]
            sib_acc[at : at + CAP, :] = rows[64 + b * CAP : 64 + (b + 1) * CAP]
    own_ref[...] = own_acc[...].astype(bf16)
    sib_ref[...] = sib_acc[...].astype(bf16)


def pick_cot(code, blocks, after):
    return pl.pallas_call(
        pick_cot_kernel,
        out_shape=(
            jax.ShapeDtypeStruct((HALF, D), bf16),
            jax.ShapeDtypeStruct((HALF, D), bf16),
        ),
        in_specs=[VM] * 10 + [pl.BlockSpec(memory_space=pl.ANY)],
        out_specs=(VM, VM),
        scratch_shapes=[pltpu.VMEM((HALF, D), f32), pltpu.VMEM((HALF, D), f32)],
        compiler_params=pltpu.CompilerParams(vmem_limit_bytes=VLIM),
        cost_estimate=cost(PICK_COST),
        name="pick_cot",
    )(code, *blocks, after)


def front_kernel(
    me_ref, own_ref, sib_ref, wg_ref, wu_ref,
    hid_ref, hid_t_ref, a_ref, b_ref, weight_ref, x_t_ref, x_scr,
):
    @pl.when(pl.program_id(0) == 0)
    def _():
        x_scr[:HALF] = own_ref[:, :D]
        x_scr[HALF:] = sib_ref[:, :D]
        x_t_ref[...] = x_scr[...].T
        meta = jnp.concatenate([own_ref[:, D:], sib_ref[:, D:]], axis=0).astype(f32)
        expert = me_ref[0].astype(f32)
        total = jnp.zeros((ROWS, 1), f32)
        for k in range(TOPK):
            total = total + jnp.where(
                meta[:, k : k + 1] == expert, meta[:, TOPK + k : TOPK + k + 1], 0.0
            )
        weight_ref[...] = jnp.broadcast_to(total, (ROWS, META))

    x = x_scr[...]
    gate = dot(x, wg_ref[...])
    up = dot(x, wu_ref[...])
    sig = jax.nn.sigmoid(gate)
    act = gate * sig
    hid = (act * up).astype(bf16)
    hid_ref[...] = hid
    hid_t_ref[...] = hid.T
    a_ref[...] = up * (sig * (1.0 + gate * (1.0 - sig)))
    b_ref[...] = act


def front(me, own, sib, wg, wu):
    whole = lambda shape: pl.BlockSpec(shape, lambda j: (0,) * len(shape))
    wide = pl.BlockSpec((ROWS, FB), lambda j: (0, j))
    return pl.pallas_call(
        front_kernel,
        grid=(NFB,),
        out_shape=(
            jax.ShapeDtypeStruct((ROWS, FF), bf16),
            jax.ShapeDtypeStruct((FF, ROWS), bf16),
            jax.ShapeDtypeStruct((ROWS, FF), f32),
            jax.ShapeDtypeStruct((ROWS, FF), f32),
            jax.ShapeDtypeStruct((ROWS, META), f32),
            jax.ShapeDtypeStruct((D, ROWS), bf16),
        ),
        in_specs=[
            SM, whole((HALF, DA)), whole((HALF, DA)),
            pl.BlockSpec((D, FB), lambda j: (0, j)),
            pl.BlockSpec((D, FB), lambda j: (0, j)),
        ],
        out_specs=(
            wide, pl.BlockSpec((FB, ROWS), lambda j: (j, 0)), wide, wide,
            whole((ROWS, META)), whole((D, ROWS)),
        ),
        scratch_shapes=[pltpu.VMEM((ROWS, D), bf16)],
        compiler_params=pltpu.CompilerParams(vmem_limit_bytes=VLIM),
        cost_estimate=cost(FRONT_COST),
        name="front",
    )(me, own, sib, wg, wu)


def whole(shape):
    return pl.BlockSpec(shape, lambda *_: (0,) * len(shape))


def place(pos_ref, piece):
    return (2 * pos_ref[1] + piece) % (2 * NDP)


def piece_into(out_ref, x_rows, g_ref, hid_t_ref, scot_cols):
    for n in range(2):
        out_ref[:, n * FF : (n + 1) * FF] = dot(x_rows, g_ref[n]).astype(bf16)
    for q in range(NFB):
        value = dot(hid_t_ref[q * FB : (q + 1) * FB], scot_cols)
        out_ref[:, 2 * FF + q * FB : 2 * FF + (q + 1) * FB] = value.astype(bf16)


def mid_kernel(
    pos_ref, own_ref, sib_ref, hid_ref, hid_t_ref, a_ref, b_ref, weight_ref, x_t_ref, wd_ref,
    pa_ref, pb_ref, pc_ref, pd_ref, g_ref, route_ref, scot_ref, cot_scr, out_scr,
):
    j = pl.program_id(0)

    @pl.when(j == 0)
    def _():
        cot_scr[:HALF] = own_ref[...]
        cot_scr[HALF:] = sib_ref[...]
        scot_ref[...] = (weight_ref[:, :1] * cot_scr[...].astype(f32)).astype(bf16)
        route_ref[...] = jnp.zeros_like(route_ref)

    back = dot(cot_scr[...], wd_ref[...], contract_last)
    part = jnp.sum(hid_ref[...].astype(f32) * back, axis=1, keepdims=True)
    route_ref[...] += jnp.broadcast_to(part, (ROWS, META))
    scaled = weight_ref[:, :1] * back
    cols = pl.ds(pl.multiple_of(j * FB, FB), FB)
    g_ref[0, :, cols] = (scaled * a_ref[...]).astype(bf16)
    g_ref[1, :, cols] = (scaled * b_ref[...]).astype(bf16)

    @pl.when(j == NFB - 1)
    def _():
        def step(n, _):
            piece = jnp.where(n == 0, 4, jnp.where(n == 1, 5, jnp.where(n == 2, 3, 6)))
            some = pl.ds(pl.multiple_of(place(pos_ref, piece) * PIECE, PIECE), PIECE)
            piece_into(
                out_scr.at[n], x_t_ref[some, :], g_ref, hid_t_ref, scot_ref[:, some]
            )
            return 0

        lax.fori_loop(0, 4, step, 0)
        for n, ref in enumerate((pa_ref, pb_ref, pc_ref, pd_ref)):
            ref[...] = out_scr[n]


def mid(pos, own, sib, hid, hid_t, a, b, weight, x_t, wd):
    wide = pl.BlockSpec((ROWS, FB), lambda j, pos_ref: (0, j))
    size = (PIECE, 3 * FF)
    return pl.pallas_call(
        mid_kernel,
        out_shape=(
            *[jax.ShapeDtypeStruct(size, bf16)] * 4,
            jax.ShapeDtypeStruct((2, ROWS, FF), bf16),
            jax.ShapeDtypeStruct((ROWS, META), f32),
            jax.ShapeDtypeStruct((ROWS, D), bf16),
        ),
        grid_spec=pltpu.PrefetchScalarGridSpec(
            num_scalar_prefetch=1,
            grid=(NFB,),
            in_specs=[
                whole((HALF, D)), whole((HALF, D)), wide, whole((FF, ROWS)), wide, wide,
                whole((ROWS, META)), whole((D, ROWS)),
                pl.BlockSpec((FB, D), lambda j, pos_ref: (j, 0)),
            ],
            out_specs=(
                *[whole(size)] * 4, whole((2, ROWS, FF)), whole((ROWS, META)), whole((ROWS, D)),
            ),
            scratch_shapes=[
                pltpu.VMEM((ROWS, D), bf16), pltpu.VMEM((4, PIECE, 3 * FF), bf16),
            ],
        ),
        compiler_params=pltpu.CompilerParams(vmem_limit_bytes=VLIM),
        name="mid",
    )(pos, own, sib, hid, hid_t, a, b, weight, x_t, wd)


def plain_kernel(pos_ref, x_ref, c_ref, g_ref, hid_t_ref, _, out_ref):
    piece_into(out_ref, x_ref[...], g_ref, hid_t_ref, c_ref[...])


def plain(pos, x_t, scot, g, hid_t, after):
    def index(n, pos_ref):
        return place(pos_ref, jnp.where(n == 0, 2, jnp.where(n == 1, 7, n - 2)))

    return pl.pallas_call(
        plain_kernel,
        out_shape=jax.ShapeDtypeStruct((4 * PIECE, 3 * FF), bf16),
        grid_spec=pltpu.PrefetchScalarGridSpec(
            num_scalar_prefetch=1,
            grid=(4,),
            in_specs=[
                pl.BlockSpec((PIECE, ROWS), lambda n, pos_ref: (index(n, pos_ref), 0)),
                pl.BlockSpec((ROWS, PIECE), lambda n, pos_ref: (0, index(n, pos_ref))),
                whole((2, ROWS, FF)), whole((FF, ROWS)),
                pl.BlockSpec(memory_space=pl.ANY),
            ],
            out_specs=pl.BlockSpec((PIECE, 3 * FF), lambda n, pos_ref: (n, 0)),
        ),
        compiler_params=pltpu.CompilerParams(vmem_limit_bytes=VLIM),
        name="plain",
    )(pos, x_t, scot, g, hid_t, after)


def chunk_kernel(own_ref, r2a, r2b, r3a, r3b, gate_ref, up_ref, down_ref):
    for n, (r2, r3) in enumerate(((r2a, r3a), (r2b, r3b))):

        @pl.when(pl.program_id(0) == n)
        def _():
            def rows(i, _):
                some = pl.ds(pl.multiple_of(i * 64, 64), 64)
                to = pl.ds(pl.multiple_of(n * PIECE + i * 64, 64), 64)
                for k, ref in enumerate((gate_ref, up_ref)):
                    cols = slice(k * FF, (k + 1) * FF)
                    value = own_ref[some, cols].astype(f32) + r2[some, cols].astype(f32)
                    ref[0, to, :] = (value + r3[some, cols].astype(f32)).astype(bf16)
                cols = slice(2 * FF, 3 * FF)
                down_ref[to, :] = own_ref[some, cols].astype(f32) + r2[some, cols].astype(f32)
                return 0

            lax.fori_loop(0, PIECE // 64, rows, 0)


def chunk(more, *arrived):
    size = (PIECE, 3 * FF)
    per = D // NDP
    return pl.pallas_call(
        chunk_kernel,
        grid=(2,),
        out_shape=(
            jax.ShapeDtypeStruct((1, per, FF), bf16),
            jax.ShapeDtypeStruct((1, per, FF), bf16),
            jax.ShapeDtypeStruct((per, FF), f32),
        ),
        in_specs=[pl.BlockSpec(size, lambda n: (n + 2, 0))]
        + [whole(size)] * 2 + [whole((PIECE, 2 * FF))] * 2,
        out_specs=(whole((1, per, FF)), whole((1, per, FF)), whole((per, FF))),
        compiler_params=pltpu.CompilerParams(vmem_limit_bytes=VLIM),
        cost_estimate=cost(CHUNK_COST),
        name="chunk",
    )(more, *arrived)


def tail_kernel(sum_ref, ra_ref, rb_ref, _, out_ref):
    for n, ref in enumerate((ra_ref, rb_ref)):
        side = slice(n * PIECE, (n + 1) * PIECE)
        for q in range(NFB):
            cols = slice(q * FB, (q + 1) * FB)
            out_ref[0, cols, side] = (sum_ref[side, cols] + ref[:, cols].astype(f32)).astype(bf16)


def tail(partial, ra, rb, after):
    return pl.pallas_call(
        tail_kernel,
        out_shape=jax.ShapeDtypeStruct((1, FF, D // NDP), bf16),
        in_specs=[VM] * 3 + [pl.BlockSpec(memory_space=pl.ANY)],
        out_specs=VM,
        compiler_params=pltpu.CompilerParams(vmem_limit_bytes=VLIM),
        name="tail",
    )(partial, ra, rb, after)


def slots_kernel(pos_ref, g_ref, route_ref, wg_ref, wu_ref, out_ref):
    me = pos_ref[0]
    j = pl.program_id(0)
    core = me % NC
    z = (me // NC) % NZ
    y = me // (NC * NZ)
    part = dot(g_ref[0], wg_ref[...], contract_last)
    part = part + dot(g_ref[1], wu_ref[...], contract_last)
    cols = pl.ds(pl.multiple_of(j * WIDE, WIDE), WIDE)
    for h in range(2):
        for b in range(NY):
            for s in range(NZ):
                src = ((y + DY[b] + NY) % NY) * NZ + (z + DZ[s] + NZ) % NZ
                to = src * NC + (core + h) % NC
                at = h * HALF + b * 64 + s * CAP
                out_ref[to, :, cols] = part[at : at + CAP].astype(bf16)

    @pl.when(j == 0)
    def _():
        def put(i, _):
            h, b, s = i // (NY * NZ), (i // NZ) % NY, i % NZ
            dy = jnp.where(b == 1, NY - 1, jnp.where(b == 2, 1, b - b // 3))
            dz = jnp.where(s % 2 == 1, NZ - (s + 1) // 2, s // 2)
            to = (((y + dy) % NY) * NZ + (z + dz) % NZ) * NC + (core + h) % NC
            rows = pl.ds(pl.multiple_of(i * CAP, CAP), CAP)
            out_ref[to, :, D:] = route_ref[rows, :].astype(bf16)
            return 0

        lax.fori_loop(0, 2 * NY * NZ, put, 0)


WIDE = 512
CHUNK_COST = 30_000_000_000
PICK_COST = 0
FRONT_COST = 5_000_000_000


def slots(pos, g, route, wg, wu):
    size = (NY * NZ * NC, CAP, DA)
    return pl.pallas_call(
        slots_kernel,
        grid=(D // WIDE,),
        out_shape=jax.ShapeDtypeStruct(size, bf16),
        in_specs=[
            SM, whole((2, ROWS, FF)), whole((ROWS, META)),
            pl.BlockSpec((WIDE, FF), lambda j: (j, 0)),
            pl.BlockSpec((WIDE, FF), lambda j: (j, 0)),
        ],
        out_specs=whole(size),
        compiler_params=pltpu.CompilerParams(vmem_limit_bytes=VLIM),
        name="slots",
    )(pos, g, route, wg, wu)


def body(tokens, cotangent, expert_ids, route_weights, w_gate, w_up, w_down):
    pos = jnp.stack([lax.axis_index("ep"), lax.axis_index("dp")]).astype(i32)
    meta = jnp.concatenate(
        [expert_ids.astype(bf16), route_weights, jnp.zeros((TOK, META - 2 * TOPK), bf16)], axis=1
    )
    xa = jnp.concatenate([tokens, meta], axis=1)

    c1 = shift(cotangent, dy=1)
    c2 = shift(cotangent, dy=-1)
    c3 = shift(c1, dy=1)

    u = [xa]
    d = [xa]
    for _ in range(3):
        u.append(shift(u[-1], dz=1))
        d.append(shift(d[-1], dz=-1))
    u.append(shift(u[-1], dz=1))

    x0 = join([xa, u[1], d[1], u[2], d[2], u[3], d[3], u[4]], after=[c2, c3])
    p1 = shift(x0, dy=1)
    m1 = shift(x0, dy=-1)

    cot0 = join([cotangent, c1, c2, c3], after=[x0])
    cu = [cot0]
    cd = [cot0]
    for _ in range(3):
        cu.append(shift(cu[-1], dz=1))
        cd.append(shift(cd[-1], dz=-1))

    n = NZ * TOK // 2
    qa, qb = p1[:n], m1[n:]
    blocks = x0, p1, m1, shift(qa, dy=1), shift(qb, dy=-1)

    n = NY * TOK // 2
    qa, qb = cu[-1][:n], cd[-1][n:]
    cq = [shift(qa, dz=1), shift(qb, dz=-1)]

    own_x, sib_x, code = pick_x(pos, blocks)
    sib_x = swap_core(sib_x)
    wg, wu, wd = w_gate[0], w_up[0], w_down[0]
    hid, hid_t, a, b, weight, x_t = front(pos, own_x, sib_x, wg, wu)

    parts = [cot0, cu[1], cd[1], cu[2], cd[2], cu[3], cd[3], *cq]
    own_c, sib_c = pick_cot(code, parts, after=code)
    sib_c = swap_core(sib_c)

    p2a, p2b, p1b, p3a, g, route, scot = mid(
        pos, own_c, sib_c, hid, hid_t, a, b, weight, x_t, wd
    )
    r1a, r1b = shift_dp(p2a, 1), shift_dp(p2b, -1)
    r2b, r2a = shift_dp(p1b, 1), shift_dp(p3a, -1)
    out = slots(pos, g, route, wg, wu)
    got = lax.all_to_all(out, "ep", split_axis=0, concat_axis=0, tiled=True)
    more = plain(pos, x_t, scot, g, hid_t, after=r1a)

    def added(n, arrived, cols):
        mine = more[n * PIECE : (n + 1) * PIECE, cols].astype(f32)
        return (mine + arrived[:, cols].astype(f32)).astype(bf16)

    first, last = slice(0, 2 * FF), slice(2 * FF, 3 * FF)
    r3a, r3b = shift_dp(added(0, r1a, first), 1), shift_dp(added(1, r1b, first), -1)
    r3a_down, r3b_down = shift_dp(added(0, r1a, last), 1), shift_dp(added(1, r1b, last), -1)
    grad_gate, grad_up, partial = chunk(more, r2a, r2b, r3a, r3b)

    experts = NY * NZ * NC
    one = (expert_ids[:, :, None] == jnp.arange(experts, dtype=i32)).astype(i32)
    named = jnp.sum(one, axis=1)
    token = jnp.arange(TOK, dtype=i32)
    lower = (token[None, :] < token[:, None]).astype(bf16)
    earlier = dot(lower, named.astype(bf16)).astype(i32)
    row = jnp.arange(experts * CAP, dtype=i32)
    code_of = jnp.repeat(jnp.where(named > 0, earlier, -1), CAP, axis=1)
    sel = code_of == (row % CAP)[None, :]
    got = got.reshape(experts * CAP, DA)
    grad_tokens = dot(sel.astype(bf16), got[:, :D]).astype(bf16)
    mine = sel[:, None, :] & (expert_ids[:, :, None] == (row // CAP)[None, None, :])
    grad_route = jnp.sum(jnp.where(mine, got[:, D].astype(f32), 0.0), axis=2).astype(bf16)

    grad_down = tail(partial, r3a_down, r3b_down, after=grad_tokens)
    return grad_tokens, grad_route, grad_gate, grad_up, grad_down


def solution(mesh):
    row = P(("ep", "dp"), None)
    expert = P("ep", None, None)
    return jax.shard_map(
        body,
        mesh=mesh,
        in_specs=(row, row, row, row, expert, expert, expert),
        out_specs=(row, row, P("ep", "dp", None), P("ep", "dp", None), P("ep", None, "dp")),
        check_vma=False,
    )
```

```python
import functools

import jax
import jax.numpy as jnp
from jax import lax
from jax.experimental import pallas as pl
from jax.experimental.pallas import tpu as pltpu
from jax.sharding import PartitionSpec as P

bf16 = jnp.bfloat16
f32 = jnp.float32
i32 = jnp.int32

NY, NZ, NC = 4, 8, 2
CAP = 8
TOK = 32
TOPK = 8
D = 2048
FF = 768
META = 128
DA = D + META
HALF = NY * NZ * CAP
ROWS = 2 * HALF
FB = 256
NFB = FF // FB
DY = (0, -1, 1, 2)
DZ = (0, -1, 1, -2, 2, -3, 3, 4)
NDP = 4
PIECE = D // NDP // 2
VLIM = 60 * 1024 * 1024

contract_last = (((1,), (1,)), ((), ()))
contract_first = (((0,), (0,)), ((), ()))
nothing = (((1,), (0,)), ((), ()))


def dot(a, b, dims=nothing):
    return lax.dot_general(a, b, dims, preferred_element_type=f32)


def flat(y, z, c):
    return ((y % NY) * NZ + (z % NZ)) * NC + c


def shift(arr, dy=0, dz=0):
    pairs = [
        (flat(y, z, c), flat(y + dy, z + dz, c))
        for y in range(NY)
        for z in range(NZ)
        for c in range(NC)
    ]
    return lax.ppermute(arr, "ep", pairs)


def swap_core(arr):
    return lax.ppermute(arr, "ep", [(i, i ^ 1) for i in range(NY * NZ * NC)])


def shift_dp(arr, by):
    return lax.ppermute(arr, "dp", [(i, (i + by) % NDP) for i in range(NDP)])


def join_kernel(count, *refs):
    out_ref = refs[-1]
    at = 0
    for ref in refs[:count]:
        out_ref[at : at + ref.shape[0], :] = ref[...]
        at += ref.shape[0]


def join(parts, after=()):
    rows = sum(part.shape[0] for part in parts)
    return pl.pallas_call(
        functools.partial(join_kernel, len(parts)),
        out_shape=jax.ShapeDtypeStruct((rows, parts[0].shape[1]), parts[0].dtype),
        in_specs=[VM] * len(parts) + [pl.BlockSpec(memory_space=pl.ANY)] * len(after),
        out_specs=VM,
        name="join",
    )(*parts, *after)


def cost(flops):
    return pl.CostEstimate(flops=flops, transcendentals=0, bytes_accessed=0)


VM = pl.BlockSpec(memory_space=pltpu.VMEM)
SM = pl.BlockSpec(memory_space=pltpu.SMEM)


def iota(shape, dim):
    return lax.broadcasted_iota(i32, shape, dim)


def pick_x_kernel(me_ref, *refs):
    blocks = refs[:5]
    own_ref, sib_ref, code_ref, meta_scr, sel_scr = refs[5:]
    me = me_ref[0]
    n = NZ * TOK
    at = 0
    for ref in blocks:
        meta_scr[at : at + ref.shape[0]] = ref[:, D:]
        at += ref.shape[0]
    lane = iota((n, META), 1)
    tok = iota((n, META), 0)
    low = iota((n, n), 0)
    col = iota((n, n), 1)
    before = jnp.where((col < low) & (col // TOK == low // TOK), 1.0, 0.0).astype(bf16)
    which = iota((2 * META, META), 0) // META == iota((2 * META, META), 1) // 64
    spread = jnp.where(which, 1.0, 0.0).astype(bf16)
    row_pos = (lane % CAP).astype(f32)
    here = tok // TOK == (lane % 64) // CAP
    mine = me.astype(f32)
    other = (me ^ 1).astype(f32)

    def step(b, _):
        part = pl.ds(pl.multiple_of(b * n, n), n)
        meta = meta_scr[part].astype(f32)
        ids = lane < TOPK
        hits = jnp.concatenate(
            [
                jnp.where(ids & (meta == mine), 1.0, 0.0).astype(bf16),
                jnp.where(ids & (meta == other), 1.0, 0.0).astype(bf16),
            ],
            axis=1,
        )
        named = dot(hits, spread)
        earlier = dot(before, named.astype(bf16))
        code = jnp.where(named > 0, earlier, -1.0)
        code_ref[b] = code.astype(bf16)
        sel_scr[part] = jnp.where((code == row_pos) & here, 1.0, 0.0).astype(bf16)
        return 0

    lax.fori_loop(0, NY, step, 0)
    for b in range(NY):
        mine_refs = blocks[b : b + 1] if b < 3 else blocks[3:]
        rows = 0.0
        at = b * n
        for ref in mine_refs:
            size = ref.shape[0]
            rows = rows + dot(sel_scr[at : at + size], ref[...], contract_first)
            at += size
        rows = rows.astype(bf16)
        own_ref[b * 64 : (b + 1) * 64, :] = rows[:64]
        sib_ref[b * 64 : (b + 1) * 64, :] = rows[64:]


def pick_x(me, blocks):
    return pl.pallas_call(
        pick_x_kernel,
        out_shape=(
            jax.ShapeDtypeStruct((HALF, DA), bf16),
            jax.ShapeDtypeStruct((HALF, DA), bf16),
            jax.ShapeDtypeStruct((NY, NZ * TOK, META), bf16),
        ),
        in_specs=[SM] + [VM] * 5,
        out_specs=(VM, VM, VM),
        scratch_shapes=[
            pltpu.VMEM((NY * NZ * TOK, META), bf16), pltpu.VMEM((NY * NZ * TOK, META), bf16),
        ],
        compiler_params=pltpu.CompilerParams(vmem_limit_bytes=VLIM),
        cost_estimate=cost(0),
        name="pick_x",
    )(me, *blocks)


def pick_cot_kernel(code_ref, *refs):
    blocks = refs[:9]
    own_ref, sib_ref, own_acc, sib_acc = refs[10:]
    n = NY * TOK
    lane = iota((n, META), 1)
    tok = iota((n, META), 0)
    row_pos = (lane % CAP).astype(f32)
    row_src = (lane % 64) // CAP
    place = 0
    for s in range(NZ):
        if DZ[s] == 4:
            blk = jnp.concatenate([blocks[place][...], blocks[place + 1][...]], axis=0)
            place += 2
        else:
            blk = blocks[place][...]
            place += 1
        code = jnp.concatenate(
            [code_ref[b, s * TOK : (s + 1) * TOK, :] for b in range(NY)], axis=0
        ).astype(f32)
        sel = jnp.where((code == row_pos) & (tok // TOK == row_src), 1.0, 0.0).astype(bf16)
        rows = dot(sel, blk, contract_first)
        for b in range(NY):
            at = b * 64 + s * CAP
            own_acc[at : at + CAP, :] = rows[b * CAP : (b + 1) * CAP]
            sib_acc[at : at + CAP, :] = rows[64 + b * CAP : 64 + (b + 1) * CAP]
    own_ref[...] = own_acc[...].astype(bf16)
    sib_ref[...] = sib_acc[...].astype(bf16)


def pick_cot(code, blocks, after):
    return pl.pallas_call(
        pick_cot_kernel,
        out_shape=(
            jax.ShapeDtypeStruct((HALF, D), bf16),
            jax.ShapeDtypeStruct((HALF, D), bf16),
        ),
        in_specs=[VM] * 10 + [pl.BlockSpec(memory_space=pl.ANY)],
        out_specs=(VM, VM),
        scratch_shapes=[pltpu.VMEM((HALF, D), f32), pltpu.VMEM((HALF, D), f32)],
        compiler_params=pltpu.CompilerParams(vmem_limit_bytes=VLIM),
        cost_estimate=cost(PICK_COST),
        name="pick_cot",
    )(code, *blocks, after)


def front_kernel(
    me_ref, own_ref, sib_ref, wg_ref, wu_ref,
    hid_ref, hid_t_ref, a_ref, b_ref, weight_ref, x_t_ref, x_scr,
):
    @pl.when(pl.program_id(0) == 0)
    def _():
        x_scr[:HALF] = own_ref[:, :D]
        x_scr[HALF:] = sib_ref[:, :D]
        x_t_ref[...] = x_scr[...].T
        meta = jnp.concatenate([own_ref[:, D:], sib_ref[:, D:]], axis=0).astype(f32)
        expert = me_ref[0].astype(f32)
        total = jnp.zeros((ROWS, 1), f32)
        for k in range(TOPK):
            total = total + jnp.where(
                meta[:, k : k + 1] == expert, meta[:, TOPK + k : TOPK + k + 1], 0.0
            )
        weight_ref[...] = jnp.broadcast_to(total, (ROWS, META))

    x = x_scr[...]
    gate = dot(x, wg_ref[...])
    up = dot(x, wu_ref[...])
    sig = jax.nn.sigmoid(gate)
    act = gate * sig
    hid = (act * up).astype(bf16)
    hid_ref[...] = hid
    hid_t_ref[...] = hid.T
    a_ref[...] = up * (sig * (1.0 + gate * (1.0 - sig)))
    b_ref[...] = act


def front(me, own, sib, wg, wu):
    whole = lambda shape: pl.BlockSpec(shape, lambda j: (0,) * len(shape))
    wide = pl.BlockSpec((ROWS, FB), lambda j: (0, j))
    return pl.pallas_call(
        front_kernel,
        grid=(NFB,),
        out_shape=(
            jax.ShapeDtypeStruct((ROWS, FF), bf16),
            jax.ShapeDtypeStruct((FF, ROWS), bf16),
            jax.ShapeDtypeStruct((ROWS, FF), f32),
            jax.ShapeDtypeStruct((ROWS, FF), f32),
            jax.ShapeDtypeStruct((ROWS, META), f32),
            jax.ShapeDtypeStruct((D, ROWS), bf16),
        ),
        in_specs=[
            SM, whole((HALF, DA)), whole((HALF, DA)),
            pl.BlockSpec((D, FB), lambda j: (0, j)),
            pl.BlockSpec((D, FB), lambda j: (0, j)),
        ],
        out_specs=(
            wide, pl.BlockSpec((FB, ROWS), lambda j: (j, 0)), wide, wide,
            whole((ROWS, META)), whole((D, ROWS)),
        ),
        scratch_shapes=[pltpu.VMEM((ROWS, D), bf16)],
        compiler_params=pltpu.CompilerParams(vmem_limit_bytes=VLIM),
        cost_estimate=cost(FRONT_COST),
        name="front",
    )(me, own, sib, wg, wu)


def whole(shape):
    return pl.BlockSpec(shape, lambda *_: (0,) * len(shape))


def place(pos_ref, piece):
    return (2 * pos_ref[1] + piece) % (2 * NDP)


def piece_into(out_ref, x_rows, g_ref, hid_t_ref, scot_cols):
    for n in range(2):
        out_ref[:, n * FF : (n + 1) * FF] = dot(x_rows, g_ref[n]).astype(bf16)
    for q in range(NFB):
        value = dot(hid_t_ref[q * FB : (q + 1) * FB], scot_cols)
        out_ref[:, 2 * FF + q * FB : 2 * FF + (q + 1) * FB] = value.astype(bf16)


def mid_kernel(
    pos_ref, own_ref, sib_ref, hid_ref, hid_t_ref, a_ref, b_ref, weight_ref, x_t_ref, wd_ref,
    pa_ref, pb_ref, pc_ref, pd_ref, g_ref, route_ref, scot_ref, cot_scr, out_scr,
):
    j = pl.program_id(0)

    @pl.when(j == 0)
    def _():
        cot_scr[:HALF] = own_ref[...]
        cot_scr[HALF:] = sib_ref[...]
        scot_ref[...] = (weight_ref[:, :1] * cot_scr[...].astype(f32)).astype(bf16)
        route_ref[...] = jnp.zeros_like(route_ref)

    back = dot(cot_scr[...], wd_ref[...], contract_last)
    part = jnp.sum(hid_ref[...].astype(f32) * back, axis=1, keepdims=True)
    route_ref[...] += jnp.broadcast_to(part, (ROWS, META))
    scaled = weight_ref[:, :1] * back
    cols = pl.ds(pl.multiple_of(j * FB, FB), FB)
    g_ref[0, :, cols] = (scaled * a_ref[...]).astype(bf16)
    g_ref[1, :, cols] = (scaled * b_ref[...]).astype(bf16)

    @pl.when(j == NFB - 1)
    def _():
        def step(n, _):
            piece = jnp.where(n == 0, 4, jnp.where(n == 1, 5, jnp.where(n == 2, 3, 6)))
            some = pl.ds(pl.multiple_of(place(pos_ref, piece) * PIECE, PIECE), PIECE)
            piece_into(
                out_scr.at[n], x_t_ref[some, :], g_ref, hid_t_ref, scot_ref[:, some]
            )
            return 0

        lax.fori_loop(0, 4, step, 0)
        for n, ref in enumerate((pa_ref, pb_ref, pc_ref, pd_ref)):
            ref[...] = out_scr[n]


def mid(pos, own, sib, hid, hid_t, a, b, weight, x_t, wd):
    wide = pl.BlockSpec((ROWS, FB), lambda j, pos_ref: (0, j))
    size = (PIECE, 3 * FF)
    return pl.pallas_call(
        mid_kernel,
        out_shape=(
            *[jax.ShapeDtypeStruct(size, bf16)] * 4,
            jax.ShapeDtypeStruct((2, ROWS, FF), bf16),
            jax.ShapeDtypeStruct((ROWS, META), f32),
            jax.ShapeDtypeStruct((ROWS, D), bf16),
        ),
        grid_spec=pltpu.PrefetchScalarGridSpec(
            num_scalar_prefetch=1,
            grid=(NFB,),
            in_specs=[
                whole((HALF, D)), whole((HALF, D)), wide, whole((FF, ROWS)), wide, wide,
                whole((ROWS, META)), whole((D, ROWS)),
                pl.BlockSpec((FB, D), lambda j, pos_ref: (j, 0)),
            ],
            out_specs=(
                *[whole(size)] * 4, whole((2, ROWS, FF)), whole((ROWS, META)), whole((ROWS, D)),
            ),
            scratch_shapes=[
                pltpu.VMEM((ROWS, D), bf16), pltpu.VMEM((4, PIECE, 3 * FF), bf16),
            ],
        ),
        compiler_params=pltpu.CompilerParams(vmem_limit_bytes=VLIM),
        name="mid",
    )(pos, own, sib, hid, hid_t, a, b, weight, x_t, wd)


def plain_kernel(pos_ref, x_ref, c_ref, g_ref, hid_t_ref, _, out_ref):
    piece_into(out_ref, x_ref[...], g_ref, hid_t_ref, c_ref[...])


def plain(pos, x_t, scot, g, hid_t, after):
    def index(n, pos_ref):
        return place(pos_ref, jnp.where(n == 0, 2, jnp.where(n == 1, 7, n - 2)))

    return pl.pallas_call(
        plain_kernel,
        out_shape=jax.ShapeDtypeStruct((4 * PIECE, 3 * FF), bf16),
        grid_spec=pltpu.PrefetchScalarGridSpec(
            num_scalar_prefetch=1,
            grid=(4,),
            in_specs=[
                pl.BlockSpec((PIECE, ROWS), lambda n, pos_ref: (index(n, pos_ref), 0)),
                pl.BlockSpec((ROWS, PIECE), lambda n, pos_ref: (0, index(n, pos_ref))),
                whole((2, ROWS, FF)), whole((FF, ROWS)),
                pl.BlockSpec(memory_space=pl.ANY),
            ],
            out_specs=pl.BlockSpec((PIECE, 3 * FF), lambda n, pos_ref: (n, 0)),
        ),
        compiler_params=pltpu.CompilerParams(vmem_limit_bytes=VLIM),
        name="plain",
    )(pos, x_t, scot, g, hid_t, after)


def chunk_kernel(own_ref, r2a, r2b, r3a, r3b, gate_ref, up_ref, down_ref):
    for n, (r2, r3) in enumerate(((r2a, r3a), (r2b, r3b))):

        @pl.when(pl.program_id(0) == n)
        def _():
            def rows(i, _):
                some = pl.ds(pl.multiple_of(i * 64, 64), 64)
                to = pl.ds(pl.multiple_of(n * PIECE + i * 64, 64), 64)
                for k, ref in enumerate((gate_ref, up_ref)):
                    cols = slice(k * FF, (k + 1) * FF)
                    value = own_ref[some, cols].astype(f32) + r2[some, cols].astype(f32)
                    ref[0, to, :] = (value + r3[some, cols].astype(f32)).astype(bf16)
                cols = slice(2 * FF, 3 * FF)
                down_ref[to, :] = own_ref[some, cols].astype(f32) + r2[some, cols].astype(f32)
                return 0

            lax.fori_loop(0, PIECE // 64, rows, 0)


def chunk(more, *arrived):
    size = (PIECE, 3 * FF)
    per = D // NDP
    return pl.pallas_call(
        chunk_kernel,
        grid=(2,),
        out_shape=(
            jax.ShapeDtypeStruct((1, per, FF), bf16),
            jax.ShapeDtypeStruct((1, per, FF), bf16),
            jax.ShapeDtypeStruct((per, FF), f32),
        ),
        in_specs=[pl.BlockSpec(size, lambda n: (n + 2, 0))]
        + [whole(size)] * 2 + [whole((PIECE, 2 * FF))] * 2,
        out_specs=(whole((1, per, FF)), whole((1, per, FF)), whole((per, FF))),
        compiler_params=pltpu.CompilerParams(vmem_limit_bytes=VLIM),
        cost_estimate=cost(CHUNK_COST),
        name="chunk",
    )(more, *arrived)


def tail_kernel(sum_ref, ra_ref, rb_ref, _, out_ref):
    for n, ref in enumerate((ra_ref, rb_ref)):
        side = slice(n * PIECE, (n + 1) * PIECE)
        for q in range(NFB):
            cols = slice(q * FB, (q + 1) * FB)
            out_ref[0, cols, side] = (sum_ref[side, cols] + ref[:, cols].astype(f32)).astype(bf16)


def tail(partial, ra, rb, after):
    return pl.pallas_call(
        tail_kernel,
        out_shape=jax.ShapeDtypeStruct((1, FF, D // NDP), bf16),
        in_specs=[VM] * 3 + [pl.BlockSpec(memory_space=pl.ANY)],
        out_specs=VM,
        compiler_params=pltpu.CompilerParams(vmem_limit_bytes=VLIM),
        name="tail",
    )(partial, ra, rb, after)


def slots_kernel(pos_ref, g_ref, route_ref, wg_ref, wu_ref, out_ref):
    me = pos_ref[0]
    j = pl.program_id(0)
    core = me % NC
    z = (me // NC) % NZ
    y = me // (NC * NZ)
    part = dot(g_ref[0], wg_ref[...], contract_last)
    part = part + dot(g_ref[1], wu_ref[...], contract_last)
    cols = pl.ds(pl.multiple_of(j * WIDE, WIDE), WIDE)
    for h in range(2):
        for b in range(NY):
            for s in range(NZ):
                src = ((y + DY[b] + NY) % NY) * NZ + (z + DZ[s] + NZ) % NZ
                to = src * NC + (core + h) % NC
                at = h * HALF + b * 64 + s * CAP
                out_ref[to, :, cols] = part[at : at + CAP].astype(bf16)

    @pl.when(j == 0)
    def _():
        def put(i, _):
            h, b, s = i // (NY * NZ), (i // NZ) % NY, i % NZ
            dy = jnp.where(b == 1, NY - 1, jnp.where(b == 2, 1, b - b // 3))
            dz = jnp.where(s % 2 == 1, NZ - (s + 1) // 2, s // 2)
            to = (((y + dy) % NY) * NZ + (z + dz) % NZ) * NC + (core + h) % NC
            rows = pl.ds(pl.multiple_of(i * CAP, CAP), CAP)
            out_ref[to, :, D:] = route_ref[rows, :].astype(bf16)
            return 0

        lax.fori_loop(0, 2 * NY * NZ, put, 0)


WIDE = 512
CHUNK_COST = 30_000_000_000
PICK_COST = 5_000_000_000
FRONT_COST = 5_000_000_000


def slots(pos, g, route, wg, wu):
    size = (NY * NZ * NC, CAP, DA)
    return pl.pallas_call(
        slots_kernel,
        grid=(D // WIDE,),
        out_shape=jax.ShapeDtypeStruct(size, bf16),
        in_specs=[
            SM, whole((2, ROWS, FF)), whole((ROWS, META)),
            pl.BlockSpec((WIDE, FF), lambda j: (j, 0)),
            pl.BlockSpec((WIDE, FF), lambda j: (j, 0)),
        ],
        out_specs=whole(size),
        compiler_params=pltpu.CompilerParams(vmem_limit_bytes=VLIM),
        name="slots",
    )(pos, g, route, wg, wu)


def body(tokens, cotangent, expert_ids, route_weights, w_gate, w_up, w_down):
    pos = jnp.stack([lax.axis_index("ep"), lax.axis_index("dp")]).astype(i32)
    meta = jnp.concatenate(
        [expert_ids.astype(bf16), route_weights, jnp.zeros((TOK, META - 2 * TOPK), bf16)], axis=1
    )
    xa = jnp.concatenate([tokens, meta], axis=1)

    c1 = shift(cotangent, dy=1)
    c2 = shift(cotangent, dy=-1)
    c3 = shift(c1, dy=1)

    u = [xa]
    d = [xa]
    for _ in range(3):
        u.append(shift(u[-1], dz=1))
        d.append(shift(d[-1], dz=-1))
    u.append(shift(u[-1], dz=1))

    cot0 = join([cotangent, c1, c2, c3], after=[u[3], d[3]])
    x0 = join([xa, u[1], d[1], u[2], d[2], u[3], d[3], u[4]], after=[cot0])
    p1 = shift(x0, dy=1)
    m1 = shift(x0, dy=-1)

    cu = [cot0]
    cd = [cot0]
    for _ in range(3):
        cu.append(shift(cu[-1], dz=1))
        cd.append(shift(cd[-1], dz=-1))

    n = NZ * TOK // 2
    qa, qb = p1[:n], m1[n:]
    blocks = x0, p1, m1, shift(qa, dy=1), shift(qb, dy=-1)

    n = NY * TOK // 2
    qa, qb = cu[-1][:n], cd[-1][n:]
    cq = [shift(qa, dz=1), shift(qb, dz=-1)]

    own_x, sib_x, code = pick_x(pos, blocks)
    sib_x = swap_core(sib_x)
    wg, wu, wd = w_gate[0], w_up[0], w_down[0]
    hid, hid_t, a, b, weight, x_t = front(pos, own_x, sib_x, wg, wu)

    parts = [cot0, cu[1], cd[1], cu[2], cd[2], cu[3], cd[3], *cq]
    own_c, sib_c = pick_cot(code, parts, after=code)
    sib_c = swap_core(sib_c)

    p2a, p2b, p1b, p3a, g, route, scot = mid(
        pos, own_c, sib_c, hid, hid_t, a, b, weight, x_t, wd
    )
    r1a, r1b = shift_dp(p2a, 1), shift_dp(p2b, -1)
    r2b, r2a = shift_dp(p1b, 1), shift_dp(p3a, -1)
    out = slots(pos, g, route, wg, wu)
    got = lax.all_to_all(out, "ep", split_axis=0, concat_axis=0, tiled=True)
    more = plain(pos, x_t, scot, g, hid_t, after=r1a)

    def added(n, arrived, cols):
        mine = more[n * PIECE : (n + 1) * PIECE, cols].astype(f32)
        return (mine + arrived[:, cols].astype(f32)).astype(bf16)

    first, last = slice(0, 2 * FF), slice(2 * FF, 3 * FF)
    r3a, r3b = shift_dp(added(0, r1a, first), 1), shift_dp(added(1, r1b, first), -1)
    r3a_down, r3b_down = shift_dp(added(0, r1a, last), 1), shift_dp(added(1, r1b, last), -1)
    grad_gate, grad_up, partial = chunk(more, r2a, r2b, r3a, r3b)

    experts = NY * NZ * NC
    one = (expert_ids[:, :, None] == jnp.arange(experts, dtype=i32)).astype(i32)
    named = jnp.sum(one, axis=1)
    token = jnp.arange(TOK, dtype=i32)
    lower = (token[None, :] < token[:, None]).astype(bf16)
    earlier = dot(lower, named.astype(bf16)).astype(i32)
    row = jnp.arange(experts * CAP, dtype=i32)
    code_of = jnp.repeat(jnp.where(named > 0, earlier, -1), CAP, axis=1)
    sel = code_of == (row % CAP)[None, :]
    got = got.reshape(experts * CAP, DA)
    grad_tokens = dot(sel.astype(bf16), got[:, :D]).astype(bf16)
    mine = sel[:, None, :] & (expert_ids[:, :, None] == (row // CAP)[None, None, :])
    grad_route = jnp.sum(jnp.where(mine, got[:, D].astype(f32), 0.0), axis=2).astype(bf16)

    grad_down = tail(partial, r3a_down, r3b_down, after=grad_tokens)
    return grad_tokens, grad_route, grad_gate, grad_up, grad_down


def solution(mesh):
    row = P(("ep", "dp"), None)
    expert = P("ep", None, None)
    return jax.shard_map(
        body,
        mesh=mesh,
        in_specs=(row, row, row, row, expert, expert, expert),
        out_specs=(row, row, P("ep", "dp", None), P("ep", "dp", None), P("ep", None, "dp")),
        check_vma=False,
    )
```

```python
import functools

import jax
import jax.numpy as jnp
from jax import lax
from jax.experimental import pallas as pl
from jax.experimental.pallas import tpu as pltpu
from jax.sharding import PartitionSpec as P

bf16 = jnp.bfloat16
f32 = jnp.float32
i32 = jnp.int32

NY, NZ, NC = 4, 8, 2
CAP = 8
TOK = 32
TOPK = 8
D = 2048
FF = 768
META = 128
DA = D + META
HALF = NY * NZ * CAP
ROWS = 2 * HALF
FB = 256
NFB = FF // FB
DY = (0, -1, 1, 2)
DZ = (0, -1, 1, -2, 2, -3, 3, 4)
NDP = 4
PIECE = D // NDP // 2
VLIM = 60 * 1024 * 1024

contract_last = (((1,), (1,)), ((), ()))
contract_first = (((0,), (0,)), ((), ()))
nothing = (((1,), (0,)), ((), ()))


def dot(a, b, dims=nothing):
    return lax.dot_general(a, b, dims, preferred_element_type=f32)


def flat(y, z, c):
    return ((y % NY) * NZ + (z % NZ)) * NC + c


def shift(arr, dy=0, dz=0):
    pairs = [
        (flat(y, z, c), flat(y + dy, z + dz, c))
        for y in range(NY)
        for z in range(NZ)
        for c in range(NC)
    ]
    return lax.ppermute(arr, "ep", pairs)


def swap_core(arr):
    return lax.ppermute(arr, "ep", [(i, i ^ 1) for i in range(NY * NZ * NC)])


def shift_dp(arr, by):
    return lax.ppermute(arr, "dp", [(i, (i + by) % NDP) for i in range(NDP)])


def join_kernel(count, *refs):
    out_ref = refs[-1]
    at = 0
    for ref in refs[:count]:
        out_ref[at : at + ref.shape[0], :] = ref[...]
        at += ref.shape[0]


def join(parts, after=()):
    rows = sum(part.shape[0] for part in parts)
    return pl.pallas_call(
        functools.partial(join_kernel, len(parts)),
        out_shape=jax.ShapeDtypeStruct((rows, parts[0].shape[1]), parts[0].dtype),
        in_specs=[VM] * len(parts) + [pl.BlockSpec(memory_space=pl.ANY)] * len(after),
        out_specs=VM,
        name="join",
    )(*parts, *after)


def cost(flops):
    return pl.CostEstimate(flops=flops, transcendentals=0, bytes_accessed=0)


VM = pl.BlockSpec(memory_space=pltpu.VMEM)
SM = pl.BlockSpec(memory_space=pltpu.SMEM)


def iota(shape, dim):
    return lax.broadcasted_iota(i32, shape, dim)


def widen_kernel(tokens_ref, ids_ref, weights_ref, out_ref, scr):
    scr[...] = jnp.zeros_like(scr)
    scr[:TOPK, :TOK] = ids_ref[...].astype(f32)
    scr[TOPK : 2 * TOPK, :TOK] = weights_ref[...].astype(f32)
    out_ref[:, :D] = tokens_ref[...]
    out_ref[:, D:] = scr[...].T[:TOK].astype(bf16)


def widen(tokens, ids, weights):
    return pl.pallas_call(
        widen_kernel,
        out_shape=jax.ShapeDtypeStruct((TOK, DA), bf16),
        in_specs=[VM] * 3,
        out_specs=VM,
        scratch_shapes=[pltpu.VMEM((META, META), f32)],
        name="widen",
    )(tokens, ids, weights)


def pick_x_kernel(me_ref, *refs):
    blocks = refs[:5]
    own_ref, sib_ref, code_ref, meta_scr, sel_scr = refs[5:]
    me = me_ref[0]
    n = NZ * TOK
    at = 0
    for ref in blocks:
        meta_scr[at : at + ref.shape[0]] = ref[:, D:]
        at += ref.shape[0]
    lane = iota((n, META), 1)
    tok = iota((n, META), 0)
    low = iota((n, n), 0)
    col = iota((n, n), 1)
    before = jnp.where((col < low) & (col // TOK == low // TOK), 1.0, 0.0).astype(bf16)
    which = iota((2 * META, META), 0) // META == iota((2 * META, META), 1) // 64
    spread = jnp.where(which, 1.0, 0.0).astype(bf16)
    row_pos = (lane % CAP).astype(f32)
    here = tok // TOK == (lane % 64) // CAP
    mine = me.astype(f32)
    other = (me ^ 1).astype(f32)

    def step(b, _):
        part = pl.ds(pl.multiple_of(b * n, n), n)
        meta = meta_scr[part].astype(f32)
        ids = lane < TOPK
        hits = jnp.concatenate(
            [
                jnp.where(ids & (meta == mine), 1.0, 0.0).astype(bf16),
                jnp.where(ids & (meta == other), 1.0, 0.0).astype(bf16),
            ],
            axis=1,
        )
        named = dot(hits, spread)
        earlier = dot(before, named.astype(bf16))
        code = jnp.where(named > 0, earlier, -1.0)
        code_ref[b] = code.astype(bf16)
        sel_scr[part] = jnp.where((code == row_pos) & here, 1.0, 0.0).astype(bf16)
        return 0

    lax.fori_loop(0, NY, step, 0)
    for b in range(NY):
        mine_refs = blocks[b : b + 1] if b < 3 else blocks[3:]
        rows = 0.0
        at = b * n
        for ref in mine_refs:
            size = ref.shape[0]
            rows = rows + dot(sel_scr[at : at + size], ref[...], contract_first)
            at += size
        rows = rows.astype(bf16)
        own_ref[b * 64 : (b + 1) * 64, :] = rows[:64]
        sib_ref[b * 64 : (b + 1) * 64, :] = rows[64:]


def pick_x(me, blocks):
    return pl.pallas_call(
        pick_x_kernel,
        out_shape=(
            jax.ShapeDtypeStruct((HALF, DA), bf16),
            jax.ShapeDtypeStruct((HALF, DA), bf16),
            jax.ShapeDtypeStruct((NY, NZ * TOK, META), bf16),
        ),
        in_specs=[SM] + [VM] * 5,
        out_specs=(VM, VM, VM),
        scratch_shapes=[
            pltpu.VMEM((NY * NZ * TOK, META), bf16), pltpu.VMEM((NY * NZ * TOK, META), bf16),
        ],
        compiler_params=pltpu.CompilerParams(vmem_limit_bytes=VLIM),
        cost_estimate=cost(0),
        name="pick_x",
    )(me, *blocks)


def pick_cot_kernel(code_ref, *refs):
    blocks = refs[:9]
    own_ref, sib_ref, own_acc, sib_acc = refs[10:]
    n = NY * TOK
    lane = iota((n, META), 1)
    tok = iota((n, META), 0)
    row_pos = (lane % CAP).astype(f32)
    row_src = (lane % 64) // CAP
    place = 0
    for s in range(NZ):
        if DZ[s] == 4:
            blk = jnp.concatenate([blocks[place][...], blocks[place + 1][...]], axis=0)
            place += 2
        else:
            blk = blocks[place][...]
            place += 1
        code = jnp.concatenate(
            [code_ref[b, s * TOK : (s + 1) * TOK, :] for b in range(NY)], axis=0
        ).astype(f32)
        sel = jnp.where((code == row_pos) & (tok // TOK == row_src), 1.0, 0.0).astype(bf16)
        rows = dot(sel, blk, contract_first)
        for b in range(NY):
            at = b * 64 + s * CAP
            own_acc[at : at + CAP, :] = rows[b * CAP : (b + 1) * CAP]
            sib_acc[at : at + CAP, :] = rows[64 + b * CAP : 64 + (b + 1) * CAP]
    own_ref[...] = own_acc[...].astype(bf16)
    sib_ref[...] = sib_acc[...].astype(bf16)


def pick_cot(code, blocks, after):
    return pl.pallas_call(
        pick_cot_kernel,
        out_shape=(
            jax.ShapeDtypeStruct((HALF, D), bf16),
            jax.ShapeDtypeStruct((HALF, D), bf16),
        ),
        in_specs=[VM] * 10 + [pl.BlockSpec(memory_space=pl.ANY)],
        out_specs=(VM, VM),
        scratch_shapes=[pltpu.VMEM((HALF, D), f32), pltpu.VMEM((HALF, D), f32)],
        compiler_params=pltpu.CompilerParams(vmem_limit_bytes=VLIM),
        cost_estimate=cost(PICK_COST),
        name="pick_cot",
    )(code, *blocks, after)


def front_kernel(
    me_ref, own_ref, sib_ref, wg_ref, wu_ref,
    hid_ref, hid_t_ref, a_ref, b_ref, weight_ref, x_t_ref, x_scr,
):
    @pl.when(pl.program_id(0) == 0)
    def _():
        x_scr[:HALF] = own_ref[:, :D]
        x_scr[HALF:] = sib_ref[:, :D]
        x_t_ref[...] = x_scr[...].T
        meta = jnp.concatenate([own_ref[:, D:], sib_ref[:, D:]], axis=0).astype(f32)
        expert = me_ref[0].astype(f32)
        total = jnp.zeros((ROWS, 1), f32)
        for k in range(TOPK):
            total = total + jnp.where(
                meta[:, k : k + 1] == expert, meta[:, TOPK + k : TOPK + k + 1], 0.0
            )
        weight_ref[...] = jnp.broadcast_to(total, (ROWS, META))

    x = x_scr[...]
    gate = dot(x, wg_ref[...])
    up = dot(x, wu_ref[...])
    sig = jax.nn.sigmoid(gate)
    act = gate * sig
    hid = (act * up).astype(bf16)
    hid_ref[...] = hid
    hid_t_ref[...] = hid.T
    a_ref[...] = up * (sig * (1.0 + gate * (1.0 - sig)))
    b_ref[...] = act


def front(me, own, sib, wg, wu):
    whole = lambda shape: pl.BlockSpec(shape, lambda j: (0,) * len(shape))
    wide = pl.BlockSpec((ROWS, FB), lambda j: (0, j))
    return pl.pallas_call(
        front_kernel,
        grid=(NFB,),
        out_shape=(
            jax.ShapeDtypeStruct((ROWS, FF), bf16),
            jax.ShapeDtypeStruct((FF, ROWS), bf16),
            jax.ShapeDtypeStruct((ROWS, FF), f32),
            jax.ShapeDtypeStruct((ROWS, FF), f32),
            jax.ShapeDtypeStruct((ROWS, META), f32),
            jax.ShapeDtypeStruct((D, ROWS), bf16),
        ),
        in_specs=[
            SM, whole((HALF, DA)), whole((HALF, DA)),
            pl.BlockSpec((D, FB), lambda j: (0, j)),
            pl.BlockSpec((D, FB), lambda j: (0, j)),
        ],
        out_specs=(
            wide, pl.BlockSpec((FB, ROWS), lambda j: (j, 0)), wide, wide,
            whole((ROWS, META)), whole((D, ROWS)),
        ),
        scratch_shapes=[pltpu.VMEM((ROWS, D), bf16)],
        compiler_params=pltpu.CompilerParams(vmem_limit_bytes=VLIM),
        cost_estimate=cost(FRONT_COST),
        name="front",
    )(me, own, sib, wg, wu)


def whole(shape):
    return pl.BlockSpec(shape, lambda *_: (0,) * len(shape))


def place(pos_ref, piece):
    return (2 * pos_ref[1] + piece) % (2 * NDP)


def piece_into(out_ref, x_rows, g_ref, hid_t_ref, scot_cols):
    for n in range(2):
        out_ref[:, n * FF : (n + 1) * FF] = dot(x_rows, g_ref[n]).astype(bf16)
    for q in range(NFB):
        value = dot(hid_t_ref[q * FB : (q + 1) * FB], scot_cols)
        out_ref[:, 2 * FF + q * FB : 2 * FF + (q + 1) * FB] = value.astype(bf16)


def mid_kernel(
    pos_ref, own_ref, sib_ref, hid_ref, hid_t_ref, a_ref, b_ref, weight_ref, x_t_ref, wd_ref,
    pa_ref, pb_ref, pc_ref, pd_ref, g_ref, route_ref, scot_ref, cot_scr, out_scr,
):
    j = pl.program_id(0)

    @pl.when(j == 0)
    def _():
        cot_scr[:HALF] = own_ref[...]
        cot_scr[HALF:] = sib_ref[...]
        scot_ref[...] = (weight_ref[:, :1] * cot_scr[...].astype(f32)).astype(bf16)
        route_ref[...] = jnp.zeros_like(route_ref)

    back = dot(cot_scr[...], wd_ref[...], contract_last)
    part = jnp.sum(hid_ref[...].astype(f32) * back, axis=1, keepdims=True)
    route_ref[...] += jnp.broadcast_to(part, (ROWS, META))
    scaled = weight_ref[:, :1] * back
    cols = pl.ds(pl.multiple_of(j * FB, FB), FB)
    g_ref[0, :, cols] = (scaled * a_ref[...]).astype(bf16)
    g_ref[1, :, cols] = (scaled * b_ref[...]).astype(bf16)

    @pl.when(j == NFB - 1)
    def _():
        def step(n, _):
            piece = jnp.where(n == 0, 4, jnp.where(n == 1, 5, jnp.where(n == 2, 3, 6)))
            some = pl.ds(pl.multiple_of(place(pos_ref, piece) * PIECE, PIECE), PIECE)
            piece_into(
                out_scr.at[n], x_t_ref[some, :], g_ref, hid_t_ref, scot_ref[:, some]
            )
            return 0

        lax.fori_loop(0, 4, step, 0)
        for n, ref in enumerate((pa_ref, pb_ref, pc_ref, pd_ref)):
            ref[...] = out_scr[n]


def mid(pos, own, sib, hid, hid_t, a, b, weight, x_t, wd):
    wide = pl.BlockSpec((ROWS, FB), lambda j, pos_ref: (0, j))
    size = (PIECE, 3 * FF)
    return pl.pallas_call(
        mid_kernel,
        out_shape=(
            *[jax.ShapeDtypeStruct(size, bf16)] * 4,
            jax.ShapeDtypeStruct((2, ROWS, FF), bf16),
            jax.ShapeDtypeStruct((ROWS, META), f32),
            jax.ShapeDtypeStruct((ROWS, D), bf16),
        ),
        grid_spec=pltpu.PrefetchScalarGridSpec(
            num_scalar_prefetch=1,
            grid=(NFB,),
            in_specs=[
                whole((HALF, D)), whole((HALF, D)), wide, whole((FF, ROWS)), wide, wide,
                whole((ROWS, META)), whole((D, ROWS)),
                pl.BlockSpec((FB, D), lambda j, pos_ref: (j, 0)),
            ],
            out_specs=(
                *[whole(size)] * 4, whole((2, ROWS, FF)), whole((ROWS, META)), whole((ROWS, D)),
            ),
            scratch_shapes=[
                pltpu.VMEM((ROWS, D), bf16), pltpu.VMEM((4, PIECE, 3 * FF), bf16),
            ],
        ),
        compiler_params=pltpu.CompilerParams(vmem_limit_bytes=VLIM),
        name="mid",
    )(pos, own, sib, hid, hid_t, a, b, weight, x_t, wd)


def plain_kernel(pos_ref, x_ref, c_ref, g_ref, hid_t_ref, _, out_ref):
    piece_into(out_ref, x_ref[...], g_ref, hid_t_ref, c_ref[...])


def plain(pos, x_t, scot, g, hid_t, after):
    def index(n, pos_ref):
        return place(pos_ref, jnp.where(n == 0, 2, jnp.where(n == 1, 7, n - 2)))

    return pl.pallas_call(
        plain_kernel,
        out_shape=jax.ShapeDtypeStruct((4 * PIECE, 3 * FF), bf16),
        grid_spec=pltpu.PrefetchScalarGridSpec(
            num_scalar_prefetch=1,
            grid=(4,),
            in_specs=[
                pl.BlockSpec((PIECE, ROWS), lambda n, pos_ref: (index(n, pos_ref), 0)),
                pl.BlockSpec((ROWS, PIECE), lambda n, pos_ref: (0, index(n, pos_ref))),
                whole((2, ROWS, FF)), whole((FF, ROWS)),
                pl.BlockSpec(memory_space=pl.ANY),
            ],
            out_specs=pl.BlockSpec((PIECE, 3 * FF), lambda n, pos_ref: (n, 0)),
        ),
        compiler_params=pltpu.CompilerParams(vmem_limit_bytes=VLIM),
        name="plain",
    )(pos, x_t, scot, g, hid_t, after)


def chunk_kernel(own_ref, r2a, r2b, r3a, r3b, gate_ref, up_ref, down_ref):
    for n, (r2, r3) in enumerate(((r2a, r3a), (r2b, r3b))):

        @pl.when(pl.program_id(0) == n)
        def _():
            def rows(i, _):
                some = pl.ds(pl.multiple_of(i * 64, 64), 64)
                to = pl.ds(pl.multiple_of(n * PIECE + i * 64, 64), 64)
                for k, ref in enumerate((gate_ref, up_ref)):
                    cols = slice(k * FF, (k + 1) * FF)
                    value = own_ref[some, cols].astype(f32) + r2[some, cols].astype(f32)
                    ref[0, to, :] = (value + r3[some, cols].astype(f32)).astype(bf16)
                cols = slice(2 * FF, 3 * FF)
                down_ref[to, :] = own_ref[some, cols].astype(f32) + r2[some, cols].astype(f32)
                return 0

            lax.fori_loop(0, PIECE // 64, rows, 0)


def chunk(more, *arrived):
    size = (PIECE, 3 * FF)
    per = D // NDP
    return pl.pallas_call(
        chunk_kernel,
        grid=(2,),
        out_shape=(
            jax.ShapeDtypeStruct((1, per, FF), bf16),
            jax.ShapeDtypeStruct((1, per, FF), bf16),
            jax.ShapeDtypeStruct((per, FF), f32),
        ),
        in_specs=[pl.BlockSpec(size, lambda n: (n + 2, 0))]
        + [whole(size)] * 2 + [whole((PIECE, 2 * FF))] * 2,
        out_specs=(whole((1, per, FF)), whole((1, per, FF)), whole((per, FF))),
        compiler_params=pltpu.CompilerParams(vmem_limit_bytes=VLIM),
        cost_estimate=cost(CHUNK_COST),
        name="chunk",
    )(more, *arrived)


def tail_kernel(sum_ref, ra_ref, rb_ref, _, out_ref):
    for n, ref in enumerate((ra_ref, rb_ref)):
        side = slice(n * PIECE, (n + 1) * PIECE)
        for q in range(NFB):
            cols = slice(q * FB, (q + 1) * FB)
            out_ref[0, cols, side] = (sum_ref[side, cols] + ref[:, cols].astype(f32)).astype(bf16)


def tail(partial, ra, rb, after):
    return pl.pallas_call(
        tail_kernel,
        out_shape=jax.ShapeDtypeStruct((1, FF, D // NDP), bf16),
        in_specs=[VM] * 3 + [pl.BlockSpec(memory_space=pl.ANY)],
        out_specs=VM,
        compiler_params=pltpu.CompilerParams(vmem_limit_bytes=VLIM),
        name="tail",
    )(partial, ra, rb, after)


def slots_kernel(pos_ref, g_ref, route_ref, wg_ref, wu_ref, out_ref):
    me = pos_ref[0]
    j = pl.program_id(0)
    core = me % NC
    z = (me // NC) % NZ
    y = me // (NC * NZ)
    part = dot(g_ref[0], wg_ref[...], contract_last)
    part = part + dot(g_ref[1], wu_ref[...], contract_last)
    cols = pl.ds(pl.multiple_of(j * WIDE, WIDE), WIDE)
    for h in range(2):
        for b in range(NY):
            for s in range(NZ):
                src = ((y + DY[b] + NY) % NY) * NZ + (z + DZ[s] + NZ) % NZ
                to = src * NC + (core + h) % NC
                at = h * HALF + b * 64 + s * CAP
                out_ref[to, :, cols] = part[at : at + CAP].astype(bf16)

    @pl.when(j == 0)
    def _():
        def put(i, _):
            h, b, s = i // (NY * NZ), (i // NZ) % NY, i % NZ
            dy = jnp.where(b == 1, NY - 1, jnp.where(b == 2, 1, b - b // 3))
            dz = jnp.where(s % 2 == 1, NZ - (s + 1) // 2, s // 2)
            to = (((y + dy) % NY) * NZ + (z + dz) % NZ) * NC + (core + h) % NC
            rows = pl.ds(pl.multiple_of(i * CAP, CAP), CAP)
            out_ref[to, :, D:] = route_ref[rows, :].astype(bf16)
            return 0

        lax.fori_loop(0, 2 * NY * NZ, put, 0)


WIDE = 512
CHUNK_COST = 30_000_000_000
PICK_COST = 5_000_000_000
FRONT_COST = 5_000_000_000


def slots(pos, g, route, wg, wu):
    size = (NY * NZ * NC, CAP, DA)
    return pl.pallas_call(
        slots_kernel,
        grid=(D // WIDE,),
        out_shape=jax.ShapeDtypeStruct(size, bf16),
        in_specs=[
            SM, whole((2, ROWS, FF)), whole((ROWS, META)),
            pl.BlockSpec((WIDE, FF), lambda j: (j, 0)),
            pl.BlockSpec((WIDE, FF), lambda j: (j, 0)),
        ],
        out_specs=whole(size),
        compiler_params=pltpu.CompilerParams(vmem_limit_bytes=VLIM),
        name="slots",
    )(pos, g, route, wg, wu)


def body(tokens, cotangent, expert_ids, route_weights, w_gate, w_up, w_down):
    pos = jnp.stack([lax.axis_index("ep"), lax.axis_index("dp")]).astype(i32)
    xa = widen(tokens, expert_ids.T, route_weights.T)

    c1 = shift(cotangent, dy=1)
    c2 = shift(cotangent, dy=-1)
    c3 = shift(c1, dy=1)

    u = [xa]
    d = [xa]
    for _ in range(3):
        u.append(shift(u[-1], dz=1))
        d.append(shift(d[-1], dz=-1))
    u.append(shift(u[-1], dz=1))

    cot0 = join([cotangent, c1, c2, c3], after=[u[3], d[3]])
    x0 = join([xa, u[1], d[1], u[2], d[2], u[3], d[3], u[4]], after=[cot0])
    p1 = shift(x0, dy=1)
    m1 = shift(x0, dy=-1)

    cu = [cot0]
    cd = [cot0]
    for _ in range(3):
        cu.append(shift(cu[-1], dz=1))
        cd.append(shift(cd[-1], dz=-1))

    n = NZ * TOK // 2
    qa, qb = p1[:n], m1[n:]
    blocks = x0, p1, m1, shift(qa, dy=1), shift(qb, dy=-1)

    n = NY * TOK // 2
    qa, qb = cu[-1][:n], cd[-1][n:]
    cq = [shift(qa, dz=1), shift(qb, dz=-1)]

    own_x, sib_x, code = pick_x(pos, blocks)
    sib_x = swap_core(sib_x)
    wg, wu, wd = w_gate[0], w_up[0], w_down[0]
    hid, hid_t, a, b, weight, x_t = front(pos, own_x, sib_x, wg, wu)

    parts = [cot0, cu[1], cd[1], cu[2], cd[2], cu[3], cd[3], *cq]
    own_c, sib_c = pick_cot(code, parts, after=code)
    sib_c = swap_core(sib_c)

    p2a, p2b, p1b, p3a, g, route, scot = mid(
        pos, own_c, sib_c, hid, hid_t, a, b, weight, x_t, wd
    )
    r1a, r1b = shift_dp(p2a, 1), shift_dp(p2b, -1)
    r2b, r2a = shift_dp(p1b, 1), shift_dp(p3a, -1)
    out = slots(pos, g, route, wg, wu)
    got = lax.all_to_all(out, "ep", split_axis=0, concat_axis=0, tiled=True)
    more = plain(pos, x_t, scot, g, hid_t, after=r1a)

    def added(n, arrived, cols):
        mine = more[n * PIECE : (n + 1) * PIECE, cols].astype(f32)
        return (mine + arrived[:, cols].astype(f32)).astype(bf16)

    first, last = slice(0, 2 * FF), slice(2 * FF, 3 * FF)
    r3a, r3b = shift_dp(added(0, r1a, first), 1), shift_dp(added(1, r1b, first), -1)
    r3a_down, r3b_down = shift_dp(added(0, r1a, last), 1), shift_dp(added(1, r1b, last), -1)
    grad_gate, grad_up, partial = chunk(more, r2a, r2b, r3a, r3b)

    experts = NY * NZ * NC
    one = (expert_ids[:, :, None] == jnp.arange(experts, dtype=i32)).astype(i32)
    named = jnp.sum(one, axis=1)
    token = jnp.arange(TOK, dtype=i32)
    lower = (token[None, :] < token[:, None]).astype(bf16)
    earlier = dot(lower, named.astype(bf16)).astype(i32)
    row = jnp.arange(experts * CAP, dtype=i32)
    code_of = jnp.repeat(jnp.where(named > 0, earlier, -1), CAP, axis=1)
    sel = code_of == (row % CAP)[None, :]
    got = got.reshape(experts * CAP, DA)
    grad_tokens = dot(sel.astype(bf16), got[:, :D]).astype(bf16)
    mine = sel[:, None, :] & (expert_ids[:, :, None] == (row // CAP)[None, None, :])
    grad_route = jnp.sum(jnp.where(mine, got[:, D].astype(f32), 0.0), axis=2).astype(bf16)

    grad_down = tail(partial, r3a_down, r3b_down, after=grad_tokens)
    return grad_tokens, grad_route, grad_gate, grad_up, grad_down


def solution(mesh):
    row = P(("ep", "dp"), None)
    expert = P("ep", None, None)
    return jax.shard_map(
        body,
        mesh=mesh,
        in_specs=(row, row, row, row, expert, expert, expert),
        out_specs=(row, row, P("ep", "dp", None), P("ep", "dp", None), P("ep", None, "dp")),
        check_vma=False,
    )
```
